32 devices in a mesh: grp: 1, uly: 8 (over z, y), doc: 4 (over x, core).
Axes of the slice: x: 2, y: 2, z: 4, core: 2. Of those that a mesh axis runs over, the one named last changes fastest.
Arguments:
- queries: bfloat16 [4096, 2048], P(('grp', 'doc', 'uly')), may hold values from -4 to 4
- key_vectors: bfloat16 [4096, 2048], P(('grp', 'doc', 'uly')), may hold values from -4 to 4
- value_vectors: bfloat16 [4096, 2048], P(('grp', 'doc', 'uly')), may hold values from -6 to 6
- layout: int32 [32, 32, 32], P('grp'), may hold values from 0 to 31, as said below
- counts: int32 [32, 32], P('grp'), may hold values from 1 to 32, as said below
Outputs:
- attended: bfloat16 [4096, 2048], P(('grp', 'doc', 'uly'))
The draws below stay inside these ranges and needn't reach their ends.
Inputs may be any that keep to these rules, and one draw needn't show every extreme that they name: layout[h, b, 0] = b; the first counts[h, b] entries of a row are distinct blocks; later entries name blocks that are not attended. `counts`: H // 4 heads have 32 // 2 to 32 used entries in every row, the others 1 to 8.
All inputs are finite; a program needn't handle non-finite values.
Results may differ from the reference program's by a relative error of at most 0.0055.
Values may be sent and summed in bfloat16 or wider, within the bound.
No kernel may reach another device: no remote copies, remote signals or barrier semaphores. Data moves between devices by JAX's collectives and lax.ppermute only.
A program may use at most 64 MiB of HBM per device.

```python
import jax
import jax.numpy as jnp
from jax import lax

H = 32
DH = 64
BLK = 128
KMAX = 32
L = 4096
NB = 32


def draw_queries(key, part):
    drawn = 0.56 * jax.random.truncated_normal(jax.random.fold_in(key, 1), -6.0, 6.0, (L, H * DH), jnp.float32)
    return drawn.astype(jnp.bfloat16)


def draw_key_vectors(key, part):
    drawn = 0.56 * jax.random.truncated_normal(jax.random.fold_in(key, 2), -6.0, 6.0, (L, H * DH), jnp.float32)
    return drawn.astype(jnp.bfloat16)


def layout_tables(key):
    base_key = jax.random.fold_in(key, 11)
    head_rank = jax.random.permutation(jax.random.fold_in(base_key, 1), H)
    heavy_heads = head_rank < H // 4
    high_counts = jax.random.randint(jax.random.fold_in(base_key, 2), (H, NB), KMAX // 2, KMAX + 1)
    low_counts = jax.random.randint(jax.random.fold_in(base_key, 3), (H, NB), 1, KMAX // 4 + 1)
    head_counts = jnp.where(heavy_heads[:, None], high_counts, low_counts)
    first_column = jnp.where(heavy_heads, KMAX, head_counts[:, 0])
    head_counts = head_counts.at[:, 0].set(first_column).astype(jnp.int32)
    random_scores = jax.random.randint(jax.random.fold_in(base_key, 4), (H, NB, NB - 1), 0, 2 ** 20)
    random_scores = random_scores * NB + jnp.arange(NB - 1, dtype=jnp.int32)[None, None, :]
    unused_values, picked = lax.top_k(random_scores, KMAX - 1)
    block_index = jnp.arange(NB, dtype=jnp.int32)[None, :, None]
    other_blocks = (block_index + picked.astype(jnp.int32) + 1) % NB
    self_blocks = jnp.broadcast_to(block_index, (H, NB, 1))
    head_layout = jnp.concatenate([self_blocks, other_blocks], axis=2).astype(jnp.int32)
    return (head_layout, head_counts)


def draw_layout(key, part):
    head_layout, head_counts = layout_tables(key)
    return head_layout


def draw_counts(key, part):
    head_layout, head_counts = layout_tables(key)
    return head_counts


def block_scale(own_key, extent, shards, smallest, largest):
    level = 1.0
    for position, shards_of in shards:
        steps = jax.random.uniform(jax.random.fold_in(jax.random.fold_in(own_key, 6), position), (shards_of,), jnp.float32, smallest / len(shards), largest / len(shards))
        level = level * jnp.repeat(jnp.exp(steps), extent[position] // shards_of).reshape((-1,) + (1,) * (len(extent) - 1 - position))
    return level


def centred(key, shape, width, bound, split=(), kind=jnp.bfloat16):
    factor_of = block_scale(key, shape, split, -0.22, 0.18) if split else 1.0
    values = jax.random.normal(key, shape, jnp.float32) * width * factor_of
    return jnp.minimum(jnp.maximum(values, -bound), bound).astype(kind)


def setup_inputs(seed: int = 0, part: int = 0) -> dict:
    arg_keys = jax.random.split(jax.random.key(seed), 6)
    part_keys = jax.random.split(jax.random.fold_in(arg_keys[5], part), 6)
    queries = draw_queries(jax.random.fold_in(jax.random.fold_in(arg_keys[5], part), 71), part)
    key_vectors = draw_key_vectors(jax.random.fold_in(jax.random.fold_in(arg_keys[5], part), 71), part)
    value_vectors = centred(part_keys[2], (L, H * DH), 1.0, 6.0, ((0, 32),))
    layout = draw_layout(jax.random.fold_in(jax.random.fold_in(arg_keys[5], part), 71), part)
    counts = draw_counts(jax.random.fold_in(jax.random.fold_in(arg_keys[5], part), 71), part)
    return dict(queries=queries, key_vectors=key_vectors, value_vectors=value_vectors, layout=layout, counts=counts)


def head_attention(inputs):
    head_of_query, key_head, value_head, head_layout, head_counts = inputs
    key_block_list = jnp.take(key_head, head_layout, axis=0).reshape(NB, KMAX * BLK, DH)
    value_block_list = jnp.take(value_head, head_layout, axis=0).reshape(NB, KMAX * BLK, DH)
    logit_scores = jnp.einsum("vth,vlh->vtl", head_of_query.astype(jnp.float32), key_block_list.astype(jnp.float32))
    live_slots = jnp.arange(KMAX, dtype=jnp.int32)[None, :] < head_counts[:, None]
    slot_mask = jnp.repeat(live_slots, BLK, axis=1)[:, None, :]
    logit_scores = jnp.where(slot_mask, logit_scores, -jnp.inf)
    row_max = jnp.max(logit_scores, axis=-1, keepdims=True)
    weights = jnp.exp(logit_scores - row_max)
    row_sum = jnp.sum(weights, axis=-1, keepdims=True)
    rounded_weights = weights.astype(jnp.bfloat16)
    blended_values = jnp.einsum("hyc,hcr->hyr", rounded_weights.astype(jnp.float32), value_block_list.astype(jnp.float32))
    return (blended_values / row_sum).astype(jnp.bfloat16).reshape(L, DH)


def reference(queries, key_vectors, value_vectors, layout, counts):
    def by_heads(tensor):
        return tensor.reshape(NB, BLK, H, DH).transpose(2, 0, 1, 3)

    result = lax.map(head_attention, (by_heads(queries), by_heads(key_vectors), by_heads(value_vectors), layout, counts))
    return result.transpose(1, 0, 2).reshape(L, H * DH)
```

```python
import functools

import jax
import jax.numpy as jnp
from jax import lax
from jax.experimental import pallas as pl
from jax.experimental.pallas import tpu as pltpu
from jax.sharding import PartitionSpec as P

H = 32
DH = 64
BLK = 128
KMAX = 32
UNROLL = 4
BIG = 1e30
VMEM = pl.BlockSpec(memory_space=pltpu.VMEM)
SMEM = pl.BlockSpec(memory_space=pltpu.SMEM)
PARAMS = pltpu.CompilerParams(vmem_limit_bytes=58 << 20)


def pack_kernel(head_ref, place_ref, q_ref, k_ref, v_ref, qt_ref, kp_ref, vt_ref):
    per = kp_ref.shape[2] // DH
    low = lax.broadcasted_iota(jnp.int32, (BLK, 2 * DH), 1) < DH
    for pair in range(H // 2):
        lanes = slice(pair * 2 * DH, (pair + 1) * 2 * DH)
        for source, target in ((q_ref, qt_ref), (v_ref, vt_ref)):
            turned = source[:, lanes].T
            target[place_ref[2 * pair]] = turned[:DH]
            target[place_ref[2 * pair + 1]] = turned[DH:]

        def fetch(place, odd):
            head = head_ref[place]
            start = pl.multiple_of((head // 2) * (2 * DH), 2 * DH)
            block = k_ref[:, pl.ds(start, 2 * DH)]
            swapped = jnp.concatenate([block[:, DH:], block[:, :DH]], axis=1)
            return jnp.where((head % 2) == odd, block, swapped)

        joined = jnp.where(low, fetch(2 * pair, 0), fetch(2 * pair + 1, 1))
        group, slot = divmod(2 * pair, per)
        kp_ref[group, :, slot * DH : slot * DH + 2 * DH] = joined


def attend_kernel(lay_ref, cnt_ref, qt_ref, k_ref, vt_ref, o_ref, unit_ref, qz_ref, m_ref, l_ref, acc_ref):
    slab, width, _ = qt_ref.shape
    per = width // DH
    rows = per * slab

    def place_row(row, base):
        count = cnt_ref[row]
        units = (count + 1) // 2

        def place_unit(step, _):
            first = lay_ref[row * KMAX + 2 * step]
            whole = 2 * step + 1 < count
            second = jnp.where(whole, lay_ref[row * KMAX + 2 * step + 1], first)
            unit_ref[0, base + step] = row
            unit_ref[1, base + step] = first
            unit_ref[2, base + step] = second
            unit_ref[3, base + step] = whole.astype(jnp.int32)
            return 0

        lax.fori_loop(0, units, place_unit, 0)
        return base + units

    total = lax.fori_loop(0, rows, place_row, 0)
    for extra in range(UNROLL):
        unit_ref[0, total + extra] = rows
        unit_ref[1, total + extra] = 0
        unit_ref[2, total + extra] = 0
        unit_ref[3, total + extra] = 1

    zeros = jnp.zeros((DH, BLK), jnp.bfloat16)
    for head in range(per):
        for block in range(slab):
            part = qt_ref[block, head * DH : (head + 1) * DH, :]
            both = [part, zeros] if head % 2 == 0 else [zeros, part]
            qz_ref[head * slab + block] = jnp.concatenate(both, axis=0)
    m_ref[...] = jnp.full(m_ref.shape, -BIG, jnp.float32)
    l_ref[...] = jnp.zeros(l_ref.shape, jnp.float32)
    acc_ref[...] = jnp.zeros(acc_ref.shape, jnp.float32)
    qz_ref[rows] = jnp.zeros((2 * DH, BLK), jnp.bfloat16)

    def one(unit):
        row = unit_ref[0, unit]
        first = unit_ref[1, unit]
        second = unit_ref[2, unit]
        whole = unit_ref[3, unit]
        head = jnp.minimum(row // slab, per - 1)
        lanes = pl.ds(pl.multiple_of((head // 2) * (2 * DH), 2 * DH), 2 * DH)
        weights = qz_ref[row]
        keys = jnp.concatenate([k_ref[first, :, lanes], k_ref[second, :, lanes]], axis=0)
        scores = jnp.dot(keys, weights, preferred_element_type=jnp.float32)
        tiles = scores.reshape(2 * BLK // 8, 8, BLK)
        top = jnp.max(tiles, axis=0)
        top = jnp.max(top, axis=0, keepdims=True)
        limit = jnp.where(whole == 1, top, top + BIG)
        first_w = jnp.exp(scores[:BLK] - top)
        second_w = jnp.exp(scores[BLK:] - limit)
        w = jnp.concatenate([first_w, second_w], axis=0)
        part_sum = jnp.sum(w.reshape(2 * BLK // 8, 8, BLK), axis=0)
        span = pl.ds(pl.multiple_of(head * DH, DH), DH)
        values = jnp.concatenate([vt_ref[first, span, :], vt_ref[second, span, :]], axis=1)
        out = jnp.dot(values, w.astype(jnp.bfloat16), preferred_element_type=jnp.float32)
        return row, top, part_sum, out

    def step(index, _):
        done = [one(index * UNROLL + lane) for lane in range(UNROLL)]
        for row, top, part_sum, out in done:
            old = m_ref[row]
            new = jnp.maximum(old, top)
            a = jnp.exp(old - new)
            b = jnp.exp(top - new)
            m_ref[row] = new
            l_ref[row] = l_ref[row] * a + part_sum * b
            acc_ref[row] = (
                acc_ref[row].reshape(DH // 8, 8, BLK) * a[None] + out.reshape(DH // 8, 8, BLK) * b[None]
            ).reshape(DH, BLK)
        return 0

    lax.fori_loop(0, (total + UNROLL - 1) // UNROLL, step, 0)

    for head in range(per):
        for block in range(slab):
            row = head * slab + block
            total_w = jnp.sum(l_ref[row], axis=0, keepdims=True)
            o_ref[block, head * DH : (head + 1) * DH, :] = (acc_ref[row] / total_w).astype(jnp.bfloat16)


def unpack_kernel(place_ref, o_ref, out_ref):
    for pair in range(H // 2):
        both = jnp.concatenate([o_ref[place_ref[2 * pair]], o_ref[place_ref[2 * pair + 1]]], axis=0)
        out_ref[:, pair * 2 * DH : (pair + 1) * 2 * DH] = both.T


def places_of(counts, groups):
    load = jnp.sum(counts, axis=1)
    ids = jnp.arange(H, dtype=jnp.int32)
    ahead = (load[None, :] > load[:, None]) | ((load[None, :] == load[:, None]) & (ids[None, :] < ids[:, None]))
    rank = jnp.sum(ahead.astype(jnp.int32), axis=1)
    turn, seat = rank // groups, rank % groups
    group = jnp.where(turn % 2 == 0, seat, groups - 1 - seat)
    place = group * (H // groups) + turn
    head_at = jnp.sum(jnp.where(place[None, :] == ids[:, None], ids[None, :], 0), axis=1)
    return head_at, place


def shards(queries, key_vectors, value_vectors, layout, counts):
    uly = lax.axis_size("uly")
    per = H // uly
    width = per * DH
    slab = queries.shape[0] // BLK * uly
    bf16 = jnp.bfloat16
    head_at, place = places_of(counts, uly)
    shape = jax.ShapeDtypeStruct
    qt, kp, vt = pl.pallas_call(
        pack_kernel,
        out_shape=(shape((H, DH, BLK), bf16), shape((uly, BLK, width), bf16), shape((H, DH, BLK), bf16)),
        in_specs=[SMEM, SMEM, VMEM, VMEM, VMEM],
        out_specs=(VMEM, VMEM, VMEM),
        compiler_params=PARAMS,
        name="pack",
    )(head_at, place, queries, key_vectors, value_vectors)
    swap = functools.partial(lax.all_to_all, axis_name="uly", split_axis=0, concat_axis=0, tiled=True)
    kp = swap(kp)
    k_full = lax.all_gather(kp, "doc", axis=0, tiled=True)
    vt = swap(vt.reshape(uly, width, BLK))
    v_full = lax.all_gather(vt, "doc", axis=0, tiled=True)
    qt = swap(qt.reshape(uly, width, BLK))
    mine = lax.dynamic_slice_in_dim(head_at, lax.axis_index("uly") * per, per)
    begin = lax.axis_index("doc") * slab
    lay = jnp.take(lax.dynamic_slice_in_dim(layout, begin, slab, axis=1), mine, axis=0).reshape(-1)
    cnt = jnp.take(lax.dynamic_slice_in_dim(counts, begin, slab, axis=1), mine, axis=0).reshape(-1)
    rows = per * slab
    ot = pl.pallas_call(
        attend_kernel,
        out_shape=shape((slab, width, BLK), bf16),
        in_specs=[SMEM, SMEM, VMEM, VMEM, VMEM],
        out_specs=VMEM,
        scratch_shapes=[
            pltpu.SMEM((4, rows * KMAX // 2 + UNROLL), jnp.int32),
            pltpu.VMEM((rows + 1, 2 * DH, BLK), bf16),
            pltpu.VMEM((rows + 1, 8, BLK), jnp.float32),
            pltpu.VMEM((rows + 1, 8, BLK), jnp.float32),
            pltpu.VMEM((rows + 1, DH, BLK), jnp.float32),
        ],
        compiler_params=PARAMS,
        name="attend",
    )(lay, cnt, qt, k_full, v_full)
    ot = swap(ot)
    return pl.pallas_call(
        unpack_kernel,
        out_shape=shape(queries.shape, bf16),
        in_specs=[SMEM, VMEM],
        out_specs=VMEM,
        compiler_params=PARAMS,
        name="unpack",
    )(place, ot.reshape(H, DH, BLK))


def solution(mesh):
    placed = (
        P(("grp", "doc", "uly"), None),
        P(("grp", "doc", "uly"), None),
        P(("grp", "doc", "uly"), None),
        P("grp", None, None),
        P("grp", None),
    )
    return jax.shard_map(
        shards,
        mesh=mesh,
        in_specs=placed,
        out_specs=P(("grp", "doc", "uly"), None),
        check_vma=False,
    )
```

```python
import functools

import jax
import jax.numpy as jnp
from jax import lax
from jax.experimental import pallas as pl
from jax.experimental.pallas import tpu as pltpu
from jax.sharding import PartitionSpec as P

H = 32
DH = 64
BLK = 128
KMAX = 32
UNROLL = 4
BIG = 1e30
F32 = jnp.float32
BF16 = jnp.bfloat16
VMEM = pl.BlockSpec(memory_space=pltpu.VMEM)
SMEM = pl.BlockSpec(memory_space=pltpu.SMEM)
ANY = pl.BlockSpec(memory_space=pl.ANY)
PARAMS = pltpu.CompilerParams(vmem_limit_bytes=58 << 20)


def pack_kernel(head_ref, q_ref, k_ref, v_ref, *refs):
    pairs = (len(refs) - 1) // 2
    kv_refs, qt_refs, turned = refs[:pairs], refs[pairs : 2 * pairs], refs[-1]
    groups = qt_refs[0].shape[0]
    low = lax.broadcasted_iota(jnp.int32, (BLK, 2 * DH), 1) < DH
    for pair in range(H // 2):
        lanes = slice(pair * 2 * DH, (pair + 1) * 2 * DH)
        for which, source in enumerate((q_ref, v_ref)):
            tile = source[:, lanes].T
            turned[which, 2 * pair] = tile[:DH]
            turned[which, 2 * pair + 1] = tile[DH:]

    def fetch(head, odd):
        start = pl.multiple_of((head // 2) * (2 * DH), 2 * DH)
        block = k_ref[:, pl.ds(start, 2 * DH)]
        swapped = jnp.concatenate([block[:, DH:], block[:, :DH]], axis=1)
        return jnp.where((head % 2) == odd, block, swapped)

    for pair in range(pairs):
        for group in range(groups):
            place = (pair * groups + group) * 2
            left, right = head_ref[place], head_ref[place + 1]
            kv_refs[pair][group, 0] = jnp.where(low, fetch(left, 0), fetch(right, 1))
            kv_refs[pair][group, 1] = jnp.concatenate([turned[1, left], turned[1, right]], axis=0)
            qt_refs[pair][group] = jnp.concatenate([turned[0, left], turned[0, right]], axis=0)


def plan_kernel(groups, me_ref, lay_ref, cnt_ref, unit_ref, total_ref):
    pairs = total_ref.shape[0]
    rows = cnt_ref.shape[0] // pairs
    own = me_ref[0]

    def local(block):
        return ((block // groups) ^ own) * groups + block % groups

    for pair in range(pairs):

        def idle(base, many):
            for extra in range(many):
                unit_ref[pair, 0, base + extra] = rows
                unit_ref[pair, 1, base + extra] = 0
                unit_ref[pair, 2, base + extra] = 0
                unit_ref[pair, 3, base + extra] = 1

        def place_row(row, base):
            count = cnt_ref[pair * rows + row]
            start = (pair * rows + row) * KMAX

            def place_unit(step, _):
                first = lay_ref[start + 2 * step]
                whole = 2 * step + 1 < count
                second = jnp.where(whole, lay_ref[start + 2 * step + 1], first)
                unit_ref[pair, 0, base + step] = row
                unit_ref[pair, 1, base + step] = local(first)
                unit_ref[pair, 2, base + step] = local(second)
                unit_ref[pair, 3, base + step] = whole.astype(jnp.int32)
                return 0

            units = (count + 1) // 2
            lax.fori_loop(0, units, place_unit, 0)
            return base + units

        idle(0, 2 * UNROLL)
        total = lax.fori_loop(0, rows, place_row, jnp.int32(2 * UNROLL))
        idle(total, 4 * UNROLL)
        total_ref[pair] = total


def attend_kernel(pair, slabs, unit_ref, total_ref, qt_ref, *refs):
    kv_hbm, o_ref = refs[:slabs], refs[slabs]
    kv_ref, qz_ref, m_ref, l_ref, acc_ref, sem = refs[slabs + 1 : slabs + 7]
    score, top_of, out_of, sum_of = (refs[slabs + 7 + 2 * at : slabs + 9 + 2 * at] for at in range(4))
    slab = qt_ref.shape[0]
    rows = 2 * slab
    copies = [
        pltpu.make_async_copy(source, kv_ref.at[pl.ds(at * slab, slab)], sem.at[at])
        for at, source in enumerate(kv_hbm)
    ]
    for copy in copies:
        copy.start()
    zeros = jnp.zeros((DH, BLK), BF16)
    for head in range(2):
        for block in range(slab):
            part = qt_ref[block, head * DH : (head + 1) * DH, :]
            up = jnp.concatenate([part, zeros], axis=0)
            down = jnp.concatenate([zeros, part], axis=0)
            qz_ref[head * slab + block] = jnp.concatenate([up, down], axis=1)
    qz_ref[rows] = jnp.zeros((2 * DH, 2 * BLK), BF16)
    m_ref[...] = jnp.full(m_ref.shape, -BIG, F32)
    for ref in (l_ref, acc_ref, *score, *top_of, *out_of, *sum_of):
        ref[...] = jnp.zeros(ref.shape, F32)
    for copy in copies:
        copy.wait()
    low = lax.broadcasted_iota(jnp.int32, (BLK, 2 * DH), 1) < DH

    def read(unit):
        row = unit_ref[pair, 0, unit]
        odd = jnp.where((row >= slab) & (row < rows), 1, 0)
        return row, odd, unit_ref[pair, 1, unit], unit_ref[pair, 2, unit]

    def make_scores(unit, lane, side):
        row, odd, first, second = read(unit)
        plain = kv_ref[jnp.where(odd == 1, second, first), 0]
        other = kv_ref[jnp.where(odd == 1, first, second), 0]
        other = jnp.concatenate([other[:, DH:], other[:, :DH]], axis=1)
        keys = jnp.where(low == (odd == 0), plain, other)
        scores = jnp.dot(keys, qz_ref[row], preferred_element_type=F32)
        score[side][lane] = scores
        top = jnp.max(scores.reshape(BLK // 8, 8, 2 * BLK), axis=0)
        top = jnp.maximum(top[:, :BLK], top[:, BLK:])
        top_of[side][lane] = jnp.broadcast_to(jnp.max(top, axis=0, keepdims=True), (8, BLK))

    def make_output(unit, lane, side):
        _, odd, first, second = read(unit)
        top = top_of[side][lane]
        limit = jnp.where(unit_ref[pair, 3, unit] == 1, top, top + BIG)
        scores = score[side][lane]
        left = jnp.exp(scores[:, :BLK].reshape(BLK // 8, 8, BLK) - top[None])
        right = jnp.exp(scores[:, BLK:].reshape(BLK // 8, 8, BLK) - limit[None])
        sum_of[side][lane] = jnp.sum(left, axis=0) + jnp.sum(right, axis=0)
        weights = jnp.concatenate([left.reshape(BLK, BLK), right.reshape(BLK, BLK)], axis=0)
        span = pl.ds(pl.multiple_of(odd * DH, DH), DH)
        values = jnp.concatenate([kv_ref[first, 1, span, :], kv_ref[second, 1, span, :]], axis=1)
        out_of[side][lane] = jnp.dot(values, weights.astype(BF16), preferred_element_type=F32)

    def merge(unit, lane, side):
        row = unit_ref[pair, 0, unit]
        top, old = top_of[side][lane], m_ref[row]
        new = jnp.maximum(old, top)
        a, b = jnp.exp(old - new), jnp.exp(top - new)
        m_ref[row] = new
        l_ref[row] = l_ref[row] * a + sum_of[side][lane] * b
        tiles = (DH // 8, 8, BLK)
        acc_ref[row] = (acc_ref[row].reshape(tiles) * a[None] + out_of[side][lane].reshape(tiles) * b[None]).reshape(
            DH, BLK
        )

    def step(index, _):
        for side in range(2):
            chunk = 2 * index + side
            for lane in range(UNROLL):
                merge(chunk * UNROLL + lane, lane, side)
            for lane in range(UNROLL):
                make_scores((chunk + 2) * UNROLL + lane, lane, side)
                make_output((chunk + 1) * UNROLL + lane, lane, 1 - side)
        return 0

    chunks = (total_ref[pair] + UNROLL - 1) // UNROLL
    lax.fori_loop(0, (chunks + 1) // 2, step, 0)
    for head in range(2):
        for block in range(slab):
            row = head * slab + block
            total_w = jnp.sum(l_ref[row], axis=0, keepdims=True)
            o_ref[block, head * DH : (head + 1) * DH, :] = (acc_ref[row] / total_w).astype(BF16)


def unpack_kernel(place_ref, *refs):
    ins, out_ref, held = refs[:-2], refs[-2], refs[-1]
    groups = ins[0].shape[0]
    for pair, source in enumerate(ins):
        for group in range(groups):
            place = (pair * groups + group) * 2
            held[place] = source[group, :DH]
            held[place + 1] = source[group, DH:]
    for pair in range(H // 2):
        both = jnp.concatenate([held[place_ref[2 * pair]], held[place_ref[2 * pair + 1]]], axis=0)
        out_ref[:, pair * 2 * DH : (pair + 1) * 2 * DH] = both.T


def places_of(counts, groups):
    load = jnp.sum(counts, axis=1)
    ids = jnp.arange(H, dtype=jnp.int32)
    ahead = (load[None, :] > load[:, None]) | ((load[None, :] == load[:, None]) & (ids[None, :] < ids[:, None]))
    rank = jnp.sum(ahead.astype(jnp.int32), axis=1)
    turn, seat = rank // groups, rank % groups
    group = jnp.where(turn % 2 == 0, seat, groups - 1 - seat)
    place = ((turn // 2) * groups + group) * 2 + turn % 2
    head_at = jnp.sum(jnp.where(place[None, :] == ids[:, None], ids[None, :], 0), axis=1)
    return head_at, place


def shards(queries, key_vectors, value_vectors, layout, counts):
    groups, slabs = lax.axis_size("uly"), lax.axis_size("doc")
    per = H // groups
    pairs = per // 2
    slab = groups
    rows = 2 * slab
    shape = jax.ShapeDtypeStruct
    head_at, place = places_of(counts, groups)
    packed = pl.pallas_call(
        pack_kernel,
        out_shape=(shape((groups, 2, BLK, BLK), BF16),) * pairs + (shape((groups, BLK, BLK), BF16),) * pairs,
        in_specs=[SMEM, VMEM, VMEM, VMEM],
        out_specs=(VMEM,) * (2 * pairs),
        scratch_shapes=[pltpu.VMEM((2, H, DH, BLK), BF16)],
        compiler_params=PARAMS,
        name="pack",
    )(head_at, queries, key_vectors, value_vectors)
    swap = functools.partial(lax.all_to_all, axis_name="uly", split_axis=0, concat_axis=0, tiled=True)

    def flip(array, bit):
        return lax.ppermute(array, "doc", [(at, at ^ bit) for at in range(slabs)])

    own = lax.axis_index("doc")
    mine = head_at.reshape(pairs, groups, 2)
    mine = lax.dynamic_index_in_dim(mine, lax.axis_index("uly"), 1, keepdims=False).reshape(-1)
    lay = jnp.take(lax.dynamic_slice_in_dim(layout, own * slab, slab, axis=1), mine, axis=0).reshape(-1)
    cnt = jnp.take(lax.dynamic_slice_in_dim(counts, own * slab, slab, axis=1), mine, axis=0).reshape(-1)
    units, totals = pl.pallas_call(
        functools.partial(plan_kernel, groups),
        out_shape=(
            shape((pairs, 4, rows * KMAX // 2 + 8 * UNROLL), jnp.int32),
            shape((pairs,), jnp.int32),
        ),
        in_specs=[SMEM, SMEM, SMEM],
        out_specs=(SMEM, SMEM),
        compiler_params=PARAMS,
        name="plan",
    )(own.reshape(1), lay, cnt)

    returned = []
    for pair in range(pairs):
        kv = swap(packed[pair])
        qt = swap(packed[pairs + pair])
        gathered = {0: kv}
        bit = slabs // 2
        while bit:
            gathered.update({at ^ bit: flip(array, bit) for at, array in list(gathered.items())})
            bit //= 2
        both = [pltpu.VMEM((UNROLL, BLK, 2 * BLK), F32)] * 2 + [pltpu.VMEM((UNROLL, 8, BLK), F32)] * 2
        both += [pltpu.VMEM((UNROLL, DH, BLK), F32)] * 2 + [pltpu.VMEM((UNROLL, 8, BLK), F32)] * 2
        out = pl.pallas_call(
            functools.partial(attend_kernel, pair, slabs),
            out_shape=shape((slab, BLK, BLK), BF16),
            in_specs=[SMEM, SMEM, VMEM] + [ANY] * slabs,
            out_specs=VMEM,
            scratch_shapes=[
                pltpu.VMEM((slabs * slab, 2, BLK, BLK), BF16),
                pltpu.VMEM((rows + 1, 2 * DH, 2 * BLK), BF16),
                pltpu.VMEM((rows + 1, 8, BLK), F32),
                pltpu.VMEM((rows + 1, 8, BLK), F32),
                pltpu.VMEM((rows + 1, DH, BLK), F32),
                pltpu.SemaphoreType.DMA((slabs,)),
                *both,
            ],
            compiler_params=PARAMS,
            name="attend",
        )(units, totals, qt, *[gathered[at] for at in range(slabs)])
        returned.append(swap(out))
    return pl.pallas_call(
        unpack_kernel,
        out_shape=shape(queries.shape, BF16),
        in_specs=[SMEM] + [VMEM] * pairs,
        out_specs=VMEM,
        scratch_shapes=[pltpu.VMEM((H, DH, BLK), BF16)],
        compiler_params=PARAMS,
        name="unpack",
    )(place, *returned)


def solution(mesh):
    placed = (
        P(("grp", "doc", "uly"), None),
        P(("grp", "doc", "uly"), None),
        P(("grp", "doc", "uly"), None),
        P("grp", None, None),
        P("grp", None),
    )
    return jax.shard_map(
        shards,
        mesh=mesh,
        in_specs=placed,
        out_specs=P(("grp", "doc", "uly"), None),
        check_vma=False,
    )
```

```python
import functools

import jax
import jax.numpy as jnp
from jax import lax
from jax.experimental import pallas as pl
from jax.experimental.pallas import tpu as pltpu
from jax.sharding import PartitionSpec as P

H = 32
DH = 64
BLK = 128
KMAX = 32
UNROLL = 4
BIG = 1e30
F32 = jnp.float32
BF16 = jnp.bfloat16
VMEM = pl.BlockSpec(memory_space=pltpu.VMEM)
SMEM = pl.BlockSpec(memory_space=pltpu.SMEM)
ANY = pl.BlockSpec(memory_space=pl.ANY)
PARAMS = pltpu.CompilerParams(vmem_limit_bytes=58 << 20)


def pack_kernel(groups, me_ref, head_ref, q_ref, k_ref, v_ref, *out_refs):
    low = lax.broadcasted_iota(jnp.int32, (BLK, 2 * DH), 1) < DH

    def fetch(source, head, odd):
        start = pl.multiple_of((head // 2) * (2 * DH), 2 * DH)
        block = source[:, pl.ds(start, 2 * DH)]
        swapped = jnp.concatenate([block[:, DH:], block[:, :DH]], axis=1)
        return jnp.where((head % 2) == odd, block, swapped)

    for at, out in enumerate(out_refs):
        pair, step = divmod(at, groups)
        place = (pair * groups + (me_ref[0] ^ step)) * 2
        left, right = head_ref[place], head_ref[place + 1]
        joined = [jnp.where(low, fetch(source, left, 0), fetch(source, right, 1)) for source in (k_ref, v_ref, q_ref)]
        out[0], out[1], out[2] = joined[0], joined[1].T, joined[2].T


def plan_kernel(groups, me_ref, lay_ref, cnt_ref, unit_ref, total_ref):
    pairs = total_ref.shape[0]
    rows = cnt_ref.shape[0] // pairs
    slab, group = me_ref[1], me_ref[0]

    def local(block):
        return ((block // groups) ^ slab) * groups + ((block % groups) ^ group)

    for pair in range(pairs):

        def idle(base, many):
            for extra in range(many):
                unit_ref[pair, 0, base + extra] = rows
                unit_ref[pair, 1, base + extra] = 0
                unit_ref[pair, 2, base + extra] = 0
                unit_ref[pair, 3, base + extra] = 1

        def place_row(row, base):
            count = cnt_ref[pair * rows + row]
            start = (pair * rows + row) * KMAX

            def place_unit(step, _):
                first = lay_ref[start + 2 * step]
                whole = 2 * step + 1 < count
                second = jnp.where(whole, lay_ref[start + 2 * step + 1], first)
                unit_ref[pair, 0, base + step] = row
                unit_ref[pair, 1, base + step] = local(first)
                unit_ref[pair, 2, base + step] = local(second)
                unit_ref[pair, 3, base + step] = whole.astype(jnp.int32)
                return 0

            units = (count + 1) // 2
            lax.fori_loop(0, units, place_unit, 0)
            return base + units

        idle(0, 2 * UNROLL)
        total = lax.fori_loop(0, rows, place_row, jnp.int32(2 * UNROLL))
        idle(total, 4 * UNROLL)
        total_ref[pair] = total


def attend_kernel(pair, slabs, slab, unit_ref, total_ref, *refs):
    pieces, others, outs = refs[:slab], refs[slab : slab + slabs - 1], refs[slab + slabs - 1 : 2 * slab + slabs - 1]
    refs = refs[2 * slab + slabs - 1 :]
    kv_ref, qt_ref, qz_ref, m_ref, l_ref, acc_ref, sem = refs[:7]
    score, top_of, out_of, sum_of = (refs[7 + 2 * at : 9 + 2 * at] for at in range(4))
    rows = 2 * slab
    first = [pltpu.make_async_copy(piece.at[2], qt_ref.at[at], sem.at[at]) for at, piece in enumerate(pieces)]
    rest = [
        pltpu.make_async_copy(piece.at[pl.ds(0, 2)], kv_ref.at[at], sem.at[slab + at]) for at, piece in enumerate(pieces)
    ]
    rest += [
        pltpu.make_async_copy(other, kv_ref.at[pl.ds((at + 1) * slab, slab)], sem.at[2 * slab + at])
        for at, other in enumerate(others)
    ]
    for copy in first + rest:
        copy.start()
    for copy in first:
        copy.wait()
    zeros = jnp.zeros((DH, BLK), BF16)
    for head in range(2):
        for block in range(slab):
            part = qt_ref[block, head * DH : (head + 1) * DH, :]
            up = jnp.concatenate([part, zeros], axis=0)
            down = jnp.concatenate([zeros, part], axis=0)
            qz_ref[head * slab + block] = jnp.concatenate([up, down], axis=1)
    qz_ref[rows] = jnp.zeros((2 * DH, 2 * BLK), BF16)
    m_ref[...] = jnp.full(m_ref.shape, -BIG, F32)
    for ref in (l_ref, acc_ref):
        ref[...] = jnp.zeros(ref.shape, F32)
    for copy in rest:
        copy.wait()
    low = lax.broadcasted_iota(jnp.int32, (BLK, 2 * DH), 1) < DH

    def read(unit):
        row = unit_ref[pair, 0, unit]
        odd = jnp.where((row >= slab) & (row < rows), 1, 0)
        return row, odd, unit_ref[pair, 1, unit], unit_ref[pair, 2, unit]

    def make_scores(unit, lane, side):
        row, odd, first, second = read(unit)
        plain = kv_ref[jnp.where(odd == 1, second, first), 0]
        other = kv_ref[jnp.where(odd == 1, first, second), 0]
        other = jnp.concatenate([other[:, DH:], other[:, :DH]], axis=1)
        keys = jnp.where(low == (odd == 0), plain, other)
        scores = jnp.dot(keys, qz_ref[row], preferred_element_type=F32)
        score[side][lane] = scores
        top = jnp.max(scores.reshape(BLK // 8, 8, 2 * BLK), axis=0)
        top = jnp.maximum(top[:, :BLK], top[:, BLK:])
        top_of[side][lane] = jnp.broadcast_to(jnp.max(top, axis=0, keepdims=True), (8, BLK))

    def make_output(unit, lane, side):
        _, odd, first, second = read(unit)
        top = top_of[side][lane]
        limit = jnp.where(unit_ref[pair, 3, unit] == 1, top, top + BIG)
        scores = score[side][lane]
        left = jnp.exp(scores[:, :BLK].reshape(BLK // 8, 8, BLK) - top[None])
        right = jnp.exp(scores[:, BLK:].reshape(BLK // 8, 8, BLK) - limit[None])
        sum_of[side][lane] = jnp.sum(left, axis=0) + jnp.sum(right, axis=0)
        weights = jnp.concatenate([left.reshape(BLK, BLK), right.reshape(BLK, BLK)], axis=0)
        span = pl.ds(pl.multiple_of(odd * DH, DH), DH)
        values = jnp.concatenate([kv_ref[first, 1, span, :], kv_ref[second, 1, span, :]], axis=1)
        out_of[side][lane] = jnp.dot(values, weights.astype(BF16), preferred_element_type=F32)

    def merge(unit, lane, side):
        row = unit_ref[pair, 0, unit]
        top, old = top_of[side][lane], m_ref[row]
        new = jnp.maximum(old, top)
        a, b = jnp.exp(old - new), jnp.exp(top - new)
        m_ref[row] = new
        l_ref[row] = l_ref[row] * a + sum_of[side][lane] * b
        tiles = (DH // 8, 8, BLK)
        acc_ref[row] = (acc_ref[row].reshape(tiles) * a[None] + out_of[side][lane].reshape(tiles) * b[None]).reshape(
            DH, BLK
        )

    def step(index, _):
        for side in range(2):
            chunk = 2 * index + side
            for lane in range(UNROLL):
                merge(chunk * UNROLL + lane, lane, side)
            for lane in range(UNROLL):
                make_scores((chunk + 2) * UNROLL + lane, lane, side)
                make_output((chunk + 1) * UNROLL + lane, lane, 1 - side)
        return 0

    chunks = (total_ref[pair] + UNROLL - 1) // UNROLL
    lax.fori_loop(0, (chunks + 1) // 2, step, 0)
    for head in range(2):
        for block in range(slab):
            row = head * slab + block
            total_w = jnp.sum(l_ref[row], axis=0, keepdims=True)
            outs[block][head * DH : (head + 1) * DH, :] = (acc_ref[row] / total_w).astype(BF16)


def unpack_kernel(spot_ref, *refs):
    ins, out_ref, held = refs[:-2], refs[-2], refs[-1]
    for at, source in enumerate(ins):
        held[2 * at] = source[:DH]
        held[2 * at + 1] = source[DH:]
    for pair in range(H // 2):
        both = jnp.concatenate([held[spot_ref[2 * pair]], held[spot_ref[2 * pair + 1]]], axis=0)
        out_ref[:, pair * 2 * DH : (pair + 1) * 2 * DH] = both.T


def places_of(counts, groups, me):
    load = jnp.sum(counts, axis=1)
    ids = jnp.arange(H, dtype=jnp.int32)
    ahead = (load[None, :] > load[:, None]) | ((load[None, :] == load[:, None]) & (ids[None, :] < ids[:, None]))
    rank = jnp.sum(ahead.astype(jnp.int32), axis=1)
    turn, seat = rank // groups, rank % groups
    group = jnp.where(turn % 2 == 0, seat, groups - 1 - seat)
    place = ((turn // 2) * groups + group) * 2 + turn % 2
    head_at = jnp.sum(jnp.where(place[None, :] == ids[:, None], ids[None, :], 0), axis=1)
    spot = ((turn // 2) * groups + (group ^ me)) * 2 + turn % 2
    return head_at, spot


def shards(queries, key_vectors, value_vectors, layout, counts):
    groups, slabs = lax.axis_size("uly"), lax.axis_size("doc")
    per = H // groups
    pairs = per // 2
    slab = groups
    rows = 2 * slab
    shape = jax.ShapeDtypeStruct
    me, own = lax.axis_index("uly"), lax.axis_index("doc")
    where = jnp.stack([me, own])
    head_at, spot = places_of(counts, groups, me)
    packed = pl.pallas_call(
        functools.partial(pack_kernel, groups),
        out_shape=(shape((3, BLK, BLK), BF16),) * (pairs * groups),
        in_specs=[SMEM, SMEM, VMEM, VMEM, VMEM],
        out_specs=(VMEM,) * (pairs * groups),
        compiler_params=PARAMS,
        name="pack",
    )(where, head_at, queries, key_vectors, value_vectors)

    def flip(array, axis, size, bit):
        return lax.ppermute(array, axis, [(at, at ^ bit) for at in range(size)])

    def exchange(pieces):
        return [piece if step == 0 else flip(piece, "uly", groups, step) for step, piece in enumerate(pieces)]

    mine = lax.dynamic_index_in_dim(head_at.reshape(pairs, groups, 2), me, 1, keepdims=False).reshape(-1)
    order = jnp.arange(groups, dtype=jnp.int32) ^ me
    lay = jnp.take(jnp.take(layout, mine, axis=0), own * slab + order, axis=1).reshape(-1)
    cnt = jnp.take(jnp.take(counts, mine, axis=0), own * slab + order, axis=1).reshape(-1)
    units, totals = pl.pallas_call(
        functools.partial(plan_kernel, groups),
        out_shape=(
            shape((pairs, 4, rows * KMAX // 2 + 8 * UNROLL), jnp.int32),
            shape((pairs,), jnp.int32),
        ),
        in_specs=[SMEM, SMEM, SMEM],
        out_specs=(SMEM, SMEM),
        compiler_params=PARAMS,
        name="plan",
    )(where, lay, cnt)

    returned = []
    for pair in range(pairs):
        pieces = exchange(packed[pair * groups : (pair + 1) * groups])
        gathered = {0: jnp.stack([piece[:2] for piece in pieces])}
        bit = slabs // 2
        while bit:
            gathered.update({at ^ bit: flip(array, "doc", slabs, bit) for at, array in list(gathered.items())})
            bit //= 2
        both = [pltpu.VMEM((UNROLL, BLK, 2 * BLK), F32)] * 2 + [pltpu.VMEM((UNROLL, 8, BLK), F32)] * 2
        both += [pltpu.VMEM((UNROLL, DH, BLK), F32)] * 2 + [pltpu.VMEM((UNROLL, 8, BLK), F32)] * 2
        out = pl.pallas_call(
            functools.partial(attend_kernel, pair, slabs, slab),
            out_shape=(shape((BLK, BLK), BF16),) * slab,
            in_specs=[SMEM, SMEM] + [ANY] * (slab + slabs - 1),
            out_specs=(VMEM,) * slab,
            scratch_shapes=[
                pltpu.VMEM((slabs * slab, 2, BLK, BLK), BF16),
                pltpu.VMEM((slab, BLK, BLK), BF16),
                pltpu.VMEM((rows + 1, 2 * DH, 2 * BLK), BF16),
                pltpu.VMEM((rows + 1, 8, BLK), F32),
                pltpu.VMEM((rows + 1, 8, BLK), F32),
                pltpu.VMEM((rows + 1, DH, BLK), F32),
                pltpu.SemaphoreType.DMA((2 * slab + slabs - 1,)),
                *both,
            ],
            compiler_params=PARAMS,
            name="attend",
        )(units, totals, *pieces, *[gathered[at] for at in range(1, slabs)])
        returned += exchange(out)
    return pl.pallas_call(
        unpack_kernel,
        out_shape=shape(queries.shape, BF16),
        in_specs=[SMEM] + [VMEM] * len(returned),
        out_specs=VMEM,
        scratch_shapes=[pltpu.VMEM((H, DH, BLK), BF16)],
        compiler_params=PARAMS,
        name="unpack",
    )(spot, *returned)


def solution(mesh):
    placed = (
        P(("grp", "doc", "uly"), None),
        P(("grp", "doc", "uly"), None),
        P(("grp", "doc", "uly"), None),
        P("grp", None, None),
        P("grp", None),
    )
    return jax.shard_map(
        shards,
        mesh=mesh,
        in_specs=placed,
        out_specs=P(("grp", "doc", "uly"), None),
        check_vma=False,
    )
```

```python
import functools

import jax
import jax.numpy as jnp
from jax import lax
from jax.experimental import pallas as pl
from jax.experimental.pallas import tpu as pltpu
from jax.sharding import PartitionSpec as P

H = 32
DH = 64
BLK = 128
KMAX = 32
UNROLL = 4
BIG = 1e30
F32 = jnp.float32
BF16 = jnp.bfloat16
VMEM = pl.BlockSpec(memory_space=pltpu.VMEM)
SMEM = pl.BlockSpec(memory_space=pltpu.SMEM)
PARAMS = pltpu.CompilerParams(vmem_limit_bytes=58 << 20)


def rank_heads(counts_ref, table_ref, groups, me):
    counts = counts_ref[...].astype(BF16)
    blocks = counts.shape[1]
    over = (((1,), (1,)), ((), ()))
    mine = lax.dot_general(counts, jnp.ones((H, blocks), BF16), over, preferred_element_type=F32)
    theirs = lax.dot_general(jnp.ones((H, blocks), BF16), counts, over, preferred_element_type=F32)
    row = lax.broadcasted_iota(jnp.int32, (H, H), 0)
    lane = lax.broadcasted_iota(jnp.int32, (H, H), 1)
    bits = groups.bit_length() - 1

    def place_of(rank, own_group):
        turn, seat = rank >> bits, rank & (groups - 1)
        group = jnp.where((turn & 1) == 0, seat, groups - 1 - seat) ^ own_group
        return (((turn >> 1) * groups + group) << 1) + (turn & 1)

    behind = (theirs > mine) | ((theirs == mine) & (lane < row))
    rank_down = jnp.sum(jnp.where(behind, 1.0, 0.0), axis=1, keepdims=True).astype(jnp.int32)
    ahead = (mine > theirs) | ((theirs == mine) & (row < lane))
    rank_along = jnp.sum(jnp.where(ahead, 1.0, 0.0), axis=0, keepdims=True).astype(jnp.int32)
    here = place_of(jnp.broadcast_to(rank_down, (H, H)), 0) == lane
    head_at = jnp.sum(jnp.where(here, row.astype(F32), 0.0), axis=0, keepdims=True).astype(jnp.int32)
    table_ref[0:1, 0:H] = head_at
    table_ref[1:2, 0:H] = place_of(rank_along, me)


def pack_kernel(groups, counts_ref, q_ref, k_ref, v_ref, table_ref, qt_ref, *refs):
    kv_refs, turned, table_vmem, sem = refs[:-3], refs[-3], refs[-2], refs[-1]
    pairs = qt_ref.shape[1]
    me = lax.axis_index("uly")
    rank_heads(counts_ref, table_vmem, groups, me)
    copy = pltpu.make_async_copy(table_vmem, table_ref, sem)
    copy.start()
    low = lax.broadcasted_iota(jnp.int32, (BLK, 2 * DH), 1) < DH
    for pair in range(H // 2):
        lanes = slice(pair * 2 * DH, (pair + 1) * 2 * DH)
        for which, source in enumerate((q_ref, v_ref)):
            tile = source[:, lanes].T
            turned[which, 2 * pair] = tile[:DH]
            turned[which, 2 * pair + 1] = tile[DH:]
    copy.wait()

    def fetch(head, odd):
        start = pl.multiple_of((head // 2) * (2 * DH), 2 * DH)
        block = k_ref[:, pl.ds(start, 2 * DH)]
        swapped = jnp.concatenate([block[:, DH:], block[:, :DH]], axis=1)
        return jnp.where((head % 2) == odd, block, swapped)

    for step, kv_ref in enumerate(kv_refs):
        group = me ^ step
        for pair in range(pairs):
            place = (pair * groups + group) * 2
            left, right = table_ref[0, place], table_ref[0, place + 1]
            kv_ref[pair, 0] = jnp.where(low, fetch(left, 0), fetch(right, 1))
            kv_ref[pair, 1] = jnp.concatenate([turned[1, left], turned[1, right]], axis=0)
            qt_ref[group, pair] = jnp.concatenate([turned[0, left], turned[0, right]], axis=0)


def join_kernel(*refs):
    *pieces, out_ref = refs[1:]
    for at, piece in enumerate(pieces):
        out_ref[at] = piece[...]


def plan_kernel(groups, slabs, table_ref, counts_ref, layout_ref, unit_ref, total_ref, lay_ref, sem):
    per = H // groups
    group, slab = lax.axis_index("uly"), lax.axis_index("doc")
    rows = per * groups

    def head_of(slot):
        return table_ref[0, ((slot // 2) * groups + group) * 2 + slot % 2]

    copies = [
        pltpu.make_async_copy(layout_ref.at[head_of(slot), pl.ds(slab * groups, groups)], lay_ref.at[slot], sem.at[slot])
        for slot in range(per)
    ]
    for copy in copies:
        copy.start()

    def local(block):
        return block ^ (slab * groups + group)

    def idle(base, many):
        for extra in range(many):
            unit_ref[0, base + extra] = rows
            unit_ref[1, base + extra] = 0
            unit_ref[2, base + extra] = 0
            unit_ref[3, base + extra] = 1

    idle(0, 2 * UNROLL)
    for copy in copies:
        copy.wait()
    base = jnp.int32(2 * UNROLL)
    for slot in range(per):
        head = head_of(slot)

        def place_row(block, base, slot=slot, head=head):
            count = counts_ref[head, slab * groups + block]

            def place_unit(step, _):
                first = lay_ref[slot, block, 2 * step]
                whole = 2 * step + 1 < count
                second = jnp.where(whole, lay_ref[slot, block, jnp.minimum(2 * step + 1, KMAX - 1)], first)
                unit_ref[0, base + step] = slot * groups + block
                unit_ref[1, base + step] = local(first)
                unit_ref[2, base + step] = local(second)
                unit_ref[3, base + step] = whole.astype(jnp.int32)
                return 0

            units = (count + 1) // 2
            lax.fori_loop(0, units, place_unit, 0)
            return base + units

        base = lax.fori_loop(0, groups, place_row, base)
    idle(base, 4 * UNROLL)
    total_ref[0] = base


def attend_kernel(sizes, unit_ref, total_ref, qt_ref, *refs):
    many = sum(size > 0 for size in sizes)
    kv_hbm, o_ref = refs[:many], refs[many]
    kv_ref, qz_ref, m_ref, l_ref, acc_ref, sem = refs[many + 1 : many + 7]
    score, top_of, out_of, sum_of = (refs[many + 7 + 2 * at : many + 9 + 2 * at] for at in range(4))
    slab, pairs = qt_ref.shape[:2]
    rows = 2 * pairs * slab
    start, copies = 0, []
    for at, source in enumerate(kv_hbm):
        copies.append(pltpu.make_async_copy(source, kv_ref.at[pl.ds(start, sizes[at])], sem.at[at]))
        copies[-1].start()
        start += sizes[at]
    zeros = jnp.zeros((DH, BLK), BF16)
    for head in range(2 * pairs):
        for block in range(slab):
            part = qt_ref[block, head // 2, (head % 2) * DH : (head % 2 + 1) * DH, :]
            up = jnp.concatenate([part, zeros], axis=0)
            down = jnp.concatenate([zeros, part], axis=0)
            qz_ref[head * slab + block] = jnp.concatenate([up, down], axis=1)
    qz_ref[rows] = jnp.zeros((2 * DH, 2 * BLK), BF16)
    m_ref[...] = jnp.full(m_ref.shape, -BIG, F32)
    for ref in (l_ref, acc_ref):
        ref[...] = jnp.zeros(ref.shape, F32)
    for copy in copies:
        copy.wait()
    low = lax.broadcasted_iota(jnp.int32, (BLK, 2 * DH), 1) < DH

    def read(unit):
        row = unit_ref[0, unit]
        head = jnp.minimum(row // slab, 2 * pairs - 1)
        return row, head // 2, head % 2, unit_ref[1, unit], unit_ref[2, unit]

    def make_scores(unit, lane, side):
        row, pair, odd, first, second = read(unit)
        plain = kv_ref[jnp.where(odd == 1, second, first), pair, 0]
        other = kv_ref[jnp.where(odd == 1, first, second), pair, 0]
        other = jnp.concatenate([other[:, DH:], other[:, :DH]], axis=1)
        keys = jnp.where(low == (odd == 0), plain, other)
        scores = jnp.dot(keys, qz_ref[row], preferred_element_type=F32)
        score[side][lane] = scores
        top = jnp.max(scores.reshape(BLK // 8, 8, 2 * BLK), axis=0)
        top = jnp.maximum(top[:, :BLK], top[:, BLK:])
        top_of[side][lane] = jnp.broadcast_to(jnp.max(top, axis=0, keepdims=True), (8, BLK))

    def make_output(unit, lane, side):
        _, pair, odd, first, second = read(unit)
        top = top_of[side][lane]
        limit = jnp.where(unit_ref[3, unit] == 1, top, top + BIG)
        scores = score[side][lane]
        left = jnp.exp(scores[:, :BLK].reshape(BLK // 8, 8, BLK) - top[None])
        right = jnp.exp(scores[:, BLK:].reshape(BLK // 8, 8, BLK) - limit[None])
        sum_of[side][lane] = jnp.sum(left, axis=0) + jnp.sum(right, axis=0)
        weights = jnp.concatenate([left.reshape(BLK, BLK), right.reshape(BLK, BLK)], axis=0)
        span = pl.ds(pl.multiple_of(odd * DH, DH), DH)
        values = jnp.concatenate([kv_ref[first, pair, 1, span, :], kv_ref[second, pair, 1, span, :]], axis=1)
        out_of[side][lane] = jnp.dot(values, weights.astype(BF16), preferred_element_type=F32)

    def merge(unit, lane, side):
        row = unit_ref[0, unit]
        top, old = top_of[side][lane], m_ref[row]
        new = jnp.maximum(old, top)
        a, b = jnp.exp(old - new), jnp.exp(top - new)
        m_ref[row] = new
        l_ref[row] = l_ref[row] * a + sum_of[side][lane] * b
        tiles = (DH // 8, 8, BLK)
        acc_ref[row] = (acc_ref[row].reshape(tiles) * a[None] + out_of[side][lane].reshape(tiles) * b[None]).reshape(
            DH, BLK
        )

    def step(index, _):
        for side in range(2):
            chunk = 2 * index + side
            for lane in range(UNROLL):
                merge(chunk * UNROLL + lane, lane, side)
            for lane in range(UNROLL):
                make_scores((chunk + 2) * UNROLL + lane, lane, side)
                make_output((chunk + 1) * UNROLL + lane, lane, 1 - side)
        return 0

    chunks = (total_ref[0] + UNROLL - 1) // UNROLL
    lax.fori_loop(0, (chunks + 1) // 2, step, 0)
    for head in range(2 * pairs):
        for block in range(slab):
            row = head * slab + block
            total_w = jnp.sum(l_ref[row], axis=0, keepdims=True)
            o_ref[block, head // 2, (head % 2) * DH : (head % 2 + 1) * DH, :] = (acc_ref[row] / total_w).astype(BF16)


def unpack_kernel(table_ref, o_ref, out_ref):
    groups = o_ref.shape[0]
    me = lax.axis_index("uly")

    def fetch(head):
        spot = table_ref[1, head]
        span = pl.ds(pl.multiple_of((spot % 2) * DH, DH), DH)
        return o_ref[((spot // 2) % groups) ^ me, spot // (2 * groups), span, :]

    for pair in range(H // 2):
        both = jnp.concatenate([fetch(2 * pair), fetch(2 * pair + 1)], axis=0)
        out_ref[:, pair * 2 * DH : (pair + 1) * 2 * DH] = both.T


def shards(queries, key_vectors, value_vectors, layout, counts):
    groups, slabs = lax.axis_size("uly"), lax.axis_size("doc")
    per = H // groups
    pairs = per // 2
    rows = per * groups
    shape = jax.ShapeDtypeStruct
    piece = (pairs, 2, BLK, BLK)
    table, qt, *pieces = pl.pallas_call(
        functools.partial(pack_kernel, groups),
        out_shape=(shape((8, 128), jnp.int32), shape((groups, pairs, BLK, BLK), BF16)) + (shape(piece, BF16),) * groups,
        in_specs=[VMEM] * 4,
        out_specs=(SMEM, VMEM) + (VMEM,) * groups,
        scratch_shapes=[
            pltpu.VMEM((2, H, DH, BLK), BF16),
            pltpu.VMEM((8, 128), jnp.int32),
            pltpu.SemaphoreType.DMA,
        ],
        compiler_params=PARAMS,
        name="pack",
    )(counts, queries, key_vectors, value_vectors)

    def flip(array, axis, size, bit):
        return lax.ppermute(array, axis, [(at, at ^ bit) for at in range(size)])

    swap = functools.partial(lax.all_to_all, axis_name="uly", split_axis=0, concat_axis=0, tiled=True)
    units, total = pl.pallas_call(
        functools.partial(plan_kernel, groups, slabs),
        out_shape=(shape((4, rows * KMAX // 2 + 8 * UNROLL), jnp.int32), shape((1,), jnp.int32)),
        in_specs=[SMEM, SMEM, VMEM],
        out_specs=(SMEM, SMEM),
        scratch_shapes=[pltpu.SMEM((per, groups, KMAX), jnp.int32), pltpu.SemaphoreType.DMA((per,))],
        compiler_params=PARAMS,
        name="plan",
    )(table, counts, layout)

    pieces = [piece if step == 0 else flip(piece, "uly", groups, step) for step, piece in enumerate(pieces)]
    bounds = [0, groups // 2, 3 * groups // 4, groups]
    parts = []
    for at, (begin, end) in enumerate(zip(bounds, bounds[1:])):
        some = pieces[begin:end]
        joined = pl.pallas_call(
            join_kernel,
            out_shape=shape((len(some),) + piece, BF16),
            in_specs=[SMEM] + [VMEM] * len(some),
            out_specs=VMEM,
            compiler_params=PARAMS,
            name="join",
        )(total if at == 1 else jnp.zeros((1,), jnp.int32), *some)
        if at == 2:
            joined, qt = lax.optimization_barrier((joined, qt))
            qt = swap(qt)
        gathered = {0: joined}
        bit = slabs // 2
        while bit:
            gathered.update({at ^ bit: flip(array, "doc", slabs, bit) for at, array in list(gathered.items())})
            bit //= 2
        parts.append(gathered)
    order = [(at, part) for at in range(slabs) for part in parts]
    sizes = [part[at].shape[0] for at, part in order]
    both = [pltpu.VMEM((UNROLL, BLK, 2 * BLK), F32)] * 2 + [pltpu.VMEM((UNROLL, 8, BLK), F32)] * 2
    both += [pltpu.VMEM((UNROLL, DH, BLK), F32)] * 2 + [pltpu.VMEM((UNROLL, 8, BLK), F32)] * 2
    out = pl.pallas_call(
        functools.partial(attend_kernel, sizes),
        out_shape=shape(qt.shape, BF16),
        in_specs=[SMEM, SMEM, VMEM] + [VMEM] * len(order),
        out_specs=VMEM,
        scratch_shapes=[
            pltpu.VMEM((slabs * groups,) + piece, BF16),
            pltpu.VMEM((rows + 1, 2 * DH, 2 * BLK), BF16),
            pltpu.VMEM((rows + 1, 8, BLK), F32),
            pltpu.VMEM((rows + 1, 8, BLK), F32),
            pltpu.VMEM((rows + 1, DH, BLK), F32),
            pltpu.SemaphoreType.DMA((len(order),)),
            *both,
        ],
        compiler_params=PARAMS,
        cost_estimate=pl.CostEstimate(flops=8 * 10**9, transcendentals=5 * 10**6, bytes_accessed=6 * 10**6),
        name="attend",
    )(units, total, qt, *[part[at] for at, part in order])
    return pl.pallas_call(
        unpack_kernel,
        out_shape=shape(queries.shape, BF16),
        in_specs=[SMEM, VMEM],
        out_specs=VMEM,
        compiler_params=PARAMS,
        name="unpack",
    )(table, swap(out))


def solution(mesh):
    placed = (
        P(("grp", "doc", "uly"), None),
        P(("grp", "doc", "uly"), None),
        P(("grp", "doc", "uly"), None),
        P("grp", None, None),
        P("grp", None),
    )
    return jax.shard_map(
        shards,
        mesh=mesh,
        in_specs=placed,
        out_specs=P(("grp", "doc", "uly"), None),
        check_vma=False,
    )
```

```python
import functools

import jax
import jax.numpy as jnp
from jax import lax
from jax.experimental import pallas as pl
from jax.experimental.pallas import tpu as pltpu
from jax.sharding import PartitionSpec as P

H = 32
DH = 64
BLK = 128
KMAX = 32
UNROLL = 4
BIG = 1e30
F32 = jnp.float32
BF16 = jnp.bfloat16
VMEM = pl.BlockSpec(memory_space=pltpu.VMEM)
SMEM = pl.BlockSpec(memory_space=pltpu.SMEM)
ANY = pl.BlockSpec(memory_space=pl.ANY)
PARAMS = pltpu.CompilerParams(vmem_limit_bytes=58 << 20)


def rank_heads(counts_ref, table_ref, groups):
    counts = counts_ref[...].astype(BF16)
    blocks = counts.shape[1]
    over = (((1,), (1,)), ((), ()))
    mine = lax.dot_general(counts, jnp.ones((H, blocks), BF16), over, preferred_element_type=F32)
    theirs = lax.dot_general(jnp.ones((H, blocks), BF16), counts, over, preferred_element_type=F32)
    row = lax.broadcasted_iota(jnp.int32, (H, H), 0)
    lane = lax.broadcasted_iota(jnp.int32, (H, H), 1)
    bits = groups.bit_length() - 1

    def place_of(rank):
        slot, seat = rank >> bits, rank & (groups - 1)
        return slot * groups + jnp.where((slot & 1) == 0, seat, groups - 1 - seat)

    behind = (theirs > mine) | ((theirs == mine) & (lane < row))
    rank_down = jnp.sum(jnp.where(behind, 1.0, 0.0), axis=1, keepdims=True).astype(jnp.int32)
    ahead = (mine > theirs) | ((theirs == mine) & (row < lane))
    rank_along = jnp.sum(jnp.where(ahead, 1.0, 0.0), axis=0, keepdims=True).astype(jnp.int32)
    here = place_of(jnp.broadcast_to(rank_down, (H, H))) == lane
    head_at = jnp.sum(jnp.where(here, row.astype(F32), 0.0), axis=0, keepdims=True).astype(jnp.int32)
    table_ref[0:1, 0:H] = head_at
    table_ref[1:2, 0:H] = place_of(rank_along)


def turn_heads(source, turned):
    for pair in range(H // 2):
        tile = source[:, pair * 2 * DH : (pair + 1) * 2 * DH].T
        turned[2 * pair] = tile[:DH]
        turned[2 * pair + 1] = tile[DH:]


def put_heads(slot, table_ref, k_ref, turned_q, turned_v, out_ref):
    groups = out_ref.shape[0]
    low = lax.broadcasted_iota(jnp.int32, (DH, 2 * DH), 1) < DH
    for group in range(groups):
        head = table_ref[0, slot * groups + group]
        odd = head % 2
        lanes = pl.ds(pl.multiple_of((head // 2) * (2 * DH), 2 * DH), 2 * DH)
        plain = k_ref[pl.ds(pl.multiple_of(odd * DH, DH), DH), lanes]
        other = k_ref[pl.ds(pl.multiple_of((1 - odd) * DH, DH), DH), lanes]
        other = jnp.concatenate([other[:, DH:], other[:, :DH]], axis=1)
        out_ref[group, 0] = jnp.where(low == (odd == 0), plain, other)
        out_ref[group, 1] = turned_v[head]
        out_ref[group, 2] = turned_q[head]


def pack_first_kernel(groups, counts_ref, q_ref, k_ref, v_ref, table_ref, out_ref, turned_q, turned_v, table_vmem, sem):
    rank_heads(counts_ref, table_vmem, groups)
    copy = pltpu.make_async_copy(table_vmem, table_ref, sem)
    copy.start()
    turn_heads(q_ref, turned_q)
    turn_heads(v_ref, turned_v)
    copy.wait()
    put_heads(0, table_ref, k_ref, turned_q, turned_v, out_ref)


def pack_rest_kernel(slot, table_ref, q_ref, k_ref, v_ref, out_ref, turned_q, turned_v):
    turn_heads(q_ref, turned_q)
    turn_heads(v_ref, turned_v)
    put_heads(slot, table_ref, k_ref, turned_q, turned_v, out_ref)


def plan_kernel(uly, gather, table_ref, counts_ref, layout_ref, unit_ref, total_ref, lay_ref, sem):
    slots = total_ref.shape[0]
    groups = H // slots
    parts = groups // uly
    doc = lax.axis_index("doc")
    part, rest = doc // gather, doc % gather
    group = part * uly + lax.axis_index("uly")

    def rows_at(at):
        return (at * gather + rest) * uly

    copies = [
        pltpu.make_async_copy(
            layout_ref.at[table_ref[0, slot * groups + group], pl.ds(rows_at(at), uly)],
            lay_ref.at[slot, pl.ds(at * uly, uly)],
            sem.at[slot, at],
        )
        for slot in range(slots)
        for at in range(parts)
    ]
    for copy in copies:
        copy.start()

    def local(block):
        its = block // uly
        return ((its % gather) ^ rest) * groups + (its // gather) * uly + block % uly

    for copy in copies:
        copy.wait()
    for slot in range(slots):
        head = table_ref[0, slot * groups + group]

        def idle(base, many, slot=slot):
            for extra in range(many):
                unit_ref[slot, 0, base + extra] = groups
                unit_ref[slot, 1, base + extra] = 0
                unit_ref[slot, 2, base + extra] = 0
                unit_ref[slot, 3, base + extra] = 1

        def place_row(row, base, slot=slot, head=head):
            count = counts_ref[head, rows_at(row // uly) + row % uly]

            def place_unit(step, _):
                first = lay_ref[slot, row, 2 * step]
                whole = 2 * step + 1 < count
                second = jnp.where(whole, lay_ref[slot, row, jnp.minimum(2 * step + 1, KMAX - 1)], first)
                unit_ref[slot, 0, base + step] = row
                unit_ref[slot, 1, base + step] = local(first)
                unit_ref[slot, 2, base + step] = local(second)
                unit_ref[slot, 3, base + step] = whole.astype(jnp.int32)
                return 0

            units = (count + 1) // 2
            lax.fori_loop(0, units, place_unit, 0)
            return base + units

        idle(0, 2 * UNROLL)
        total = lax.fori_loop(0, groups, place_row, jnp.int32(2 * UNROLL))
        idle(total, 4 * UNROLL)
        total_ref[slot] = total


def attend_kernel(slot, gather, unit_ref, total_ref, *refs):
    arrived, refs = refs[:gather], refs[gather:]
    earlier, refs = refs[:slot], refs[slot:]
    out_ref, kv_ref, qt_ref, qz_ref, m_ref, l_ref, acc_ref, sem = refs[:8]
    score, top_of, out_of, sum_of = (refs[8 + 2 * at : 10 + 2 * at] for at in range(4))
    rows = qt_ref.shape[0]
    copies = [pltpu.make_async_copy(arrived[0].at[:, 2], qt_ref, sem.at[0])]
    copies += [
        pltpu.make_async_copy(array.at[:, 0:2], kv_ref.at[pl.ds(at * rows, rows)], sem.at[1 + at])
        for at, array in enumerate(arrived)
    ]
    copies += [
        pltpu.make_async_copy(result, out_ref.at[:, at], sem.at[1 + gather + at]) for at, result in enumerate(earlier)
    ]
    for copy in copies:
        copy.start()
    m_ref[...] = jnp.full(m_ref.shape, -BIG, F32)
    for ref in (l_ref, acc_ref):
        ref[...] = jnp.zeros(ref.shape, F32)
    zeros = jnp.zeros((DH, BLK), BF16)
    copies[0].wait()
    for row in range(rows):
        part = qt_ref[row]
        up = jnp.concatenate([part, zeros], axis=0)
        down = jnp.concatenate([zeros, part], axis=0)
        qz_ref[row] = jnp.concatenate([up, down], axis=1)
    qz_ref[rows] = jnp.zeros((2 * DH, 2 * BLK), BF16)
    for copy in copies[1:]:
        copy.wait()

    def make_scores(unit, lane, side):
        row, first, second = unit_ref[slot, 0, unit], unit_ref[slot, 1, unit], unit_ref[slot, 2, unit]
        keys = jnp.concatenate([kv_ref[first, 0], kv_ref[second, 0]], axis=0)
        scores = jnp.dot(keys, qz_ref[row], preferred_element_type=F32)
        score[side][lane] = scores
        top = jnp.max(scores.reshape(BLK // 8, 8, 2 * BLK), axis=0)
        top = jnp.maximum(top[:, :BLK], top[:, BLK:])
        top_of[side][lane] = jnp.broadcast_to(jnp.max(top, axis=0, keepdims=True), (8, BLK))

    def make_output(unit, lane, side):
        first, second = unit_ref[slot, 1, unit], unit_ref[slot, 2, unit]
        top = top_of[side][lane]
        limit = jnp.where(unit_ref[slot, 3, unit] == 1, top, top + BIG)
        scores = score[side][lane]
        tiles = (DH // 8, 8, BLK)
        weights = [
            jnp.exp(scores[at : at + DH, lanes : lanes + BLK].reshape(tiles) - bound[None])
            for at, bound in ((0, top), (DH, limit))
            for lanes in (0, BLK)
        ]
        sum_of[side][lane] = jnp.sum(sum(weights[1:], weights[0]), axis=0)
        weights = jnp.concatenate([part.reshape(DH, BLK) for part in weights], axis=0)
        values = jnp.concatenate([kv_ref[first, 1], kv_ref[second, 1]], axis=1)
        out_of[side][lane] = jnp.dot(values, weights.astype(BF16), preferred_element_type=F32)

    def merge(unit, lane, side):
        row = unit_ref[slot, 0, unit]
        top, old = top_of[side][lane], m_ref[row]
        new = jnp.maximum(old, top)
        a, b = jnp.exp(old - new), jnp.exp(top - new)
        m_ref[row] = new
        l_ref[row] = l_ref[row] * a + sum_of[side][lane] * b
        tiles = (DH // 8, 8, BLK)
        acc_ref[row] = (acc_ref[row].reshape(tiles) * a[None] + out_of[side][lane].reshape(tiles) * b[None]).reshape(
            DH, BLK
        )

    def step(index, _):
        for side in range(2):
            chunk = 2 * index + side
            for lane in range(UNROLL):
                merge(chunk * UNROLL + lane, lane, side)
            for lane in range(UNROLL):
                make_scores((chunk + 2) * UNROLL + lane, lane, side)
                make_output((chunk + 1) * UNROLL + lane, lane, 1 - side)
        return 0

    chunks = (total_ref[slot] + UNROLL - 1) // UNROLL
    lax.fori_loop(0, (chunks + 1) // 2, step, 0)
    for row in range(rows):
        total_w = jnp.sum(l_ref[row], axis=0, keepdims=True)
        result = (acc_ref[row] / total_w).astype(BF16)
        if len(out_ref.shape) == 4:
            out_ref[row, slot] = result
        else:
            out_ref[row] = result


def unpack_kernel(table_ref, o_ref, out_ref):
    groups = o_ref.shape[0]

    def fetch(head):
        place = table_ref[1, head]
        return o_ref[place % groups, place // groups]

    for pair in range(H // 2):
        both = jnp.concatenate([fetch(2 * pair), fetch(2 * pair + 1)], axis=0)
        out_ref[:, pair * 2 * DH : (pair + 1) * 2 * DH] = both.T


def shards(queries, key_vectors, value_vectors, layout, counts):
    uly, doc = lax.axis_size("uly"), lax.axis_size("doc")
    parts = max(min(doc // 2, H // (2 * uly)), 1)
    gather = doc // parts
    groups = uly * parts
    slots = H // groups
    shape = jax.ShapeDtypeStruct
    packed_shape = shape((groups, 3, DH, BLK), BF16)
    turned = [pltpu.VMEM((H, DH, BLK), BF16)] * 2
    table, first = pl.pallas_call(
        functools.partial(pack_first_kernel, groups),
        out_shape=(shape((8, 128), jnp.int32), packed_shape),
        in_specs=[VMEM] * 4,
        out_specs=(SMEM, VMEM),
        scratch_shapes=[*turned, pltpu.VMEM((8, 128), jnp.int32), pltpu.SemaphoreType.DMA],
        compiler_params=PARAMS,
        name="pack",
    )(counts, queries, key_vectors, value_vectors)
    packed = [first]
    for slot in range(1, slots):
        packed.append(
            pl.pallas_call(
                functools.partial(pack_rest_kernel, slot),
                out_shape=packed_shape,
                in_specs=[SMEM] + [VMEM] * 3,
                out_specs=VMEM,
                scratch_shapes=turned,
                compiler_params=PARAMS,
                name="pack",
            )(table, queries, key_vectors, value_vectors)
        )
    units, totals = pl.pallas_call(
        functools.partial(plan_kernel, uly, gather),
        out_shape=(shape((slots, 4, groups * KMAX // 2 + 8 * UNROLL), jnp.int32), shape((slots,), jnp.int32)),
        in_specs=[SMEM, SMEM, VMEM],
        out_specs=(SMEM, SMEM),
        scratch_shapes=[pltpu.SMEM((slots, groups, KMAX), jnp.int32), pltpu.SemaphoreType.DMA((slots, parts))],
        compiler_params=PARAMS,
        name="plan",
    )(table, counts, layout)

    members = [
        [(part * gather + rest) * uly + at for part in range(parts) for at in range(uly)] for rest in range(gather)
    ]
    swap = functools.partial(
        lax.all_to_all,
        axis_name=("doc", "uly"),
        split_axis=0,
        concat_axis=0,
        axis_index_groups=members,
        tiled=True,
    )

    def flip(array, bit):
        return lax.ppermute(array, "doc", [(at, at ^ bit) for at in range(doc)])

    arrived = swap(packed[0])
    arrived, units, totals, *packed = lax.optimization_barrier((arrived, units, totals, *packed))
    results = []
    for slot in range(slots):
        if slot:
            arrived, *results = lax.optimization_barrier((swap(packed[slot]), *results))
        arrays, bit = {0: arrived}, gather // 2
        while bit:
            arrays.update({at ^ bit: flip(array, bit) for at, array in list(arrays.items())})
            bit //= 2
        last = slot == slots - 1
        both = [pltpu.VMEM((UNROLL, BLK, 2 * BLK), F32)] * 2 + [pltpu.VMEM((UNROLL, 8, BLK), F32)] * 2
        both += [pltpu.VMEM((UNROLL, DH, BLK), F32)] * 2 + [pltpu.VMEM((UNROLL, 8, BLK), F32)] * 2
        earlier = results if last else []
        results.append(
            pl.pallas_call(
                functools.partial(attend_kernel, slot, gather),
                out_shape=shape((groups, slots, DH, BLK) if last else (groups, DH, BLK), BF16),
                in_specs=[SMEM, SMEM] + [ANY] * (gather + len(earlier)),
                out_specs=VMEM,
                scratch_shapes=[
                    pltpu.VMEM((gather * groups, 2, DH, BLK), BF16),
                    pltpu.VMEM((groups, DH, BLK), BF16),
                    pltpu.VMEM((groups + 1, 2 * DH, 2 * BLK), BF16),
                    pltpu.VMEM((groups + 1, 8, BLK), F32),
                    pltpu.VMEM((groups + 1, 8, BLK), F32),
                    pltpu.VMEM((groups + 1, DH, BLK), F32),
                    pltpu.SemaphoreType.DMA((1 + gather + slots,)),
                    *both,
                ],
                compiler_params=PARAMS,
                cost_estimate=pl.CostEstimate(flops=10**10, transcendentals=6 * 10**6, bytes_accessed=6 * 10**6),
                name="attend",
            )(units, totals, *[arrays[at] for at in range(gather)], *earlier)
        )
    return pl.pallas_call(
        unpack_kernel,
        out_shape=shape(queries.shape, BF16),
        in_specs=[SMEM, VMEM],
        out_specs=VMEM,
        compiler_params=PARAMS,
        name="unpack",
    )(table, swap(results[-1]))


def solution(mesh):
    placed = (
        P(("grp", "doc", "uly"), None),
        P(("grp", "doc", "uly"), None),
        P(("grp", "doc", "uly"), None),
        P("grp", None, None),
        P("grp", None),
    )
    return jax.shard_map(
        shards,
        mesh=mesh,
        in_specs=placed,
        out_specs=P(("grp", "doc", "uly"), None),
        check_vma=False,
    )
```

```python
import functools

import jax
import jax.numpy as jnp
from jax import lax
from jax.experimental import pallas as pl
from jax.experimental.pallas import tpu as pltpu
from jax.sharding import PartitionSpec as P

H = 32
DH = 64
BLK = 128
KMAX = 32
UNROLL = 4
BIG = 1e30
F32 = jnp.float32
BF16 = jnp.bfloat16
VMEM = pl.BlockSpec(memory_space=pltpu.VMEM)
SMEM = pl.BlockSpec(memory_space=pltpu.SMEM)
PARAMS = pltpu.CompilerParams(vmem_limit_bytes=28 << 20)


def rank_heads(counts_ref, table_ref, groups):
    counts = counts_ref[...].astype(BF16)
    blocks = counts.shape[1]
    over = (((1,), (1,)), ((), ()))
    mine = lax.dot_general(counts, jnp.ones((H, blocks), BF16), over, preferred_element_type=F32)
    theirs = lax.dot_general(jnp.ones((H, blocks), BF16), counts, over, preferred_element_type=F32)
    row = lax.broadcasted_iota(jnp.int32, (H, H), 0)
    lane = lax.broadcasted_iota(jnp.int32, (H, H), 1)
    bits = groups.bit_length() - 1

    def place_of(rank):
        slot, seat = rank >> bits, rank & (groups - 1)
        return slot * groups + jnp.where((slot & 1) == 0, seat, groups - 1 - seat)

    behind = (theirs > mine) | ((theirs == mine) & (lane < row))
    rank_down = jnp.sum(jnp.where(behind, 1.0, 0.0), axis=1, keepdims=True).astype(jnp.int32)
    ahead = (mine > theirs) | ((theirs == mine) & (row < lane))
    rank_along = jnp.sum(jnp.where(ahead, 1.0, 0.0), axis=0, keepdims=True).astype(jnp.int32)
    here = place_of(jnp.broadcast_to(rank_down, (H, H))) == lane
    head_at = jnp.sum(jnp.where(here, row.astype(F32), 0.0), axis=0, keepdims=True).astype(jnp.int32)
    table_ref[0:1, 0:H] = head_at
    table_ref[1:2, 0:H] = place_of(rank_along)


def turn_heads(source, turned):
    for pair in range(H // 2):
        tile = source[:, pair * 2 * DH : (pair + 1) * 2 * DH].T
        turned[2 * pair] = tile[:DH]
        turned[2 * pair + 1] = tile[DH:]


def fold_head(source, head):
    odd = head % 2
    low = lax.broadcasted_iota(jnp.int32, (DH, 2 * DH), 1) < DH
    lanes = pl.ds(pl.multiple_of((head // 2) * (2 * DH), 2 * DH), 2 * DH)
    plain = source[pl.ds(pl.multiple_of(odd * DH, DH), DH), lanes]
    other = source[pl.ds(pl.multiple_of((1 - odd) * DH, DH), DH), lanes]
    return jnp.where(low == (odd == 0), plain, swap_halves(other))


def swap_halves(tile):
    return jnp.concatenate([tile[:, DH:], tile[:, :DH]], axis=1)


def turn_folded(first, second):
    low = lax.broadcasted_iota(jnp.int32, (DH, 2 * DH), 1) < DH
    turned = jnp.concatenate([first, second], axis=0).T
    early, late = turned[:DH], turned[DH:]
    return jnp.where(low, early, swap_halves(late)), jnp.where(low, swap_halves(early), late)


def pack_first_kernel(groups, counts_ref, q_ref, k_ref, v_ref, table_ref, out_ref, table_vmem, sem):
    rank_heads(counts_ref, table_vmem, groups)
    copy = pltpu.make_async_copy(table_vmem, table_ref, sem)
    copy.start()
    copy.wait()
    for group in range(groups):
        head = table_ref[0, group]
        for at, source in enumerate((k_ref, v_ref, q_ref)):
            out_ref[group, at] = fold_head(source, head)


def pack_rest_kernel(slot, table_ref, q_ref, k_ref, v_ref, out_ref, turned_q, turned_v):
    turn_heads(q_ref, turned_q)
    turn_heads(v_ref, turned_v)
    groups = out_ref.shape[0]
    for group in range(groups):
        head = table_ref[0, slot * groups + group]
        out_ref[group, 0] = fold_head(k_ref, head)
        out_ref[group, 1] = turned_v[head]
        out_ref[group, 2] = turned_q[head]


def plan_kernel(uly, gather, table_ref, counts_ref, layout_ref, unit_ref, total_ref, lay_ref, sem):
    slots = total_ref.shape[0]
    groups = H // slots
    parts = groups // uly
    doc = lax.axis_index("doc")
    part, rest = doc // gather, doc % gather
    group = part * uly + lax.axis_index("uly")

    def rows_at(at):
        return (at * gather + rest) * uly

    copies = [
        pltpu.make_async_copy(
            layout_ref.at[table_ref[0, slot * groups + group], pl.ds(rows_at(at), uly)],
            lay_ref.at[slot, pl.ds(at * uly, uly)],
            sem.at[slot, at],
        )
        for slot in range(slots)
        for at in range(parts)
    ]
    for copy in copies:
        copy.start()

    def local(block):
        its = block // uly
        return ((its % gather) ^ rest) * groups + (its // gather) * uly + block % uly

    for copy in copies:
        copy.wait()
    for slot in range(slots):
        head = table_ref[0, slot * groups + group]

        def idle(base, many, slot=slot):
            for extra in range(many):
                unit_ref[slot, 0, base + extra] = groups
                unit_ref[slot, 1, base + extra] = 0
                unit_ref[slot, 2, base + extra] = 0
                unit_ref[slot, 3, base + extra] = 1

        def place_row(row, base, slot=slot, head=head):
            count = counts_ref[head, rows_at(row // uly) + row % uly]

            def place_unit(step, _):
                first = lay_ref[slot, row, 2 * step]
                whole = 2 * step + 1 < count
                second = jnp.where(whole, lay_ref[slot, row, jnp.minimum(2 * step + 1, KMAX - 1)], first)
                unit_ref[slot, 0, base + step] = row
                unit_ref[slot, 1, base + step] = local(first)
                unit_ref[slot, 2, base + step] = local(second)
                unit_ref[slot, 3, base + step] = whole.astype(jnp.int32)
                return 0

            units = (count + 1) // 2
            lax.fori_loop(0, units, place_unit, 0)
            return base + units

        idle(0, 2 * UNROLL)
        total = lax.fori_loop(0, groups, place_row, jnp.int32(2 * UNROLL))
        idle(total, 4 * UNROLL)
        total_ref[slot] = total


def attend_kernel(slot, gather, unit_ref, total_ref, *refs):
    arrived, refs = refs[:gather], refs[gather:]
    earlier, refs = refs[:slot], refs[slot:]
    out_ref, kv_ref, qz_ref, m_ref, l_ref, acc_ref = refs[:6]
    score, top_of, out_of, sum_of = (refs[6 + 2 * at : 8 + 2 * at] for at in range(4))
    rows = arrived[0].shape[0]
    m_ref[...] = jnp.full(m_ref.shape, -BIG, F32)
    for ref in (l_ref, acc_ref):
        ref[...] = jnp.zeros(ref.shape, F32)
    zeros = jnp.zeros((DH, BLK), BF16)

    def put_query(row, part):
        up = jnp.concatenate([part, zeros], axis=0)
        down = jnp.concatenate([zeros, part], axis=0)
        qz_ref[row] = jnp.concatenate([up, down], axis=1)

    for row in range(0, rows, 2):
        pair = [arrived[0][row, 2], arrived[0][row + 1, 2]]
        for at, part in enumerate(turn_folded(*pair) if slot == 0 else pair):
            put_query(row + at, part)
    qz_ref[rows] = jnp.zeros((2 * DH, 2 * BLK), BF16)
    for at, array in enumerate(arrived):
        for row in range(0, rows, 2):
            place = at * rows + row
            kv_ref[place, 0], kv_ref[place + 1, 0] = array[row, 0], array[row + 1, 0]
            pair = [array[row, 1], array[row + 1, 1]]
            kv_ref[place, 1], kv_ref[place + 1, 1] = turn_folded(*pair) if slot == 0 else pair
    for at, result in enumerate(earlier):
        for row in range(rows):
            out_ref[row, at] = result[row]

    def make_scores(unit, lane, side):
        row, first, second = unit_ref[slot, 0, unit], unit_ref[slot, 1, unit], unit_ref[slot, 2, unit]
        keys = jnp.concatenate([kv_ref[first, 0], kv_ref[second, 0]], axis=0)
        scores = jnp.dot(keys, qz_ref[row], preferred_element_type=F32)
        score[side][lane] = scores
        top = jnp.max(scores.reshape(BLK // 8, 8, 2 * BLK), axis=0)
        top = jnp.maximum(top[:, :BLK], top[:, BLK:])
        top_of[side][lane] = jnp.broadcast_to(jnp.max(top, axis=0, keepdims=True), (8, BLK))

    def make_output(unit, lane, side):
        first, second = unit_ref[slot, 1, unit], unit_ref[slot, 2, unit]
        top = top_of[side][lane]
        limit = jnp.where(unit_ref[slot, 3, unit] == 1, top, top + BIG)
        scores = score[side][lane]
        tiles = (DH // 8, 8, BLK)
        weights = [
            jnp.exp(scores[at : at + DH, lanes : lanes + BLK].reshape(tiles) - bound[None])
            for at, bound in ((0, top), (DH, limit))
            for lanes in (0, BLK)
        ]
        sum_of[side][lane] = jnp.sum(sum(weights[1:], weights[0]), axis=0)
        weights = jnp.concatenate([part.reshape(DH, BLK) for part in weights], axis=0)
        values = jnp.concatenate([kv_ref[first, 1], kv_ref[second, 1]], axis=1)
        out_of[side][lane] = jnp.dot(values, weights.astype(BF16), preferred_element_type=F32)

    def merge(unit, lane, side):
        row = unit_ref[slot, 0, unit]
        top, old = top_of[side][lane], m_ref[row]
        new = jnp.maximum(old, top)
        a, b = jnp.exp(old - new), jnp.exp(top - new)
        m_ref[row] = new
        l_ref[row] = l_ref[row] * a + sum_of[side][lane] * b
        tiles = (DH // 8, 8, BLK)
        acc_ref[row] = (acc_ref[row].reshape(tiles) * a[None] + out_of[side][lane].reshape(tiles) * b[None]).reshape(
            DH, BLK
        )

    def step(index, _):
        for side in range(2):
            chunk = 2 * index + side
            for lane in range(UNROLL):
                merge(chunk * UNROLL + lane, lane, side)
            for lane in range(UNROLL):
                make_scores((chunk + 2) * UNROLL + lane, lane, side)
                make_output((chunk + 1) * UNROLL + lane, lane, 1 - side)
        return 0

    chunks = (total_ref[slot] + UNROLL - 1) // UNROLL
    lax.fori_loop(0, (chunks + 1) // 2, step, 0)
    for row in range(rows):
        total_w = jnp.sum(l_ref[row], axis=0, keepdims=True)
        result = (acc_ref[row] / total_w).astype(BF16)
        if len(out_ref.shape) == 4:
            out_ref[row, slot] = result
        else:
            out_ref[row] = result


def unpack_kernel(table_ref, o_ref, out_ref):
    groups = o_ref.shape[0]

    def fetch(head):
        place = table_ref[1, head]
        return o_ref[place % groups, place // groups]

    for pair in range(H // 2):
        both = jnp.concatenate([fetch(2 * pair), fetch(2 * pair + 1)], axis=0)
        out_ref[:, pair * 2 * DH : (pair + 1) * 2 * DH] = both.T


def shards(queries, key_vectors, value_vectors, layout, counts):
    uly, doc = lax.axis_size("uly"), lax.axis_size("doc")
    parts = max(min(doc // 2, H // (2 * uly)), 1)
    gather = doc // parts
    groups = uly * parts
    slots = H // groups
    shape = jax.ShapeDtypeStruct
    packed_shape = pltpu.VMEM((groups, 3, DH, BLK), BF16)
    turned = [pltpu.VMEM((H, DH, BLK), BF16)] * 2
    table, first = pl.pallas_call(
        functools.partial(pack_first_kernel, groups),
        out_shape=(shape((8, 128), jnp.int32), packed_shape),
        in_specs=[VMEM] * 4,
        out_specs=(SMEM, VMEM),
        scratch_shapes=[pltpu.VMEM((8, 128), jnp.int32), pltpu.SemaphoreType.DMA],
        compiler_params=PARAMS,
        name="pack",
    )(counts, queries, key_vectors, value_vectors)
    packed = [first]
    for slot in range(1, slots):
        packed.append(
            pl.pallas_call(
                functools.partial(pack_rest_kernel, slot),
                out_shape=packed_shape,
                in_specs=[SMEM] + [VMEM] * 3,
                out_specs=VMEM,
                scratch_shapes=turned,
                compiler_params=PARAMS,
                name="pack",
            )(table, queries, key_vectors, value_vectors)
        )
    units, totals = pl.pallas_call(
        functools.partial(plan_kernel, uly, gather),
        out_shape=(shape((slots, 4, groups * KMAX // 2 + 8 * UNROLL), jnp.int32), shape((slots,), jnp.int32)),
        in_specs=[SMEM, SMEM, VMEM],
        out_specs=(SMEM, SMEM),
        scratch_shapes=[pltpu.SMEM((slots, groups, KMAX), jnp.int32), pltpu.SemaphoreType.DMA((slots, parts))],
        compiler_params=PARAMS,
        name="plan",
    )(table, counts, layout)

    members = [
        [(part * gather + rest) * uly + at for part in range(parts) for at in range(uly)] for rest in range(gather)
    ]
    swap = functools.partial(
        lax.all_to_all,
        axis_name=("doc", "uly"),
        split_axis=0,
        concat_axis=0,
        axis_index_groups=members,
        tiled=True,
    )

    def hold(array):
        return pltpu.with_memory_space_constraint(array, pltpu.VMEM)

    def flip(array, bit):
        return lax.ppermute(array, "doc", [(at, at ^ bit) for at in range(doc)])

    arrived = swap(packed[0])
    arrived, units, totals, *packed = lax.optimization_barrier((arrived, units, totals, *packed))
    results = []
    for slot in range(slots):
        if slot:
            arrived, *results = lax.optimization_barrier((swap(packed[slot]), *results))
        arrays, bit = {0: arrived}, gather // 2
        while bit:
            arrays.update({at ^ bit: flip(array, bit) for at, array in list(arrays.items())})
            bit //= 2
        last = slot == slots - 1
        both = [pltpu.VMEM((UNROLL, BLK, 2 * BLK), F32)] * 2 + [pltpu.VMEM((UNROLL, 8, BLK), F32)] * 2
        both += [pltpu.VMEM((UNROLL, DH, BLK), F32)] * 2 + [pltpu.VMEM((UNROLL, 8, BLK), F32)] * 2
        earlier = results if last else []
        results.append(
            pl.pallas_call(
                functools.partial(attend_kernel, slot, gather),
                out_shape=pltpu.VMEM((groups, slots, DH, BLK) if last else (groups, DH, BLK), BF16),
                in_specs=[SMEM, SMEM] + [VMEM] * (gather + len(earlier)),
                out_specs=VMEM,
                scratch_shapes=[
                    pltpu.VMEM((gather * groups, 2, DH, BLK), BF16),
                    pltpu.VMEM((groups + 1, 2 * DH, 2 * BLK), BF16),
                    pltpu.VMEM((groups + 1, 8, BLK), F32),
                    pltpu.VMEM((groups + 1, 8, BLK), F32),
                    pltpu.VMEM((groups + 1, DH, BLK), F32),
                    *both,
                ],
                compiler_params=PARAMS,
                cost_estimate=pl.CostEstimate(flops=10**10, transcendentals=6 * 10**6, bytes_accessed=6 * 10**6),
                name="attend",
            )(units, totals, *[hold(arrays[at]) for at in range(gather)], *[hold(result) for result in earlier])
        )
    return pl.pallas_call(
        unpack_kernel,
        out_shape=shape(queries.shape, BF16),
        in_specs=[SMEM, VMEM],
        out_specs=VMEM,
        compiler_params=PARAMS,
        name="unpack",
    )(table, hold(swap(results[-1])))


def solution(mesh):
    placed = (
        P(("grp", "doc", "uly"), None),
        P(("grp", "doc", "uly"), None),
        P(("grp", "doc", "uly"), None),
        P("grp", None, None),
        P("grp", None),
    )
    return jax.shard_map(
        shards,
        mesh=mesh,
        in_specs=placed,
        out_specs=P(("grp", "doc", "uly"), None),
        check_vma=False,
    )
```

```python
import functools

import jax
import jax.numpy as jnp
from jax import lax
from jax.experimental import pallas as pl
from jax.experimental.pallas import tpu as pltpu
from jax.sharding import PartitionSpec as P

H = 32
DH = 64
BLK = 128
KMAX = 32
UNROLL = 4
BIG = 1e30
F32 = jnp.float32
BF16 = jnp.bfloat16
VMEM = pl.BlockSpec(memory_space=pltpu.VMEM)
SMEM = pl.BlockSpec(memory_space=pltpu.SMEM)
HBM = pl.BlockSpec(memory_space=pltpu.HBM)
PARAMS = pltpu.CompilerParams(vmem_limit_bytes=28 << 20)


def rank_heads(counts_ref, table_ref, groups):
    counts = counts_ref[...].astype(BF16)
    blocks = counts.shape[1]
    over = (((1,), (1,)), ((), ()))
    mine = lax.dot_general(counts, jnp.ones((H, blocks), BF16), over, preferred_element_type=F32)
    theirs = lax.dot_general(jnp.ones((H, blocks), BF16), counts, over, preferred_element_type=F32)
    row = lax.broadcasted_iota(jnp.int32, (H, H), 0)
    lane = lax.broadcasted_iota(jnp.int32, (H, H), 1)
    bits = groups.bit_length() - 1

    def place_of(rank):
        slot, seat = rank >> bits, rank & (groups - 1)
        return slot * groups + jnp.where((slot & 1) == 0, seat, groups - 1 - seat)

    behind = (theirs > mine) | ((theirs == mine) & (lane < row))
    rank_down = jnp.sum(jnp.where(behind, 1.0, 0.0), axis=1, keepdims=True).astype(jnp.int32)
    ahead = (mine > theirs) | ((theirs == mine) & (row < lane))
    rank_along = jnp.sum(jnp.where(ahead, 1.0, 0.0), axis=0, keepdims=True).astype(jnp.int32)
    here = place_of(jnp.broadcast_to(rank_down, (H, H))) == lane
    head_at = jnp.sum(jnp.where(here, row.astype(F32), 0.0), axis=0, keepdims=True).astype(jnp.int32)
    table_ref[0:1, 0:H] = head_at
    table_ref[1:2, 0:H] = place_of(rank_along)


def turn_heads(source, turned):
    for pair in range(H // 2):
        tile = source[:, pair * 2 * DH : (pair + 1) * 2 * DH].T
        turned[2 * pair] = tile[:DH]
        turned[2 * pair + 1] = tile[DH:]


def fold_head(source, head):
    odd = head % 2
    low = lax.broadcasted_iota(jnp.int32, (DH, 2 * DH), 1) < DH
    lanes = pl.ds(pl.multiple_of((head // 2) * (2 * DH), 2 * DH), 2 * DH)
    plain = source[pl.ds(pl.multiple_of(odd * DH, DH), DH), lanes]
    other = source[pl.ds(pl.multiple_of((1 - odd) * DH, DH), DH), lanes]
    return jnp.where(low == (odd == 0), plain, swap_halves(other))


def swap_halves(tile):
    return jnp.concatenate([tile[:, DH:], tile[:, :DH]], axis=1)


def turn_folded(first, second):
    low = lax.broadcasted_iota(jnp.int32, (DH, 2 * DH), 1) < DH
    turned = jnp.concatenate([first, second], axis=0).T
    early, late = turned[:DH], turned[DH:]
    return jnp.where(low, early, swap_halves(late)), jnp.where(low, swap_halves(early), late)


def load(arrays, buffers, sems):
    rows = arrays[0].shape[0] // 4
    copies = [
        [
            pltpu.make_async_copy(array.at[pl.ds(at * rows, rows)], buffer.at[pl.ds(at * rows, rows)], sems.at[which, at])
            for at in range(4)
        ]
        for which, (array, buffer) in enumerate(zip(arrays, buffers))
    ]
    for group in copies:
        for copy in group:
            copy.start()
    return copies


def pack_first_kernel(groups, counts_ref, q_hbm, k_hbm, v_hbm, table_ref, out_hbm, q_ref, k_ref, v_ref, sems, table_vmem, sem, out_ref, out_sem):
    copies = load((k_hbm, v_hbm, q_hbm), (k_ref, v_ref, q_ref), sems)
    rank_heads(counts_ref, table_vmem, groups)
    copy = pltpu.make_async_copy(table_vmem, table_ref, sem)
    copy.start()
    copy.wait()
    leave = []
    for which, source, places in ((0, k_ref, ((2, 0), (3, 1))), (1, v_ref, ((0, 0),)), (2, q_ref, ((1, 0),))):
        for copy in copies[which]:
            copy.wait()
        for at, slot in places:
            if at < out_ref.shape[0]:
                for group in range(groups):
                    out_ref[at, group] = fold_head(source, table_ref[0, slot * groups + group])
                leave.append(pltpu.make_async_copy(out_ref.at[at], out_hbm.at[:, at], out_sem.at[at]))
                leave[-1].start()
    for copy in leave:
        copy.wait()


def pack_rest_kernel(slot, table_ref, q_hbm, k_hbm, v_hbm, out_ref, q_ref, k_ref, v_ref, sems, turned_q, turned_v):
    copies = load((k_hbm, v_hbm, q_hbm), (k_ref, v_ref, q_ref), sems)
    for group in copies:
        for copy in group:
            copy.wait()
    turn_heads(q_ref, turned_q)
    turn_heads(v_ref, turned_v)
    groups, tiles = out_ref.shape[:2]
    for group in range(groups):
        head = table_ref[0, slot * groups + group]
        out_ref[group, 0] = turned_v[head]
        out_ref[group, 1] = turned_q[head]
        if tiles > 2:
            out_ref[group, 2] = fold_head(k_ref, table_ref[0, (slot + 1) * groups + group])


def mirror(value, size):
    bits = size.bit_length() - 1
    return sum(((value >> at) & 1) << (bits - 1 - at) for at in range(bits)) if bits else value


def plan_kernel(uly, gather, table_ref, counts_ref, layout_ref, unit_ref, total_ref, lay_ref, sem):
    slots = total_ref.shape[0]
    groups = H // slots
    parts = groups // uly
    doc = lax.axis_index("doc")
    part, rest = doc // gather, doc % gather
    group = part * uly + mirror(lax.axis_index("uly"), uly)

    def rows_at(at):
        return (at * gather + rest) * uly

    copies = [
        pltpu.make_async_copy(
            layout_ref.at[table_ref[0, slot * groups + group], pl.ds(rows_at(at), uly)],
            lay_ref.at[slot, pl.ds(at * uly, uly)],
            sem.at[slot, at],
        )
        for slot in range(slots)
        for at in range(parts)
    ]
    for copy in copies:
        copy.start()

    def local(block):
        its = block // uly
        return ((its % gather) ^ rest) * groups + (its // gather) * uly + mirror(block % uly, uly)

    for copy in copies:
        copy.wait()
    for slot in range(slots):
        head = table_ref[0, slot * groups + group]

        def idle(base, many, slot=slot):
            for extra in range(many):
                unit_ref[slot, 0, base + extra] = groups
                unit_ref[slot, 1, base + extra] = 0
                unit_ref[slot, 2, base + extra] = 0
                unit_ref[slot, 3, base + extra] = 1

        def place_row(row, base, slot=slot, head=head):
            token = (row // uly) * uly + mirror(row % uly, uly)
            count = counts_ref[head, rows_at(row // uly) + mirror(row % uly, uly)]

            def place_unit(step, _):
                first = lay_ref[slot, token, 2 * step]
                whole = 2 * step + 1 < count
                second = jnp.where(whole, lay_ref[slot, token, jnp.minimum(2 * step + 1, KMAX - 1)], first)
                unit_ref[slot, 0, base + step] = row
                unit_ref[slot, 1, base + step] = local(first)
                unit_ref[slot, 2, base + step] = local(second)
                unit_ref[slot, 3, base + step] = whole.astype(jnp.int32)
                return 0

            units = (count + 1) // 2
            lax.fori_loop(0, units, place_unit, 0)
            return base + units

        idle(0, 2 * UNROLL)
        total = lax.fori_loop(0, groups, place_row, jnp.int32(2 * UNROLL))
        idle(total, 4 * UNROLL)
        total_ref[slot] = total


def attend_kernel(slot, gather, unit_ref, total_ref, *refs):
    arrived, refs = refs[:gather], refs[gather:]
    before, refs = (refs[:gather], refs[gather:]) if slot else (arrived, refs)
    key_at = 3 if slot == 1 else 2
    earlier, refs = refs[:slot], refs[slot:]
    out_ref, kv_ref, qz_ref, m_ref, l_ref, acc_ref = refs[:6]
    score, top_of, out_of, sum_of = (refs[6 + 2 * at : 8 + 2 * at] for at in range(4))
    rows = arrived[0].shape[0]
    m_ref[...] = jnp.full(m_ref.shape, -BIG, F32)
    for ref in (l_ref, acc_ref):
        ref[...] = jnp.zeros(ref.shape, F32)
    zeros = jnp.zeros((DH, BLK), BF16)

    def put_query(row, part):
        up = jnp.concatenate([part, zeros], axis=0)
        down = jnp.concatenate([zeros, part], axis=0)
        qz_ref[row] = jnp.concatenate([up, down], axis=1)

    for row in range(0, rows, 2):
        pair = [arrived[0][row, 1], arrived[0][row + 1, 1]]
        for at, part in enumerate(turn_folded(*pair) if slot == 0 else pair):
            put_query(row + at, part)
    qz_ref[rows] = jnp.zeros((2 * DH, 2 * BLK), BF16)
    for at, (array, keys) in enumerate(zip(arrived, before)):
        for row in range(0, rows, 2):
            place = at * rows + row
            kv_ref[place, 0], kv_ref[place + 1, 0] = keys[row, key_at], keys[row + 1, key_at]
            pair = [array[row, 0], array[row + 1, 0]]
            kv_ref[place, 1], kv_ref[place + 1, 1] = turn_folded(*pair) if slot == 0 else pair
    for at, result in enumerate(earlier):
        for row in range(rows):
            out_ref[row, at] = result[row]

    def make_scores(unit, lane, side):
        row, first, second = unit_ref[slot, 0, unit], unit_ref[slot, 1, unit], unit_ref[slot, 2, unit]
        keys = jnp.concatenate([kv_ref[first, 0], kv_ref[second, 0]], axis=0)
        scores = jnp.dot(keys, qz_ref[row], preferred_element_type=F32)
        score[side][lane] = scores
        top = jnp.max(scores.reshape(BLK // 8, 8, 2 * BLK), axis=0)
        top = jnp.maximum(top[:, :BLK], top[:, BLK:])
        top_of[side][lane] = jnp.broadcast_to(jnp.max(top, axis=0, keepdims=True), (8, BLK))

    def make_output(unit, lane, side):
        first, second = unit_ref[slot, 1, unit], unit_ref[slot, 2, unit]
        top = top_of[side][lane]
        limit = jnp.where(unit_ref[slot, 3, unit] == 1, top, top + BIG)
        scores = score[side][lane]
        tiles = (DH // 8, 8, BLK)
        weights = [
            jnp.exp(scores[at : at + DH, lanes : lanes + BLK].reshape(tiles) - bound[None])
            for at, bound in ((0, top), (DH, limit))
            for lanes in (0, BLK)
        ]
        sum_of[side][lane] = jnp.sum(sum(weights[1:], weights[0]), axis=0)
        weights = jnp.concatenate([part.reshape(DH, BLK) for part in weights], axis=0)
        values = jnp.concatenate([kv_ref[first, 1], kv_ref[second, 1]], axis=1)
        out_of[side][lane] = jnp.dot(values, weights.astype(BF16), preferred_element_type=F32)

    def merge(unit, lane, side):
        row = unit_ref[slot, 0, unit]
        top, old = top_of[side][lane], m_ref[row]
        new = jnp.maximum(old, top)
        a, b = jnp.exp(old - new), jnp.exp(top - new)
        m_ref[row] = new
        l_ref[row] = l_ref[row] * a + sum_of[side][lane] * b
        tiles = (DH // 8, 8, BLK)
        acc_ref[row] = (acc_ref[row].reshape(tiles) * a[None] + out_of[side][lane].reshape(tiles) * b[None]).reshape(
            DH, BLK
        )

    def step(index, _):
        for side in range(2):
            chunk = 2 * index + side
            for lane in range(UNROLL):
                merge(chunk * UNROLL + lane, lane, side)
            for lane in range(UNROLL):
                make_scores((chunk + 2) * UNROLL + lane, lane, side)
                make_output((chunk + 1) * UNROLL + lane, lane, 1 - side)
        return 0

    chunks = (total_ref[slot] + UNROLL - 1) // UNROLL
    lax.fori_loop(0, (chunks + 1) // 2, step, 0)
    for row in range(rows):
        total_w = jnp.sum(l_ref[row], axis=0, keepdims=True)
        result = (acc_ref[row] / total_w).astype(BF16)
        if len(out_ref.shape) == 4:
            out_ref[row, slot] = result
        else:
            out_ref[row] = result


def unpack_kernel(table_ref, o_ref, out_ref):
    groups = o_ref.shape[0]

    def fetch(head):
        place = table_ref[1, head]
        return o_ref[place % groups, place // groups]

    for pair in range(H // 2):
        both = jnp.concatenate([fetch(2 * pair), fetch(2 * pair + 1)], axis=0)
        out_ref[:, pair * 2 * DH : (pair + 1) * 2 * DH] = both.T


def shards(queries, key_vectors, value_vectors, layout, counts):
    uly, doc = lax.axis_size("uly"), lax.axis_size("doc")
    parts = max(min(doc // 2, H // (2 * uly)), 1)
    gather = doc // parts
    groups = uly * parts
    slots = H // groups
    shape = jax.ShapeDtypeStruct
    slot_tiles = [2 + (slot == 0) + (slot + 1 < slots) for slot in range(slots)]
    held = [pltpu.VMEM(queries.shape, BF16)] * 3 + [pltpu.SemaphoreType.DMA((3, 4))]
    table, first = pl.pallas_call(
        functools.partial(pack_first_kernel, groups),
        out_shape=(shape((8, 128), jnp.int32), shape((groups, slot_tiles[0], DH, BLK), BF16)),
        in_specs=[VMEM] + [HBM] * 3,
        out_specs=(SMEM, HBM),
        scratch_shapes=[
            *held,
            pltpu.VMEM((8, 128), jnp.int32),
            pltpu.SemaphoreType.DMA,
            pltpu.VMEM((slot_tiles[0], groups, DH, BLK), BF16),
            pltpu.SemaphoreType.DMA((slot_tiles[0],)),
        ],
        compiler_params=PARAMS,
        name="pack",
    )(counts, queries, key_vectors, value_vectors)
    packed = [first]
    for slot in range(1, slots):
        packed.append(
            pl.pallas_call(
                functools.partial(pack_rest_kernel, slot),
                out_shape=pltpu.VMEM((groups, slot_tiles[slot], DH, BLK), BF16),
                in_specs=[SMEM] + [HBM] * 3,
                out_specs=VMEM,
                scratch_shapes=[*held] + [pltpu.VMEM((H, DH, BLK), BF16)] * 2,
                compiler_params=PARAMS,
                name="pack",
            )(table, queries, key_vectors, value_vectors)
        )
    units, totals = pl.pallas_call(
        functools.partial(plan_kernel, uly, gather),
        out_shape=(shape((slots, 4, groups * KMAX // 2 + 8 * UNROLL), jnp.int32), shape((slots,), jnp.int32)),
        in_specs=[SMEM, SMEM, VMEM],
        out_specs=(SMEM, SMEM),
        scratch_shapes=[pltpu.SMEM((slots, groups, KMAX), jnp.int32), pltpu.SemaphoreType.DMA((slots, parts))],
        compiler_params=PARAMS,
        name="plan",
    )(table, counts, layout)

    members = [
        [(part * gather + rest) * uly + mirror(at, uly) for part in range(parts) for at in range(uly)]
        for rest in range(gather)
    ]
    swap = functools.partial(
        lax.all_to_all,
        axis_name=("doc", "uly"),
        split_axis=0,
        concat_axis=0,
        axis_index_groups=members,
        tiled=True,
    )

    def hold(array):
        return pltpu.with_memory_space_constraint(array, pltpu.VMEM)

    def flip(array, bit):
        return lax.ppermute(array, "doc", [(at, at ^ bit) for at in range(doc)])

    arrived = swap(packed[0])
    arrived, units, totals, *packed = lax.optimization_barrier((arrived, units, totals, *packed))
    results, arrays = [], {}
    for slot in range(slots):
        before = arrays if slot else {}
        if slot:
            arrived, *results = lax.optimization_barrier((swap(packed[slot]), *results))
        arrays, bit = {0: arrived}, gather // 2
        while bit:
            arrays.update({at ^ bit: flip(array, bit) for at, array in list(arrays.items())})
            bit //= 2
        last = slot == slots - 1
        both = [pltpu.VMEM((UNROLL, BLK, 2 * BLK), F32)] * 2 + [pltpu.VMEM((UNROLL, 8, BLK), F32)] * 2
        both += [pltpu.VMEM((UNROLL, DH, BLK), F32)] * 2 + [pltpu.VMEM((UNROLL, 8, BLK), F32)] * 2
        earlier = results if last else []
        results.append(
            pl.pallas_call(
                functools.partial(attend_kernel, slot, gather),
                out_shape=pltpu.VMEM((groups, slots, DH, BLK) if last else (groups, DH, BLK), BF16),
                in_specs=[SMEM, SMEM] + [VMEM] * (gather + len(before) + len(earlier)),
                out_specs=VMEM,
                scratch_shapes=[
                    pltpu.VMEM((gather * groups, 2, DH, BLK), BF16),
                    pltpu.VMEM((groups + 1, 2 * DH, 2 * BLK), BF16),
                    pltpu.VMEM((groups + 1, 8, BLK), F32),
                    pltpu.VMEM((groups + 1, 8, BLK), F32),
                    pltpu.VMEM((groups + 1, DH, BLK), F32),
                    *both,
                ],
                compiler_params=PARAMS,
                cost_estimate=pl.CostEstimate(flops=10**10, transcendentals=6 * 10**6, bytes_accessed=6 * 10**6),
                name="attend",
            )(units, totals, *[hold(part[at]) for part in (arrays, before) for at in range(len(part))], *[hold(result) for result in earlier])
        )
    return pl.pallas_call(
        unpack_kernel,
        out_shape=shape(queries.shape, BF16),
        in_specs=[SMEM, VMEM],
        out_specs=VMEM,
        compiler_params=PARAMS,
        name="unpack",
    )(table, hold(swap(results[-1])))


def solution(mesh):
    placed = (
        P(("grp", "doc", "uly"), None),
        P(("grp", "doc", "uly"), None),
        P(("grp", "doc", "uly"), None),
        P("grp", None, None),
        P("grp", None),
    )
    return jax.shard_map(
        shards,
        mesh=mesh,
        in_specs=placed,
        out_specs=P(("grp", "doc", "uly"), None),
        check_vma=False,
    )
```

```python
import functools

import jax
import jax.numpy as jnp
from jax import lax
from jax.experimental import pallas as pl
from jax.experimental.pallas import tpu as pltpu
from jax.sharding import PartitionSpec as P

H = 32
DH = 64
BLK = 128
KMAX = 32
UNROLL = 4
BIG = 1e30
F32 = jnp.float32
BF16 = jnp.bfloat16
VMEM = pl.BlockSpec(memory_space=pltpu.VMEM)
SMEM = pl.BlockSpec(memory_space=pltpu.SMEM)
HBM = pl.BlockSpec(memory_space=pltpu.HBM)
PARAMS = pltpu.CompilerParams(vmem_limit_bytes=28 << 20)


def rank_heads(counts_ref, table_ref, groups):
    counts = counts_ref[...].astype(BF16)
    blocks = counts.shape[1]
    over = (((1,), (1,)), ((), ()))
    mine = lax.dot_general(counts, jnp.ones((H, blocks), BF16), over, preferred_element_type=F32)
    theirs = lax.dot_general(jnp.ones((H, blocks), BF16), counts, over, preferred_element_type=F32)
    row = lax.broadcasted_iota(jnp.int32, (H, H), 0)
    lane = lax.broadcasted_iota(jnp.int32, (H, H), 1)
    bits = groups.bit_length() - 1

    def place_of(rank):
        slot, seat = rank >> bits, rank & (groups - 1)
        return slot * groups + jnp.where((slot & 1) == 0, seat, groups - 1 - seat)

    behind = (theirs > mine) | ((theirs == mine) & (lane < row))
    rank_down = jnp.sum(jnp.where(behind, 1.0, 0.0), axis=1, keepdims=True).astype(jnp.int32)
    ahead = (mine > theirs) | ((theirs == mine) & (row < lane))
    rank_along = jnp.sum(jnp.where(ahead, 1.0, 0.0), axis=0, keepdims=True).astype(jnp.int32)
    here = place_of(jnp.broadcast_to(rank_down, (H, H))) == lane
    head_at = jnp.sum(jnp.where(here, row.astype(F32), 0.0), axis=0, keepdims=True).astype(jnp.int32)
    table_ref[0:1, 0:H] = head_at
    table_ref[1:2, 0:H] = place_of(rank_along)


def turn_heads(source, turned):
    for pair in range(H // 2):
        tile = source[:, pair * 2 * DH : (pair + 1) * 2 * DH].T
        turned[2 * pair] = tile[:DH]
        turned[2 * pair + 1] = tile[DH:]


def fold_head(source, head):
    odd = head % 2
    low = lax.broadcasted_iota(jnp.int32, (DH, 2 * DH), 1) < DH
    lanes = pl.ds(pl.multiple_of((head // 2) * (2 * DH), 2 * DH), 2 * DH)
    plain = source[pl.ds(pl.multiple_of(odd * DH, DH), DH), lanes]
    other = source[pl.ds(pl.multiple_of((1 - odd) * DH, DH), DH), lanes]
    return jnp.where(low == (odd == 0), plain, swap_halves(other))


def swap_halves(tile):
    return jnp.concatenate([tile[:, DH:], tile[:, :DH]], axis=1)


def turn_folded(first, second):
    low = lax.broadcasted_iota(jnp.int32, (DH, 2 * DH), 1) < DH
    turned = jnp.concatenate([first, second], axis=0).T
    early, late = turned[:DH], turned[DH:]
    return jnp.where(low, early, swap_halves(late)), jnp.where(low, swap_halves(early), late)


def load(arrays, buffers, sems):
    rows = arrays[0].shape[0] // 4
    copies = [
        [
            pltpu.make_async_copy(array.at[pl.ds(at * rows, rows)], buffer.at[pl.ds(at * rows, rows)], sems.at[which, at])
            for at in range(4)
        ]
        for which, (array, buffer) in enumerate(zip(arrays, buffers))
    ]
    for group in copies:
        for copy in group:
            copy.start()
    return copies


def pack_first_kernel(
    groups, counts_hbm, q_hbm, k_hbm, v_hbm, table_ref, out_hbm, q_ref, k_ref, v_ref, sems, counts_ref, table_vmem, sem, out_ref, out_sem
):
    fetch = pltpu.make_async_copy(counts_hbm, counts_ref, sem)
    fetch.start()
    copies = load((k_hbm, v_hbm, q_hbm), (k_ref, v_ref, q_ref), sems)
    fetch.wait()
    rank_heads(counts_ref, table_vmem, groups)
    copy = pltpu.make_async_copy(table_vmem, table_ref, sem)
    copy.start()
    copy.wait()
    leave = []
    for which, source, places in ((0, k_ref, ((2, 0), (3, 1))), (1, v_ref, ((0, 0),)), (2, q_ref, ((1, 0),))):
        for copy in copies[which]:
            copy.wait()
        for at, slot in places:
            if at < out_ref.shape[0]:
                for group in range(groups):
                    out_ref[at, group] = fold_head(source, table_ref[0, slot * groups + group])
                leave.append(pltpu.make_async_copy(out_ref.at[at], out_hbm.at[:, at], out_sem.at[at]))
                leave[-1].start()
    for copy in leave:
        copy.wait()


def pack_rest_kernel(slot, table_ref, q_hbm, k_hbm, v_hbm, out_ref, q_ref, k_ref, v_ref, sems, turned_q, turned_v):
    copies = load((k_hbm, v_hbm, q_hbm), (k_ref, v_ref, q_ref), sems)
    for group in copies:
        for copy in group:
            copy.wait()
    turn_heads(q_ref, turned_q)
    turn_heads(v_ref, turned_v)
    groups, tiles = out_ref.shape[:2]
    for group in range(groups):
        head = table_ref[0, slot * groups + group]
        out_ref[group, 0] = turned_v[head]
        out_ref[group, 1] = turned_q[head]
        if tiles > 2:
            out_ref[group, 2] = fold_head(k_ref, table_ref[0, (slot + 1) * groups + group])


def mirror(value, size):
    bits = size.bit_length() - 1
    return sum(((value >> at) & 1) << (bits - 1 - at) for at in range(bits)) if bits else value


def plan_kernel(uly, gather, table_ref, counts_ref, layout_ref, unit_ref, total_ref, lay_ref, sem):
    slots = total_ref.shape[0]
    groups = H // slots
    parts = groups // uly
    doc = lax.axis_index("doc")
    part, rest = doc // gather, doc % gather
    group = part * uly + mirror(lax.axis_index("uly"), uly)

    def rows_at(at):
        return (at * gather + rest) * uly

    copies = [
        pltpu.make_async_copy(
            layout_ref.at[table_ref[0, slot * groups + group], pl.ds(rows_at(at), uly)],
            lay_ref.at[slot, pl.ds(at * uly, uly)],
            sem.at[slot, at],
        )
        for slot in range(slots)
        for at in range(parts)
    ]
    for copy in copies:
        copy.start()

    def local(block):
        its = block // uly
        return ((its % gather) ^ rest) * groups + (its // gather) * uly + mirror(block % uly, uly)

    for copy in copies:
        copy.wait()
    for slot in range(slots):
        head = table_ref[0, slot * groups + group]

        def idle(base, many, slot=slot):
            for extra in range(many):
                unit_ref[slot, 0, base + extra] = groups
                unit_ref[slot, 1, base + extra] = 0
                unit_ref[slot, 2, base + extra] = 0
                unit_ref[slot, 3, base + extra] = 1

        def place_row(row, base, slot=slot, head=head):
            token = (row // uly) * uly + mirror(row % uly, uly)
            count = counts_ref[head, rows_at(row // uly) + mirror(row % uly, uly)]

            def place_unit(step, _):
                first = lay_ref[slot, token, 2 * step]
                whole = 2 * step + 1 < count
                second = jnp.where(whole, lay_ref[slot, token, jnp.minimum(2 * step + 1, KMAX - 1)], first)
                unit_ref[slot, 0, base + step] = row
                unit_ref[slot, 1, base + step] = local(first)
                unit_ref[slot, 2, base + step] = local(second)
                unit_ref[slot, 3, base + step] = whole.astype(jnp.int32)
                return 0

            units = (count + 1) // 2
            lax.fori_loop(0, units, place_unit, 0)
            return base + units

        idle(0, 2 * UNROLL)
        total = lax.fori_loop(0, groups, place_row, jnp.int32(2 * UNROLL))
        idle(total, 4 * UNROLL)
        total_ref[slot] = total


def attend_kernel(slot, gather, unit_ref, total_ref, *refs):
    arrived, refs = refs[:gather], refs[gather:]
    before, refs = (refs[:gather], refs[gather:]) if slot else (arrived, refs)
    key_at = 3 if slot == 1 else 2
    earlier, refs = refs[:slot], refs[slot:]
    out_ref, kv_ref, qz_ref, m_ref, l_ref, acc_ref = refs[:6]
    score, top_of, out_of, sum_of = (refs[6 + 2 * at : 8 + 2 * at] for at in range(4))
    rows = arrived[0].shape[0]
    m_ref[...] = jnp.full(m_ref.shape, -BIG, F32)
    for ref in (l_ref, acc_ref):
        ref[...] = jnp.zeros(ref.shape, F32)
    zeros = jnp.zeros((DH, BLK), BF16)

    def put_query(row, part):
        up = jnp.concatenate([part, zeros], axis=0)
        down = jnp.concatenate([zeros, part], axis=0)
        qz_ref[row] = jnp.concatenate([up, down], axis=1)

    for row in range(0, rows, 2):
        pair = [arrived[0][row, 1], arrived[0][row + 1, 1]]
        for at, part in enumerate(turn_folded(*pair) if slot == 0 else pair):
            put_query(row + at, part)
    qz_ref[rows] = jnp.zeros((2 * DH, 2 * BLK), BF16)
    for at, (array, keys) in enumerate(zip(arrived, before)):
        for row in range(0, rows, 2):
            place = at * rows + row
            kv_ref[place, 0], kv_ref[place + 1, 0] = keys[row, key_at], keys[row + 1, key_at]
            pair = [array[row, 0], array[row + 1, 0]]
            kv_ref[place, 1], kv_ref[place + 1, 1] = turn_folded(*pair) if slot == 0 else pair
    for at, result in enumerate(earlier):
        for row in range(rows):
            out_ref[row, at] = result[row]

    def make_scores(unit, lane, side):
        row, first, second = unit_ref[slot, 0, unit], unit_ref[slot, 1, unit], unit_ref[slot, 2, unit]
        keys = jnp.concatenate([kv_ref[first, 0], kv_ref[second, 0]], axis=0)
        scores = jnp.dot(keys, qz_ref[row], preferred_element_type=F32)
        score[side][lane] = scores
        top = jnp.max(scores.reshape(BLK // 8, 8, 2 * BLK), axis=0)
        top = jnp.maximum(top[:, :BLK], top[:, BLK:])
        top_of[side][lane] = jnp.broadcast_to(jnp.max(top, axis=0, keepdims=True), (8, BLK))

    def make_output(unit, lane, side):
        first, second = unit_ref[slot, 1, unit], unit_ref[slot, 2, unit]
        top = top_of[side][lane]
        limit = jnp.where(unit_ref[slot, 3, unit] == 1, top, top + BIG)
        scores = score[side][lane]
        tiles = (DH // 8, 8, BLK)
        weights = [
            jnp.exp(scores[at : at + DH, lanes : lanes + BLK].reshape(tiles) - bound[None])
            for at, bound in ((0, top), (DH, limit))
            for lanes in (0, BLK)
        ]
        sum_of[side][lane] = jnp.sum(sum(weights[1:], weights[0]), axis=0)
        weights = jnp.concatenate([part.reshape(DH, BLK) for part in weights], axis=0)
        values = jnp.concatenate([kv_ref[first, 1], kv_ref[second, 1]], axis=1)
        out_of[side][lane] = jnp.dot(values, weights.astype(BF16), preferred_element_type=F32)

    def merge(unit, lane, side):
        row = unit_ref[slot, 0, unit]
        top, old = top_of[side][lane], m_ref[row]
        new = jnp.maximum(old, top)
        a, b = jnp.exp(old - new), jnp.exp(top - new)
        m_ref[row] = new
        l_ref[row] = l_ref[row] * a + sum_of[side][lane] * b
        tiles = (DH // 8, 8, BLK)
        acc_ref[row] = (acc_ref[row].reshape(tiles) * a[None] + out_of[side][lane].reshape(tiles) * b[None]).reshape(
            DH, BLK
        )

    def step(index, _):
        for side in range(2):
            chunk = 2 * index + side
            for lane in range(UNROLL):
                merge(chunk * UNROLL + lane, lane, side)
            for lane in range(UNROLL):
                make_scores((chunk + 2) * UNROLL + lane, lane, side)
                make_output((chunk + 1) * UNROLL + lane, lane, 1 - side)
        return 0

    chunks = (total_ref[slot] + UNROLL - 1) // UNROLL
    lax.fori_loop(0, (chunks + 1) // 2, step, 0)
    for row in range(rows):
        total_w = jnp.sum(l_ref[row], axis=0, keepdims=True)
        result = (acc_ref[row] / total_w).astype(BF16)
        if len(out_ref.shape) == 4:
            out_ref[row, slot] = result
        else:
            out_ref[row] = result


def unpack_kernel(table_ref, o_ref, out_ref):
    groups = o_ref.shape[0]

    def fetch(head):
        place = table_ref[1, head]
        return o_ref[place % groups, place // groups]

    for pair in range(H // 2):
        both = jnp.concatenate([fetch(2 * pair), fetch(2 * pair + 1)], axis=0)
        out_ref[:, pair * 2 * DH : (pair + 1) * 2 * DH] = both.T


def shards(queries, key_vectors, value_vectors, layout, counts):
    uly, doc = lax.axis_size("uly"), lax.axis_size("doc")
    parts = max(min(doc // 2, H // (2 * uly)), 1)
    gather = doc // parts
    groups = uly * parts
    slots = H // groups
    shape = jax.ShapeDtypeStruct
    queries, key_vectors, value_vectors = (
        pltpu.with_memory_space_constraint(array, pltpu.HBM) for array in (queries, key_vectors, value_vectors)
    )
    slot_tiles = [2 + (slot == 0) + (slot + 1 < slots) for slot in range(slots)]
    held = [pltpu.VMEM(queries.shape, BF16)] * 3 + [pltpu.SemaphoreType.DMA((3, 4))]
    table, first = pl.pallas_call(
        functools.partial(pack_first_kernel, groups),
        out_shape=(shape((8, 128), jnp.int32), pltpu.HBM((groups, slot_tiles[0], DH, BLK), BF16)),
        in_specs=[HBM] * 4,
        out_specs=(SMEM, HBM),
        scratch_shapes=[
            *held,
            pltpu.VMEM(counts.shape, jnp.int32),
            pltpu.VMEM((8, 128), jnp.int32),
            pltpu.SemaphoreType.DMA,
            pltpu.VMEM((slot_tiles[0], groups, DH, BLK), BF16),
            pltpu.SemaphoreType.DMA((slot_tiles[0],)),
        ],
        compiler_params=PARAMS,
        name="pack",
    )(pltpu.with_memory_space_constraint(counts, pltpu.HBM), queries, key_vectors, value_vectors)
    packed = [first]
    for slot in range(1, slots):
        packed.append(
            pl.pallas_call(
                functools.partial(pack_rest_kernel, slot),
                out_shape=pltpu.VMEM((groups, slot_tiles[slot], DH, BLK), BF16),
                in_specs=[SMEM] + [HBM] * 3,
                out_specs=VMEM,
                scratch_shapes=[*held] + [pltpu.VMEM((H, DH, BLK), BF16)] * 2,
                compiler_params=PARAMS,
                name="pack",
            )(table, queries, key_vectors, value_vectors)
        )
    units, totals = pl.pallas_call(
        functools.partial(plan_kernel, uly, gather),
        out_shape=(shape((slots, 4, groups * KMAX // 2 + 8 * UNROLL), jnp.int32), shape((slots,), jnp.int32)),
        in_specs=[SMEM, SMEM, VMEM],
        out_specs=(SMEM, SMEM),
        scratch_shapes=[pltpu.SMEM((slots, groups, KMAX), jnp.int32), pltpu.SemaphoreType.DMA((slots, parts))],
        compiler_params=PARAMS,
        name="plan",
    )(table, counts, layout)

    members = [
        [(part * gather + rest) * uly + mirror(at, uly) for part in range(parts) for at in range(uly)]
        for rest in range(gather)
    ]
    swap = functools.partial(
        lax.all_to_all,
        axis_name=("doc", "uly"),
        split_axis=0,
        concat_axis=0,
        axis_index_groups=members,
        tiled=True,
    )

    def hold(array):
        return pltpu.with_memory_space_constraint(array, pltpu.VMEM)

    def flip(array, bit):
        return lax.ppermute(array, "doc", [(at, at ^ bit) for at in range(doc)])

    arrived = swap(packed[0])
    arrived, units, totals, *packed = lax.optimization_barrier((arrived, units, totals, *packed))
    results, arrays = [], {}
    for slot in range(slots):
        before = arrays if slot else {}
        if slot:
            arrived, *results = lax.optimization_barrier((swap(packed[slot]), *results))
        arrays, bit = {0: arrived}, gather // 2
        while bit:
            arrays.update({at ^ bit: flip(array, bit) for at, array in list(arrays.items())})
            bit //= 2
        last = slot == slots - 1
        both = [pltpu.VMEM((UNROLL, BLK, 2 * BLK), F32)] * 2 + [pltpu.VMEM((UNROLL, 8, BLK), F32)] * 2
        both += [pltpu.VMEM((UNROLL, DH, BLK), F32)] * 2 + [pltpu.VMEM((UNROLL, 8, BLK), F32)] * 2
        earlier = results if last else []
        results.append(
            pl.pallas_call(
                functools.partial(attend_kernel, slot, gather),
                out_shape=pltpu.VMEM((groups, slots, DH, BLK) if last else (groups, DH, BLK), BF16),
                in_specs=[SMEM, SMEM] + [VMEM] * (gather + len(before) + len(earlier)),
                out_specs=VMEM,
                scratch_shapes=[
                    pltpu.VMEM((gather * groups, 2, DH, BLK), BF16),
                    pltpu.VMEM((groups + 1, 2 * DH, 2 * BLK), BF16),
                    pltpu.VMEM((groups + 1, 8, BLK), F32),
                    pltpu.VMEM((groups + 1, 8, BLK), F32),
                    pltpu.VMEM((groups + 1, DH, BLK), F32),
                    *both,
                ],
                compiler_params=PARAMS,
                cost_estimate=pl.CostEstimate(flops=10**10, transcendentals=6 * 10**6, bytes_accessed=6 * 10**6),
                name="attend",
            )(units, totals, *[hold(part[at]) for part in (arrays, before) for at in range(len(part))], *[hold(result) for result in earlier])
        )
    return pl.pallas_call(
        unpack_kernel,
        out_shape=shape(queries.shape, BF16),
        in_specs=[SMEM, VMEM],
        out_specs=VMEM,
        compiler_params=PARAMS,
        name="unpack",
    )(table, hold(swap(results[-1])))


def solution(mesh):
    placed = (
        P(("grp", "doc", "uly"), None),
        P(("grp", "doc", "uly"), None),
        P(("grp", "doc", "uly"), None),
        P("grp", None, None),
        P("grp", None),
    )
    return jax.shard_map(
        shards,
        mesh=mesh,
        in_specs=placed,
        out_specs=P(("grp", "doc", "uly"), None),
        check_vma=False,
    )
```

```python
import functools

import jax
import jax.numpy as jnp
from jax import lax
from jax.experimental import pallas as pl
from jax.experimental.pallas import tpu as pltpu
from jax.sharding import PartitionSpec as P

H = 32
DH = 64
BLK = 128
KMAX = 32
UNROLL = 6
BIG = 1e30
F32 = jnp.float32
BF16 = jnp.bfloat16
VMEM = pl.BlockSpec(memory_space=pltpu.VMEM)
SMEM = pl.BlockSpec(memory_space=pltpu.SMEM)
HBM = pl.BlockSpec(memory_space=pltpu.HBM)
PARAMS = pltpu.CompilerParams(vmem_limit_bytes=28 << 20)


def rank_heads(counts_ref, table_ref, groups):
    counts = counts_ref[...].astype(BF16)
    blocks = counts.shape[1]
    over = (((1,), (1,)), ((), ()))
    mine = lax.dot_general(counts, jnp.ones((H, blocks), BF16), over, preferred_element_type=F32)
    theirs = lax.dot_general(jnp.ones((H, blocks), BF16), counts, over, preferred_element_type=F32)
    row = lax.broadcasted_iota(jnp.int32, (H, H), 0)
    lane = lax.broadcasted_iota(jnp.int32, (H, H), 1)
    bits = groups.bit_length() - 1

    def place_of(rank):
        slot, seat = rank >> bits, rank & (groups - 1)
        return slot * groups + jnp.where((slot & 1) == 0, seat, groups - 1 - seat)

    behind = (theirs > mine) | ((theirs == mine) & (lane < row))
    rank_down = jnp.sum(jnp.where(behind, 1.0, 0.0), axis=1, keepdims=True).astype(jnp.int32)
    ahead = (mine > theirs) | ((theirs == mine) & (row < lane))
    rank_along = jnp.sum(jnp.where(ahead, 1.0, 0.0), axis=0, keepdims=True).astype(jnp.int32)
    here = place_of(jnp.broadcast_to(rank_down, (H, H))) == lane
    head_at = jnp.sum(jnp.where(here, row.astype(F32), 0.0), axis=0, keepdims=True).astype(jnp.int32)
    table_ref[0:1, 0:H] = head_at
    table_ref[1:2, 0:H] = place_of(rank_along)


def turn_heads(source, turned):
    for pair in range(H // 2):
        tile = source[:, pair * 2 * DH : (pair + 1) * 2 * DH].T
        turned[2 * pair] = tile[:DH]
        turned[2 * pair + 1] = tile[DH:]


def fold_head(source, head):
    odd = head % 2
    low = lax.broadcasted_iota(jnp.int32, (DH, 2 * DH), 1) < DH
    lanes = pl.ds(pl.multiple_of((head // 2) * (2 * DH), 2 * DH), 2 * DH)
    plain = source[pl.ds(pl.multiple_of(odd * DH, DH), DH), lanes]
    other = source[pl.ds(pl.multiple_of((1 - odd) * DH, DH), DH), lanes]
    return jnp.where(low == (odd == 0), plain, swap_halves(other))


def swap_halves(tile):
    return jnp.concatenate([tile[:, DH:], tile[:, :DH]], axis=1)


def turn_folded(first, second):
    low = lax.broadcasted_iota(jnp.int32, (DH, 2 * DH), 1) < DH
    turned = jnp.concatenate([first, second], axis=0).T
    early, late = turned[:DH], turned[DH:]
    return jnp.where(low, early, swap_halves(late)), jnp.where(low, swap_halves(early), late)


def load(arrays, buffers, sems):
    rows = arrays[0].shape[0] // 4
    copies = [
        [
            pltpu.make_async_copy(array.at[pl.ds(at * rows, rows)], buffer.at[pl.ds(at * rows, rows)], sems.at[which, at])
            for at in range(4)
        ]
        for which, (array, buffer) in enumerate(zip(arrays, buffers))
    ]
    for group in copies:
        for copy in group:
            copy.start()
    return copies


def pack_first_kernel(
    groups, counts_hbm, q_hbm, k_hbm, v_hbm, table_ref, out_hbm, q_ref, k_ref, v_ref, sems, counts_ref, table_vmem, sem, out_ref, out_sem
):
    fetch = pltpu.make_async_copy(counts_hbm, counts_ref, sem)
    fetch.start()
    copies = load((k_hbm, v_hbm, q_hbm), (k_ref, v_ref, q_ref), sems)
    fetch.wait()
    rank_heads(counts_ref, table_vmem, groups)
    copy = pltpu.make_async_copy(table_vmem, table_ref, sem)
    copy.start()
    copy.wait()
    leave = []
    for which, source, places in ((0, k_ref, ((2, 0), (3, 1))), (1, v_ref, ((0, 0),)), (2, q_ref, ((1, 0),))):
        for copy in copies[which]:
            copy.wait()
        for at, slot in places:
            if at < out_ref.shape[0]:
                for group in range(groups):
                    out_ref[at, group] = fold_head(source, table_ref[0, slot * groups + group])
                leave.append(pltpu.make_async_copy(out_ref.at[at], out_hbm.at[:, at], out_sem.at[at]))
                leave[-1].start()
    for copy in leave:
        copy.wait()


def pack_rest_kernel(slot, table_ref, q_hbm, k_hbm, v_hbm, out_ref, q_ref, k_ref, v_ref, sems, turned_q, turned_v):
    copies = load((k_hbm, v_hbm, q_hbm), (k_ref, v_ref, q_ref), sems)
    for group in copies:
        for copy in group:
            copy.wait()
    turn_heads(q_ref, turned_q)
    turn_heads(v_ref, turned_v)
    groups, tiles = out_ref.shape[:2]
    for group in range(groups):
        head = table_ref[0, slot * groups + group]
        out_ref[group, 0] = turned_v[head]
        out_ref[group, 1] = turned_q[head]
        if tiles > 2:
            out_ref[group, 2] = fold_head(k_ref, table_ref[0, (slot + 1) * groups + group])


def mirror(value, size):
    bits = size.bit_length() - 1
    return sum(((value >> at) & 1) << (bits - 1 - at) for at in range(bits)) if bits else value


def plan_kernel(uly, gather, table_ref, counts_ref, layout_ref, unit_ref, total_ref, lay_ref, sem):
    slots = total_ref.shape[0]
    groups = H // slots
    parts = groups // uly
    doc = lax.axis_index("doc")
    part, rest = doc // gather, doc % gather
    group = part * uly + mirror(lax.axis_index("uly"), uly)

    def rows_at(at):
        return (at * gather + rest) * uly

    copies = [
        pltpu.make_async_copy(
            layout_ref.at[table_ref[0, slot * groups + group], pl.ds(rows_at(at), uly)],
            lay_ref.at[slot, pl.ds(at * uly, uly)],
            sem.at[slot, at],
        )
        for slot in range(slots)
        for at in range(parts)
    ]
    for copy in copies:
        copy.start()

    def local(block):
        its = block // uly
        return ((its % gather) ^ rest) * groups + (its // gather) * uly + mirror(block % uly, uly)

    for copy in copies:
        copy.wait()
    for slot in range(slots):
        head = table_ref[0, slot * groups + group]

        def idle(base, many, slot=slot):
            for extra in range(many):
                unit_ref[slot, 0, base + extra] = groups
                unit_ref[slot, 1, base + extra] = 0
                unit_ref[slot, 2, base + extra] = 0
                unit_ref[slot, 3, base + extra] = 1

        def place_row(row, base, slot=slot, head=head):
            token = (row // uly) * uly + mirror(row % uly, uly)
            count = counts_ref[head, rows_at(row // uly) + mirror(row % uly, uly)]

            def place_unit(step, _):
                first = lay_ref[slot, token, 2 * step]
                whole = 2 * step + 1 < count
                second = jnp.where(whole, lay_ref[slot, token, jnp.minimum(2 * step + 1, KMAX - 1)], first)
                unit_ref[slot, 0, base + step] = row
                unit_ref[slot, 1, base + step] = local(first)
                unit_ref[slot, 2, base + step] = local(second)
                unit_ref[slot, 3, base + step] = whole.astype(jnp.int32)
                return 0

            units = (count + 1) // 2
            lax.fori_loop(0, units, place_unit, 0)
            return base + units

        idle(0, 2 * UNROLL)
        total = lax.fori_loop(0, groups, place_row, jnp.int32(2 * UNROLL))
        idle(total, 4 * UNROLL)
        total_ref[slot] = total


def attend_kernel(slot, gather, unit_ref, total_ref, *refs):
    arrived, refs = refs[:gather], refs[gather:]
    before, refs = (refs[:gather], refs[gather:]) if slot else (arrived, refs)
    key_at = 3 if slot == 1 else 2
    earlier, refs = refs[:slot], refs[slot:]
    out_ref, kv_ref, qz_ref, m_ref, l_ref, acc_ref = refs[:6]
    score, top_of, out_of, sum_of = (refs[6 + 2 * at : 8 + 2 * at] for at in range(4))
    rows = arrived[0].shape[0]
    m_ref[...] = jnp.full(m_ref.shape, -BIG, F32)
    for ref in (l_ref, acc_ref):
        ref[...] = jnp.zeros(ref.shape, F32)
    zeros = jnp.zeros((DH, BLK), BF16)

    def put_query(row, part):
        up = jnp.concatenate([part, zeros], axis=0)
        down = jnp.concatenate([zeros, part], axis=0)
        qz_ref[row] = jnp.concatenate([up, down], axis=1)

    for row in range(0, rows, 2):
        pair = [arrived[0][row, 1], arrived[0][row + 1, 1]]
        for at, part in enumerate(turn_folded(*pair) if slot == 0 else pair):
            put_query(row + at, part)
    qz_ref[rows] = jnp.zeros((2 * DH, 2 * BLK), BF16)
    for at, (array, keys) in enumerate(zip(arrived, before)):
        for row in range(0, rows, 2):
            place = at * rows + row
            kv_ref[place, 0], kv_ref[place + 1, 0] = keys[row, key_at], keys[row + 1, key_at]
            pair = [array[row, 0], array[row + 1, 0]]
            kv_ref[place, 1], kv_ref[place + 1, 1] = turn_folded(*pair) if slot == 0 else pair
    for at, result in enumerate(earlier):
        for row in range(rows):
            out_ref[row, at] = result[row]

    def make_scores(unit, lane, side):
        row, first, second = unit_ref[slot, 0, unit], unit_ref[slot, 1, unit], unit_ref[slot, 2, unit]
        keys = jnp.concatenate([kv_ref[first, 0], kv_ref[second, 0]], axis=0)
        scores = jnp.dot(keys, qz_ref[row], preferred_element_type=F32)
        score[side][lane] = scores
        top = jnp.max(scores.reshape(BLK // 8, 8, 2 * BLK), axis=0)
        top = jnp.maximum(top[:, :BLK], top[:, BLK:])
        top_of[side][lane] = jnp.broadcast_to(jnp.max(top, axis=0, keepdims=True), (8, BLK))

    def make_output(unit, lane, side):
        first, second = unit_ref[slot, 1, unit], unit_ref[slot, 2, unit]
        top = top_of[side][lane]
        limit = jnp.where(unit_ref[slot, 3, unit] == 1, top, top + BIG)
        scores = score[side][lane]
        tiles = (DH // 8, 8, BLK)
        weights = [
            jnp.exp(scores[at : at + DH, lanes : lanes + BLK].reshape(tiles) - bound[None])
            for at, bound in ((0, top), (DH, limit))
            for lanes in (0, BLK)
        ]
        sum_of[side][lane] = jnp.sum(sum(weights[1:], weights[0]), axis=0)
        weights = jnp.concatenate([part.reshape(DH, BLK) for part in weights], axis=0)
        values = jnp.concatenate([kv_ref[first, 1], kv_ref[second, 1]], axis=1)
        out_of[side][lane] = jnp.dot(values, weights.astype(BF16), preferred_element_type=F32)

    def merge(unit, lane, side):
        row = unit_ref[slot, 0, unit]
        top, old = top_of[side][lane], m_ref[row]
        new = jnp.maximum(old, top)
        a, b = jnp.exp(old - new), jnp.exp(top - new)
        m_ref[row] = new
        l_ref[row] = l_ref[row] * a + sum_of[side][lane] * b
        tiles = (DH // 8, 8, BLK)
        acc_ref[row] = (acc_ref[row].reshape(tiles) * a[None] + out_of[side][lane].reshape(tiles) * b[None]).reshape(
            DH, BLK
        )

    def step(index, _):
        for side in range(2):
            chunk = 2 * index + side
            for lane in range(UNROLL):
                merge(chunk * UNROLL + lane, lane, side)
                make_scores((chunk + 2) * UNROLL + lane, lane, side)
                make_output((chunk + 1) * UNROLL + lane, lane, 1 - side)
        return 0

    chunks = (total_ref[slot] + UNROLL - 1) // UNROLL
    lax.fori_loop(0, (chunks + 1) // 2, step, 0)
    for row in range(rows):
        total_w = jnp.sum(l_ref[row], axis=0, keepdims=True)
        result = (acc_ref[row] / total_w).astype(BF16)
        if len(out_ref.shape) == 4:
            out_ref[row, slot] = result
        else:
            out_ref[row] = result


def unpack_kernel(table_ref, o_ref, out_ref):
    groups = o_ref.shape[0]

    def fetch(head):
        place = table_ref[1, head]
        return o_ref[place % groups, place // groups]

    for pair in range(H // 2):
        both = jnp.concatenate([fetch(2 * pair), fetch(2 * pair + 1)], axis=0)
        out_ref[:, pair * 2 * DH : (pair + 1) * 2 * DH] = both.T


def shards(queries, key_vectors, value_vectors, layout, counts):
    uly, doc = lax.axis_size("uly"), lax.axis_size("doc")
    parts = max(min(doc // 2, H // (2 * uly)), 1)
    gather = doc // parts
    groups = uly * parts
    slots = H // groups
    shape = jax.ShapeDtypeStruct
    queries, key_vectors, value_vectors = (
        pltpu.with_memory_space_constraint(array, pltpu.HBM) for array in (queries, key_vectors, value_vectors)
    )
    slot_tiles = [2 + (slot == 0) + (slot + 1 < slots) for slot in range(slots)]
    held = [pltpu.VMEM(queries.shape, BF16)] * 3 + [pltpu.SemaphoreType.DMA((3, 4))]
    table, first = pl.pallas_call(
        functools.partial(pack_first_kernel, groups),
        out_shape=(shape((8, 128), jnp.int32), pltpu.HBM((groups, slot_tiles[0], DH, BLK), BF16)),
        in_specs=[HBM] * 4,
        out_specs=(SMEM, HBM),
        scratch_shapes=[
            *held,
            pltpu.VMEM(counts.shape, jnp.int32),
            pltpu.VMEM((8, 128), jnp.int32),
            pltpu.SemaphoreType.DMA,
            pltpu.VMEM((slot_tiles[0], groups, DH, BLK), BF16),
            pltpu.SemaphoreType.DMA((slot_tiles[0],)),
        ],
        compiler_params=PARAMS,
        name="pack",
    )(pltpu.with_memory_space_constraint(counts, pltpu.HBM), queries, key_vectors, value_vectors)
    packed = [first]
    for slot in range(1, slots):
        packed.append(
            pl.pallas_call(
                functools.partial(pack_rest_kernel, slot),
                out_shape=pltpu.VMEM((groups, slot_tiles[slot], DH, BLK), BF16),
                in_specs=[SMEM] + [HBM] * 3,
                out_specs=VMEM,
                scratch_shapes=[*held] + [pltpu.VMEM((H, DH, BLK), BF16)] * 2,
                compiler_params=PARAMS,
                name="pack",
            )(table, queries, key_vectors, value_vectors)
        )
    units, totals = pl.pallas_call(
        functools.partial(plan_kernel, uly, gather),
        out_shape=(shape((slots, 4, groups * KMAX // 2 + 8 * UNROLL), jnp.int32), shape((slots,), jnp.int32)),
        in_specs=[SMEM, SMEM, VMEM],
        out_specs=(SMEM, SMEM),
        scratch_shapes=[pltpu.SMEM((slots, groups, KMAX), jnp.int32), pltpu.SemaphoreType.DMA((slots, parts))],
        compiler_params=PARAMS,
        name="plan",
    )(table, counts, layout)

    members = [
        [(part * gather + rest) * uly + mirror(at, uly) for part in range(parts) for at in range(uly)]
        for rest in range(gather)
    ]
    swap = functools.partial(
        lax.all_to_all,
        axis_name=("doc", "uly"),
        split_axis=0,
        concat_axis=0,
        axis_index_groups=members,
        tiled=True,
    )

    def hold(array):
        return pltpu.with_memory_space_constraint(array, pltpu.VMEM)

    def flip(array, bit):
        return lax.ppermute(array, "doc", [(at, at ^ bit) for at in range(doc)])

    arrived = swap(packed[0])
    arrived, units, totals, *packed = lax.optimization_barrier((arrived, units, totals, *packed))
    results, arrays = [], {}
    for slot in range(slots):
        before = arrays if slot else {}
        if slot:
            arrived, *results = lax.optimization_barrier((swap(packed[slot]), *results))
        arrays, bit = {0: arrived}, gather // 2
        while bit:
            arrays.update({at ^ bit: flip(array, bit) for at, array in list(arrays.items())})
            bit //= 2
        last = slot == slots - 1
        both = [pltpu.VMEM((UNROLL, BLK, 2 * BLK), F32)] * 2 + [pltpu.VMEM((UNROLL, 8, BLK), F32)] * 2
        both += [pltpu.VMEM((UNROLL, DH, BLK), F32)] * 2 + [pltpu.VMEM((UNROLL, 8, BLK), F32)] * 2
        earlier = results if last else []
        results.append(
            pl.pallas_call(
                functools.partial(attend_kernel, slot, gather),
                out_shape=pltpu.VMEM((groups, slots, DH, BLK) if last else (groups, DH, BLK), BF16),
                in_specs=[SMEM, SMEM] + [VMEM] * (gather + len(before) + len(earlier)),
                out_specs=VMEM,
                scratch_shapes=[
                    pltpu.VMEM((gather * groups, 2, DH, BLK), BF16),
                    pltpu.VMEM((groups + 1, 2 * DH, 2 * BLK), BF16),
                    pltpu.VMEM((groups + 1, 8, BLK), F32),
                    pltpu.VMEM((groups + 1, 8, BLK), F32),
                    pltpu.VMEM((groups + 1, DH, BLK), F32),
                    *both,
                ],
                compiler_params=PARAMS,
                cost_estimate=pl.CostEstimate(flops=10**10, transcendentals=6 * 10**6, bytes_accessed=6 * 10**6),
                name="attend",
            )(units, totals, *[hold(part[at]) for part in (arrays, before) for at in range(len(part))], *[hold(result) for result in earlier])
        )
    return pl.pallas_call(
        unpack_kernel,
        out_shape=shape(queries.shape, BF16),
        in_specs=[SMEM, VMEM],
        out_specs=VMEM,
        compiler_params=PARAMS,
        name="unpack",
    )(table, hold(swap(results[-1])))


def solution(mesh):
    placed = (
        P(("grp", "doc", "uly"), None),
        P(("grp", "doc", "uly"), None),
        P(("grp", "doc", "uly"), None),
        P("grp", None, None),
        P("grp", None),
    )
    return jax.shard_map(
        shards,
        mesh=mesh,
        in_specs=placed,
        out_specs=P(("grp", "doc", "uly"), None),
        check_vma=False,
    )
```

```python
import functools

import jax
import jax.numpy as jnp
from jax import lax
from jax.experimental import pallas as pl
from jax.experimental.pallas import tpu as pltpu
from jax.sharding import PartitionSpec as P

H = 32
DH = 64
BLK = 128
KMAX = 32
UNROLL = 6
BIG = 1e30
F32 = jnp.float32
BF16 = jnp.bfloat16
VMEM = pl.BlockSpec(memory_space=pltpu.VMEM)
SMEM = pl.BlockSpec(memory_space=pltpu.SMEM)
HBM = pl.BlockSpec(memory_space=pltpu.HBM)
PARAMS = pltpu.CompilerParams(vmem_limit_bytes=28 << 20)


def rank_heads(counts_ref, table_ref, groups):
    counts = counts_ref[...].astype(BF16)
    blocks = counts.shape[1]
    over = (((1,), (1,)), ((), ()))
    mine = lax.dot_general(counts, jnp.ones((H, blocks), BF16), over, preferred_element_type=F32)
    theirs = lax.dot_general(jnp.ones((H, blocks), BF16), counts, over, preferred_element_type=F32)
    row = lax.broadcasted_iota(jnp.int32, (H, H), 0)
    lane = lax.broadcasted_iota(jnp.int32, (H, H), 1)
    bits = groups.bit_length() - 1

    def place_of(rank):
        slot, seat = rank >> bits, rank & (groups - 1)
        return slot * groups + jnp.where((slot & 1) == 0, seat, groups - 1 - seat)

    behind = (theirs > mine) | ((theirs == mine) & (lane < row))
    rank_down = jnp.sum(jnp.where(behind, 1.0, 0.0), axis=1, keepdims=True).astype(jnp.int32)
    ahead = (mine > theirs) | ((theirs == mine) & (row < lane))
    rank_along = jnp.sum(jnp.where(ahead, 1.0, 0.0), axis=0, keepdims=True).astype(jnp.int32)
    here = place_of(jnp.broadcast_to(rank_down, (H, H))) == lane
    head_at = jnp.sum(jnp.where(here, row.astype(F32), 0.0), axis=0, keepdims=True).astype(jnp.int32)
    table_ref[0:1, 0:H] = head_at
    table_ref[1:2, 0:H] = place_of(rank_along)


def turn_heads(source, turned):
    for pair in range(H // 2):
        tile = source[:, pair * 2 * DH : (pair + 1) * 2 * DH].T
        turned[2 * pair] = tile[:DH]
        turned[2 * pair + 1] = tile[DH:]


def fold_head(source, head):
    odd = head % 2
    low = lax.broadcasted_iota(jnp.int32, (DH, 2 * DH), 1) < DH
    lanes = pl.ds(pl.multiple_of((head // 2) * (2 * DH), 2 * DH), 2 * DH)
    plain = source[pl.ds(pl.multiple_of(odd * DH, DH), DH), lanes]
    other = source[pl.ds(pl.multiple_of((1 - odd) * DH, DH), DH), lanes]
    return jnp.where(low == (odd == 0), plain, swap_halves(other))


def swap_halves(tile):
    return jnp.concatenate([tile[:, DH:], tile[:, :DH]], axis=1)


def turn_folded(first, second):
    low = lax.broadcasted_iota(jnp.int32, (DH, 2 * DH), 1) < DH
    turned = jnp.concatenate([first, second], axis=0).T
    early, late = turned[:DH], turned[DH:]
    return jnp.where(low, early, swap_halves(late)), jnp.where(low, swap_halves(early), late)


def load(arrays, buffers, sems):
    rows = arrays[0].shape[0] // 4
    copies = [
        [
            pltpu.make_async_copy(array.at[pl.ds(at * rows, rows)], buffer.at[pl.ds(at * rows, rows)], sems.at[which, at])
            for at in range(4)
        ]
        for which, (array, buffer) in enumerate(zip(arrays, buffers))
    ]
    for group in copies:
        for copy in group:
            copy.start()
    return copies


def pack_first_kernel(groups, counts_ref, q_ref, k_ref, v_ref, table_ref, out_ref, table_vmem, sem):
    rank_heads(counts_ref, table_vmem, groups)
    copy = pltpu.make_async_copy(table_vmem, table_ref, sem)
    copy.start()
    copy.wait()
    for group in range(groups):
        head = table_ref[0, group]
        for at, source in enumerate((v_ref, q_ref, k_ref)):
            out_ref[group, at] = fold_head(source, head)


def pack_rest_kernel(slot, table_ref, q_hbm, k_hbm, v_hbm, out_ref, q_ref, k_ref, v_ref, sems, turned_q, turned_v):
    copies = load((k_hbm, v_hbm, q_hbm), (k_ref, v_ref, q_ref), sems)
    for group in copies:
        for copy in group:
            copy.wait()
    turn_heads(q_ref, turned_q)
    turn_heads(v_ref, turned_v)
    groups = out_ref.shape[0]
    for group in range(groups):
        head = table_ref[0, slot * groups + group]
        out_ref[group, 0] = turned_v[head]
        out_ref[group, 1] = turned_q[head]
        out_ref[group, 2] = fold_head(k_ref, head)


def mirror(value, size):
    bits = size.bit_length() - 1
    return sum(((value >> at) & 1) << (bits - 1 - at) for at in range(bits)) if bits else value


def plan_kernel(uly, gather, table_ref, counts_ref, layout_ref, unit_ref, total_ref, lay_ref, sem):
    slots = total_ref.shape[0]
    groups = H // slots
    parts = groups // uly
    doc = lax.axis_index("doc")
    part, rest = doc // gather, doc % gather
    group = part * uly + mirror(lax.axis_index("uly"), uly)

    def rows_at(at):
        return (at * gather + rest) * uly

    copies = [
        pltpu.make_async_copy(
            layout_ref.at[table_ref[0, slot * groups + group], pl.ds(rows_at(at), uly)],
            lay_ref.at[slot, pl.ds(at * uly, uly)],
            sem.at[slot, at],
        )
        for slot in range(slots)
        for at in range(parts)
    ]
    for copy in copies:
        copy.start()

    def local(block):
        its = block // uly
        return ((its % gather) ^ rest) * groups + (its // gather) * uly + mirror(block % uly, uly)

    for copy in copies:
        copy.wait()
    for slot in range(slots):
        head = table_ref[0, slot * groups + group]

        def idle(base, many, slot=slot):
            for extra in range(many):
                unit_ref[slot, 0, base + extra] = groups
                unit_ref[slot, 1, base + extra] = 0
                unit_ref[slot, 2, base + extra] = 0
                unit_ref[slot, 3, base + extra] = 1

        def place_row(row, base, slot=slot, head=head):
            token = (row // uly) * uly + mirror(row % uly, uly)
            count = counts_ref[head, rows_at(row // uly) + mirror(row % uly, uly)]

            def place_unit(step, _):
                first = lay_ref[slot, token, 2 * step]
                whole = 2 * step + 1 < count
                second = jnp.where(whole, lay_ref[slot, token, jnp.minimum(2 * step + 1, KMAX - 1)], first)
                unit_ref[slot, 0, base + step] = row
                unit_ref[slot, 1, base + step] = local(first)
                unit_ref[slot, 2, base + step] = local(second)
                unit_ref[slot, 3, base + step] = whole.astype(jnp.int32)
                return 0

            units = (count + 1) // 2
            lax.fori_loop(0, units, place_unit, 0)
            return base + units

        idle(0, 2 * UNROLL)
        total = lax.fori_loop(0, groups, place_row, jnp.int32(2 * UNROLL))
        idle(total, 4 * UNROLL)
        total_ref[slot] = total


def attend_kernel(slot, gather, unit_ref, total_ref, *refs):
    arrived, refs = refs[:gather], refs[gather:]
    earlier, refs = refs[:slot], refs[slot:]
    out_ref, kv_ref, qz_ref, m_ref, l_ref, acc_ref = refs[:6]
    score, top_of, out_of, sum_of = (refs[6 + 2 * at : 8 + 2 * at] for at in range(4))
    rows = arrived[0].shape[0]
    m_ref[...] = jnp.full(m_ref.shape, -BIG, F32)
    for ref in (l_ref, acc_ref):
        ref[...] = jnp.zeros(ref.shape, F32)
    zeros = jnp.zeros((DH, BLK), BF16)

    def put_query(row, part):
        up = jnp.concatenate([part, zeros], axis=0)
        down = jnp.concatenate([zeros, part], axis=0)
        qz_ref[row] = jnp.concatenate([up, down], axis=1)

    for row in range(0, rows, 2):
        pair = [arrived[0][row, 1], arrived[0][row + 1, 1]]
        for at, part in enumerate(turn_folded(*pair) if slot == 0 else pair):
            put_query(row + at, part)
    qz_ref[rows] = jnp.zeros((2 * DH, 2 * BLK), BF16)
    for at, array in enumerate(arrived):
        for row in range(0, rows, 2):
            place = at * rows + row
            kv_ref[place, 0], kv_ref[place + 1, 0] = array[row, 2], array[row + 1, 2]
            pair = [array[row, 0], array[row + 1, 0]]
            kv_ref[place, 1], kv_ref[place + 1, 1] = turn_folded(*pair) if slot == 0 else pair
    for at, result in enumerate(earlier):
        for row in range(rows):
            out_ref[row, at] = result[row]

    def make_scores(unit, lane, side):
        row, first, second = unit_ref[slot, 0, unit], unit_ref[slot, 1, unit], unit_ref[slot, 2, unit]
        keys = jnp.concatenate([kv_ref[first, 0], kv_ref[second, 0]], axis=0)
        scores = jnp.dot(keys, qz_ref[row], preferred_element_type=F32)
        score[side][lane] = scores
        top = jnp.max(scores.reshape(BLK // 8, 8, 2 * BLK), axis=0)
        top = jnp.maximum(top[:, :BLK], top[:, BLK:])
        top_of[side][lane] = jnp.broadcast_to(jnp.max(top, axis=0, keepdims=True), (8, BLK))

    def make_output(unit, lane, side):
        first, second = unit_ref[slot, 1, unit], unit_ref[slot, 2, unit]
        top = top_of[side][lane]
        limit = jnp.where(unit_ref[slot, 3, unit] == 1, top, top + BIG)
        scores = score[side][lane]
        tiles = (DH // 8, 8, BLK)
        weights = [
            jnp.exp(scores[at : at + DH, lanes : lanes + BLK].reshape(tiles) - bound[None])
            for at, bound in ((0, top), (DH, limit))
            for lanes in (0, BLK)
        ]
        sum_of[side][lane] = jnp.sum(sum(weights[1:], weights[0]), axis=0)
        weights = jnp.concatenate([part.reshape(DH, BLK) for part in weights], axis=0)
        values = jnp.concatenate([kv_ref[first, 1], kv_ref[second, 1]], axis=1)
        out_of[side][lane] = jnp.dot(values, weights.astype(BF16), preferred_element_type=F32)

    def merge(unit, lane, side):
        row = unit_ref[slot, 0, unit]
        top, old = top_of[side][lane], m_ref[row]
        new = jnp.maximum(old, top)
        a, b = jnp.exp(old - new), jnp.exp(top - new)
        m_ref[row] = new
        l_ref[row] = l_ref[row] * a + sum_of[side][lane] * b
        tiles = (DH // 8, 8, BLK)
        acc_ref[row] = (acc_ref[row].reshape(tiles) * a[None] + out_of[side][lane].reshape(tiles) * b[None]).reshape(
            DH, BLK
        )

    def step(index, _):
        for side in range(2):
            chunk = 2 * index + side
            for lane in range(UNROLL):
                merge(chunk * UNROLL + lane, lane, side)
                make_scores((chunk + 2) * UNROLL + lane, lane, side)
                make_output((chunk + 1) * UNROLL + lane, lane, 1 - side)
        return 0

    chunks = (total_ref[slot] + UNROLL - 1) // UNROLL
    lax.fori_loop(0, (chunks + 1) // 2, step, 0)
    for row in range(rows):
        total_w = jnp.sum(l_ref[row], axis=0, keepdims=True)
        result = (acc_ref[row] * (1.0 / total_w)).astype(BF16)
        if len(out_ref.shape) == 4:
            out_ref[row, slot] = result
        else:
            out_ref[row] = result


def unpack_kernel(table_ref, o_ref, out_ref):
    groups = o_ref.shape[0]

    def fetch(head):
        place = table_ref[1, head]
        return o_ref[place % groups, place // groups]

    for pair in range(H // 2):
        both = jnp.concatenate([fetch(2 * pair), fetch(2 * pair + 1)], axis=0)
        out_ref[:, pair * 2 * DH : (pair + 1) * 2 * DH] = both.T


def shards(queries, key_vectors, value_vectors, layout, counts):
    uly, doc = lax.axis_size("uly"), lax.axis_size("doc")
    parts = max(min(doc // 2, H // (2 * uly)), 1)
    gather = doc // parts
    groups = uly * parts
    slots = H // groups
    shape = jax.ShapeDtypeStruct
    queries, key_vectors, value_vectors = (
        pltpu.with_memory_space_constraint(array, pltpu.HBM) for array in (queries, key_vectors, value_vectors)
    )
    packed_shape = pltpu.HBM((groups, 3, DH, BLK), BF16)
    held = [pltpu.VMEM(queries.shape, BF16)] * 3 + [pltpu.SemaphoreType.DMA((3, 4))]
    table, first = pl.pallas_call(
        functools.partial(pack_first_kernel, groups),
        out_shape=(shape((8, 128), jnp.int32), packed_shape),
        in_specs=[VMEM] * 4,
        out_specs=(SMEM, VMEM),
        scratch_shapes=[pltpu.VMEM((8, 128), jnp.int32), pltpu.SemaphoreType.DMA],
        compiler_params=PARAMS,
        name="pack",
    )(pltpu.with_memory_space_constraint(counts, pltpu.HBM), queries, key_vectors, value_vectors)
    packed = [first]
    for slot in range(1, slots):
        packed.append(
            pl.pallas_call(
                functools.partial(pack_rest_kernel, slot),
                out_shape=packed_shape,
                in_specs=[SMEM] + [HBM] * 3,
                out_specs=VMEM,
                scratch_shapes=[*held] + [pltpu.VMEM((H, DH, BLK), BF16)] * 2,
                compiler_params=PARAMS,
                name="pack",
            )(table, queries, key_vectors, value_vectors)
        )
    units, totals = pl.pallas_call(
        functools.partial(plan_kernel, uly, gather),
        out_shape=(shape((slots, 4, groups * KMAX // 2 + 8 * UNROLL), jnp.int32), shape((slots,), jnp.int32)),
        in_specs=[SMEM, SMEM, VMEM],
        out_specs=(SMEM, SMEM),
        scratch_shapes=[pltpu.SMEM((slots, groups, KMAX), jnp.int32), pltpu.SemaphoreType.DMA((slots, parts))],
        compiler_params=PARAMS,
        name="plan",
    )(table, counts, layout)

    members = [
        [(part * gather + rest) * uly + mirror(at, uly) for part in range(parts) for at in range(uly)]
        for rest in range(gather)
    ]
    swap = functools.partial(
        lax.all_to_all,
        axis_name=("doc", "uly"),
        split_axis=0,
        concat_axis=0,
        axis_index_groups=members,
        tiled=True,
    )

    def hold(array):
        return pltpu.with_memory_space_constraint(array, pltpu.VMEM)

    def flip(array, bit):
        return lax.ppermute(array, "doc", [(at, at ^ bit) for at in range(doc)])

    arrived = swap(packed[0])
    arrived, units, totals, *packed = lax.optimization_barrier((arrived, units, totals, *packed))
    results = []
    for slot in range(slots):
        if slot:
            arrived, *results = lax.optimization_barrier((swap(packed[slot]), *results))
        arrays, bit = {0: arrived}, gather // 2
        while bit:
            arrays.update({at ^ bit: flip(array, bit) for at, array in list(arrays.items())})
            bit //= 2
        last = slot == slots - 1
        both = [pltpu.VMEM((UNROLL, BLK, 2 * BLK), F32)] * 2 + [pltpu.VMEM((UNROLL, 8, BLK), F32)] * 2
        both += [pltpu.VMEM((UNROLL, DH, BLK), F32)] * 2 + [pltpu.VMEM((UNROLL, 8, BLK), F32)] * 2
        earlier = results if last else []
        results.append(
            pl.pallas_call(
                functools.partial(attend_kernel, slot, gather),
                out_shape=pltpu.VMEM((groups, slots, DH, BLK) if last else (groups, DH, BLK), BF16),
                in_specs=[SMEM, SMEM] + [VMEM] * (gather + len(earlier)),
                out_specs=VMEM,
                scratch_shapes=[
                    pltpu.VMEM((gather * groups, 2, DH, BLK), BF16),
                    pltpu.VMEM((groups + 1, 2 * DH, 2 * BLK), BF16),
                    pltpu.VMEM((groups + 1, 8, BLK), F32),
                    pltpu.VMEM((groups + 1, 8, BLK), F32),
                    pltpu.VMEM((groups + 1, DH, BLK), F32),
                    *both,
                ],
                compiler_params=PARAMS,
                cost_estimate=pl.CostEstimate(flops=10**10, transcendentals=6 * 10**6, bytes_accessed=6 * 10**6),
                name="attend",
            )(units, totals, *[hold(arrays[at]) for at in range(gather)], *[hold(result) for result in earlier])
        )
    return pl.pallas_call(
        unpack_kernel,
        out_shape=shape(queries.shape, BF16),
        in_specs=[SMEM, VMEM],
        out_specs=VMEM,
        compiler_params=PARAMS,
        name="unpack",
    )(table, hold(swap(results[-1])))


def solution(mesh):
    placed = (
        P(("grp", "doc", "uly"), None),
        P(("grp", "doc", "uly"), None),
        P(("grp", "doc", "uly"), None),
        P("grp", None, None),
        P("grp", None),
    )
    return jax.shard_map(
        shards,
        mesh=mesh,
        in_specs=placed,
        out_specs=P(("grp", "doc", "uly"), None),
        check_vma=False,
    )
```

```python
import functools

import jax
import jax.numpy as jnp
from jax import lax
from jax.experimental import pallas as pl
from jax.experimental.pallas import tpu as pltpu
from jax.sharding import PartitionSpec as P

H = 32
DH = 64
BLK = 128
KMAX = 32
UNROLL = 6
BIG = 1e30
F32 = jnp.float32
BF16 = jnp.bfloat16
VMEM = pl.BlockSpec(memory_space=pltpu.VMEM)
SMEM = pl.BlockSpec(memory_space=pltpu.SMEM)
HBM = pl.BlockSpec(memory_space=pltpu.HBM)
PARAMS = pltpu.CompilerParams(vmem_limit_bytes=28 << 20)


def rank_heads(counts_ref, table_ref, groups):
    counts = counts_ref[...].astype(BF16)
    blocks = counts.shape[1]
    over = (((1,), (1,)), ((), ()))
    mine = lax.dot_general(counts, jnp.ones((H, blocks), BF16), over, preferred_element_type=F32)
    theirs = lax.dot_general(jnp.ones((H, blocks), BF16), counts, over, preferred_element_type=F32)
    row = lax.broadcasted_iota(jnp.int32, (H, H), 0)
    lane = lax.broadcasted_iota(jnp.int32, (H, H), 1)
    bits = groups.bit_length() - 1

    def place_of(rank):
        slot, seat = rank >> bits, rank & (groups - 1)
        return slot * groups + jnp.where((slot & 1) == 0, seat, groups - 1 - seat)

    behind = (theirs > mine) | ((theirs == mine) & (lane < row))
    rank_down = jnp.sum(jnp.where(behind, 1.0, 0.0), axis=1, keepdims=True).astype(jnp.int32)
    ahead = (mine > theirs) | ((theirs == mine) & (row < lane))
    rank_along = jnp.sum(jnp.where(ahead, 1.0, 0.0), axis=0, keepdims=True).astype(jnp.int32)
    here = place_of(jnp.broadcast_to(rank_down, (H, H))) == lane
    head_at = jnp.sum(jnp.where(here, row.astype(F32), 0.0), axis=0, keepdims=True).astype(jnp.int32)
    table_ref[0:1, 0:H] = head_at
    table_ref[1:2, 0:H] = place_of(rank_along)


def turn_heads(source, turned):
    for pair in range(H // 2):
        tile = source[:, pair * 2 * DH : (pair + 1) * 2 * DH].T
        turned[2 * pair] = tile[:DH]
        turned[2 * pair + 1] = tile[DH:]


def fold_head(source, head):
    odd = head % 2
    low = lax.broadcasted_iota(jnp.int32, (DH, 2 * DH), 1) < DH
    lanes = pl.ds(pl.multiple_of((head // 2) * (2 * DH), 2 * DH), 2 * DH)
    plain = source[pl.ds(pl.multiple_of(odd * DH, DH), DH), lanes]
    other = source[pl.ds(pl.multiple_of((1 - odd) * DH, DH), DH), lanes]
    return jnp.where(low == (odd == 0), plain, swap_halves(other))


def swap_halves(tile):
    return jnp.concatenate([tile[:, DH:], tile[:, :DH]], axis=1)


def turn_folded(first, second):
    low = lax.broadcasted_iota(jnp.int32, (DH, 2 * DH), 1) < DH
    turned = jnp.concatenate([first, second], axis=0).T
    early, late = turned[:DH], turned[DH:]
    return jnp.where(low, early, swap_halves(late)), jnp.where(low, swap_halves(early), late)


def load(arrays, buffers, sems):
    rows = arrays[0].shape[0] // 4
    copies = [
        [
            pltpu.make_async_copy(array.at[pl.ds(at * rows, rows)], buffer.at[pl.ds(at * rows, rows)], sems.at[which, at])
            for at in range(4)
        ]
        for which, (array, buffer) in enumerate(zip(arrays, buffers))
    ]
    for group in copies:
        for copy in group:
            copy.start()
    return copies


def pack_first_kernel(groups, counts_ref, q_ref, k_ref, v_ref, table_ref, out_ref, table_vmem, sem):
    rank_heads(counts_ref, table_vmem, groups)
    copy = pltpu.make_async_copy(table_vmem, table_ref, sem)
    copy.start()
    copy.wait()
    for group in range(groups):
        head = table_ref[0, group]
        for at, source in enumerate((v_ref, q_ref, k_ref)):
            out_ref[group, at] = fold_head(source, head)


def pack_rest_kernel(slot, table_ref, q_hbm, k_hbm, v_hbm, out_ref, q_ref, k_ref, v_ref, sems, turned_q, turned_v):
    copies = load((k_hbm, v_hbm, q_hbm), (k_ref, v_ref, q_ref), sems)
    for group in copies:
        for copy in group:
            copy.wait()
    turn_heads(q_ref, turned_q)
    turn_heads(v_ref, turned_v)
    groups = out_ref.shape[0]
    for group in range(groups):
        head = table_ref[0, slot * groups + group]
        out_ref[group, 0] = turned_v[head]
        out_ref[group, 1] = turned_q[head]
        out_ref[group, 2] = fold_head(k_ref, head)


def mirror(value, size):
    bits = size.bit_length() - 1
    return sum(((value >> at) & 1) << (bits - 1 - at) for at in range(bits)) if bits else value


def plan_kernel(uly, gather, table_ref, counts_ref, layout_ref, unit_ref, total_ref, lay_ref, sem):
    slots = total_ref.shape[0]
    groups = H // slots
    parts = groups // uly
    doc = lax.axis_index("doc")
    part, rest = doc // gather, doc % gather
    group = part * uly + mirror(lax.axis_index("uly"), uly)

    def rows_at(at):
        return (at * gather + rest) * uly

    copies = [
        pltpu.make_async_copy(
            layout_ref.at[table_ref[0, slot * groups + group], pl.ds(rows_at(at), uly)],
            lay_ref.at[slot, pl.ds(at * uly, uly)],
            sem.at[slot, at],
        )
        for slot in range(slots)
        for at in range(parts)
    ]
    for copy in copies:
        copy.start()

    def local(block):
        its = block // uly
        return ((its % gather) ^ rest) * groups + (its // gather) * uly + mirror(block % uly, uly)

    for copy in copies:
        copy.wait()
    for slot in range(slots):
        head = table_ref[0, slot * groups + group]

        def idle(base, many, slot=slot):
            for extra in range(many):
                unit_ref[slot, 0, base + extra] = groups
                unit_ref[slot, 1, base + extra] = 0
                unit_ref[slot, 2, base + extra] = 0
                unit_ref[slot, 3, base + extra] = 1

        def place_row(row, base, slot=slot, head=head):
            token = (row // uly) * uly + mirror(row % uly, uly)
            count = counts_ref[head, rows_at(row // uly) + mirror(row % uly, uly)]

            def place_unit(step, _):
                first = lay_ref[slot, token, 2 * step]
                whole = 2 * step + 1 < count
                second = jnp.where(whole, lay_ref[slot, token, jnp.minimum(2 * step + 1, KMAX - 1)], first)
                unit_ref[slot, 0, base + step] = row
                unit_ref[slot, 1, base + step] = local(first)
                unit_ref[slot, 2, base + step] = local(second)
                unit_ref[slot, 3, base + step] = whole.astype(jnp.int32)
                return 0

            units = (count + 1) // 2
            lax.fori_loop(0, units, place_unit, 0)
            return base + units

        idle(0, 2 * UNROLL)
        total = lax.fori_loop(0, groups, place_row, jnp.int32(2 * UNROLL))
        idle(total, 4 * UNROLL)
        total_ref[slot] = total


def attend_kernel(slot, gather, unit_ref, total_ref, *refs):
    arrived, refs = refs[:gather], refs[gather:]
    earlier, refs = refs[:slot], refs[slot:]
    out_ref, kv_ref, qz_ref, m_ref, l_ref, acc_ref = refs[:6]
    score, top_of, out_of, sum_of = (refs[6 + 2 * at : 8 + 2 * at] for at in range(4))
    rows = arrived[0].shape[0]
    m_ref[...] = jnp.full(m_ref.shape, -BIG, F32)
    for ref in (l_ref, acc_ref):
        ref[...] = jnp.zeros(ref.shape, F32)
    zeros = jnp.zeros((DH, BLK), BF16)

    def put_query(row, part):
        up = jnp.concatenate([part, zeros], axis=0)
        down = jnp.concatenate([zeros, part], axis=0)
        qz_ref[row] = jnp.concatenate([up, down], axis=1)

    for row in range(0, rows, 2):
        pair = [arrived[0][row, 1], arrived[0][row + 1, 1]]
        for at, part in enumerate(turn_folded(*pair) if slot == 0 else pair):
            put_query(row + at, part)
    qz_ref[rows] = jnp.zeros((2 * DH, 2 * BLK), BF16)
    for at, array in enumerate(arrived):
        for row in range(0, rows, 2):
            place = at * rows + row
            kv_ref[place, 0], kv_ref[place + 1, 0] = array[row, 2], array[row + 1, 2]
            pair = [array[row, 0], array[row + 1, 0]]
            kv_ref[place, 1], kv_ref[place + 1, 1] = turn_folded(*pair) if slot == 0 else pair
    for at, result in enumerate(earlier):
        for row in range(rows):
            out_ref[row, at] = result[row]

    def make_scores(unit, lane, side):
        row, first, second = unit_ref[slot, 0, unit], unit_ref[slot, 1, unit], unit_ref[slot, 2, unit]
        keys = jnp.concatenate([kv_ref[first, 0], kv_ref[second, 0]], axis=0)
        scores = jnp.dot(keys, qz_ref[row], preferred_element_type=F32)
        score[side][lane] = scores
        top = jnp.max(scores.reshape(BLK // 8, 8, 2 * BLK), axis=0)
        top = jnp.maximum(top[:, :BLK], top[:, BLK:])
        top_of[side][lane] = jnp.broadcast_to(jnp.max(top, axis=0, keepdims=True), (8, BLK))

    def make_output(unit, lane, side):
        first, second = unit_ref[slot, 1, unit], unit_ref[slot, 2, unit]
        top = top_of[side][lane]
        limit = jnp.where(unit_ref[slot, 3, unit] == 1, top, top + BIG)
        scores = score[side][lane]
        tiles = (DH // 8, 8, BLK)
        weights = [
            jnp.exp(scores[at : at + DH, lanes : lanes + BLK].reshape(tiles) - bound[None])
            for at, bound in ((0, top), (DH, limit))
            for lanes in (0, BLK)
        ]
        sum_of[side][lane] = jnp.sum(sum(weights[1:], weights[0]), axis=0)
        weights = jnp.concatenate([part.reshape(DH, BLK) for part in weights], axis=0)
        values = jnp.concatenate([kv_ref[first, 1], kv_ref[second, 1]], axis=1)
        out_of[side][lane] = jnp.dot(values, weights.astype(BF16), preferred_element_type=F32)

    def merge(unit, lane, side):
        row = unit_ref[slot, 0, unit]
        top, old = top_of[side][lane], m_ref[row]
        new = jnp.maximum(old, top)
        a, b = jnp.exp(old - new), jnp.exp(top - new)
        m_ref[row] = new
        l_ref[row] = l_ref[row] * a + sum_of[side][lane] * b
        tiles = (DH // 8, 8, BLK)
        acc_ref[row] = (acc_ref[row].reshape(tiles) * a[None] + out_of[side][lane].reshape(tiles) * b[None]).reshape(
            DH, BLK
        )

    def advance(chunk, side):
        for lane in range(UNROLL):
            merge(chunk * UNROLL + lane, lane, side)
            make_scores((chunk + 2) * UNROLL + lane, lane, side)
            make_output((chunk + 1) * UNROLL + lane, lane, 1 - side)

    def step(index, _):
        advance(2 * index, 0)
        advance(2 * index + 1, 1)
        return 0

    chunks = (total_ref[slot] + UNROLL - 1) // UNROLL
    lax.fori_loop(0, chunks // 2, step, 0)

    @pl.when(chunks % 2 == 1)
    def _():
        advance(chunks - 1, 0)

    for row in range(rows):
        total_w = jnp.sum(l_ref[row], axis=0, keepdims=True)
        result = (acc_ref[row] * (1.0 / total_w)).astype(BF16)
        if len(out_ref.shape) == 4:
            out_ref[row, slot] = result
        else:
            out_ref[row] = result


def unpack_kernel(table_ref, o_ref, out_hbm, out_ref, sem):
    groups = o_ref.shape[0]
    pairs = H // 2 // out_ref.shape[0]

    def fetch(head):
        place = table_ref[1, head]
        return o_ref[place % groups, place // groups]

    copies = []
    for part in range(out_ref.shape[0]):
        for at in range(pairs):
            head = 2 * (part * pairs + at)
            both = jnp.concatenate([fetch(head), fetch(head + 1)], axis=0)
            out_ref[part, :, at * 2 * DH : (at + 1) * 2 * DH] = both.T
        lanes = pl.ds(part * pairs * 2 * DH, pairs * 2 * DH)
        copies.append(pltpu.make_async_copy(out_ref.at[part], out_hbm.at[:, lanes], sem.at[part]))
        copies[-1].start()
    for copy in copies:
        copy.wait()


def shards(queries, key_vectors, value_vectors, layout, counts):
    uly, doc = lax.axis_size("uly"), lax.axis_size("doc")
    parts = max(min(doc // 2, H // (2 * uly)), 1)
    gather = doc // parts
    groups = uly * parts
    slots = H // groups
    shape = jax.ShapeDtypeStruct
    queries, key_vectors, value_vectors = (
        pltpu.with_memory_space_constraint(array, pltpu.HBM) for array in (queries, key_vectors, value_vectors)
    )
    packed_shape = pltpu.HBM((groups, 3, DH, BLK), BF16)
    held = [pltpu.VMEM(queries.shape, BF16)] * 3 + [pltpu.SemaphoreType.DMA((3, 4))]
    table, first = pl.pallas_call(
        functools.partial(pack_first_kernel, groups),
        out_shape=(shape((8, 128), jnp.int32), packed_shape),
        in_specs=[VMEM] * 4,
        out_specs=(SMEM, VMEM),
        scratch_shapes=[pltpu.VMEM((8, 128), jnp.int32), pltpu.SemaphoreType.DMA],
        compiler_params=PARAMS,
        name="pack",
    )(pltpu.with_memory_space_constraint(counts, pltpu.HBM), queries, key_vectors, value_vectors)
    packed = [first]
    for slot in range(1, slots):
        packed.append(
            pl.pallas_call(
                functools.partial(pack_rest_kernel, slot),
                out_shape=packed_shape,
                in_specs=[SMEM] + [HBM] * 3,
                out_specs=VMEM,
                scratch_shapes=[*held] + [pltpu.VMEM((H, DH, BLK), BF16)] * 2,
                compiler_params=PARAMS,
                name="pack",
            )(table, queries, key_vectors, value_vectors)
        )
    units, totals = pl.pallas_call(
        functools.partial(plan_kernel, uly, gather),
        out_shape=(shape((slots, 4, groups * KMAX // 2 + 8 * UNROLL), jnp.int32), shape((slots,), jnp.int32)),
        in_specs=[SMEM, SMEM, VMEM],
        out_specs=(SMEM, SMEM),
        scratch_shapes=[pltpu.SMEM((slots, groups, KMAX), jnp.int32), pltpu.SemaphoreType.DMA((slots, parts))],
        compiler_params=PARAMS,
        name="plan",
    )(table, counts, layout)

    members = [
        [(part * gather + rest) * uly + mirror(at, uly) for part in range(parts) for at in range(uly)]
        for rest in range(gather)
    ]
    swap = functools.partial(
        lax.all_to_all,
        axis_name=("doc", "uly"),
        split_axis=0,
        concat_axis=0,
        axis_index_groups=members,
        tiled=True,
    )

    def hold(array):
        return pltpu.with_memory_space_constraint(array, pltpu.VMEM)

    def flip(array, bit):
        return lax.ppermute(array, "doc", [(at, at ^ bit) for at in range(doc)])

    arrived = swap(packed[0])
    arrived, units, totals, *packed = lax.optimization_barrier((arrived, units, totals, *packed))
    results = []
    for slot in range(slots):
        if slot:
            arrived, *results = lax.optimization_barrier((swap(packed[slot]), *results))
        arrays, bit = {0: arrived}, gather // 2
        while bit:
            arrays.update({at ^ bit: flip(array, bit) for at, array in list(arrays.items())})
            bit //= 2
        last = slot == slots - 1
        both = [pltpu.VMEM((UNROLL, BLK, 2 * BLK), F32)] * 2 + [pltpu.VMEM((UNROLL, 8, BLK), F32)] * 2
        both += [pltpu.VMEM((UNROLL, DH, BLK), F32)] * 2 + [pltpu.VMEM((UNROLL, 8, BLK), F32)] * 2
        earlier = results if last else []
        results.append(
            pl.pallas_call(
                functools.partial(attend_kernel, slot, gather),
                out_shape=pltpu.VMEM((groups, slots, DH, BLK) if last else (groups, DH, BLK), BF16),
                in_specs=[SMEM, SMEM] + [VMEM] * (gather + len(earlier)),
                out_specs=VMEM,
                scratch_shapes=[
                    pltpu.VMEM((gather * groups, 2, DH, BLK), BF16),
                    pltpu.VMEM((groups + 1, 2 * DH, 2 * BLK), BF16),
                    pltpu.VMEM((groups + 1, 8, BLK), F32),
                    pltpu.VMEM((groups + 1, 8, BLK), F32),
                    pltpu.VMEM((groups + 1, DH, BLK), F32),
                    *both,
                ],
                compiler_params=PARAMS,
                cost_estimate=pl.CostEstimate(flops=10**10, transcendentals=6 * 10**6, bytes_accessed=6 * 10**6),
                name="attend",
            )(units, totals, *[hold(arrays[at]) for at in range(gather)], *[hold(result) for result in earlier])
        )
    return pl.pallas_call(
        unpack_kernel,
        out_shape=pltpu.HBM(queries.shape, BF16),
        in_specs=[SMEM, VMEM],
        out_specs=HBM,
        scratch_shapes=[pltpu.VMEM((4, BLK, H * DH // 4), BF16), pltpu.SemaphoreType.DMA((4,))],
        compiler_params=PARAMS,
        name="unpack",
    )(table, hold(swap(results[-1])))


def solution(mesh):
    placed = (
        P(("grp", "doc", "uly"), None),
        P(("grp", "doc", "uly"), None),
        P(("grp", "doc", "uly"), None),
        P("grp", None, None),
        P("grp", None),
    )
    return jax.shard_map(
        shards,
        mesh=mesh,
        in_specs=placed,
        out_specs=P(("grp", "doc", "uly"), None),
        check_vma=False,
    )
```

```python
import functools

import jax
import jax.numpy as jnp
from jax import lax
from jax.experimental import pallas as pl
from jax.experimental.pallas import tpu as pltpu
from jax.sharding import PartitionSpec as P

H = 32
DH = 64
BLK = 128
KMAX = 32
UNROLL = 6
BIG = 1e30
F32 = jnp.float32
BF16 = jnp.bfloat16
VMEM = pl.BlockSpec(memory_space=pltpu.VMEM)
SMEM = pl.BlockSpec(memory_space=pltpu.SMEM)
HBM = pl.BlockSpec(memory_space=pltpu.HBM)
PARAMS = pltpu.CompilerParams(vmem_limit_bytes=28 << 20)


def rank_heads(counts_ref, table_ref, groups):
    counts = counts_ref[...].astype(BF16)
    blocks = counts.shape[1]
    over = (((1,), (1,)), ((), ()))
    mine = lax.dot_general(counts, jnp.ones((H, blocks), BF16), over, preferred_element_type=F32)
    theirs = lax.dot_general(jnp.ones((H, blocks), BF16), counts, over, preferred_element_type=F32)
    row = lax.broadcasted_iota(jnp.int32, (H, H), 0)
    lane = lax.broadcasted_iota(jnp.int32, (H, H), 1)
    bits = groups.bit_length() - 1

    def place_of(rank):
        slot, seat = rank >> bits, rank & (groups - 1)
        return slot * groups + jnp.where((slot & 1) == 0, seat, groups - 1 - seat)

    behind = (theirs > mine) | ((theirs == mine) & (lane < row))
    rank_down = jnp.sum(jnp.where(behind, 1.0, 0.0), axis=1, keepdims=True).astype(jnp.int32)
    ahead = (mine > theirs) | ((theirs == mine) & (row < lane))
    rank_along = jnp.sum(jnp.where(ahead, 1.0, 0.0), axis=0, keepdims=True).astype(jnp.int32)
    here = place_of(jnp.broadcast_to(rank_down, (H, H))) == lane
    head_at = jnp.sum(jnp.where(here, row.astype(F32), 0.0), axis=0, keepdims=True).astype(jnp.int32)
    table_ref[0:1, 0:H] = head_at
    table_ref[1:2, 0:H] = place_of(rank_along)


def turn_heads(source, turned):
    for pair in range(H // 2):
        tile = source[:, pair * 2 * DH : (pair + 1) * 2 * DH].T
        turned[2 * pair] = tile[:DH]
        turned[2 * pair + 1] = tile[DH:]


def fold_head(source, head):
    odd = head % 2
    low = lax.broadcasted_iota(jnp.int32, (DH, 2 * DH), 1) < DH
    lanes = pl.ds(pl.multiple_of((head // 2) * (2 * DH), 2 * DH), 2 * DH)
    plain = source[pl.ds(pl.multiple_of(odd * DH, DH), DH), lanes]
    other = source[pl.ds(pl.multiple_of((1 - odd) * DH, DH), DH), lanes]
    return jnp.where(low == (odd == 0), plain, swap_halves(other))


def swap_halves(tile):
    return jnp.concatenate([tile[:, DH:], tile[:, :DH]], axis=1)


def turn_folded(first, second):
    low = lax.broadcasted_iota(jnp.int32, (DH, 2 * DH), 1) < DH
    turned = jnp.concatenate([first, second], axis=0).T
    early, late = turned[:DH], turned[DH:]
    return jnp.where(low, early, swap_halves(late)), jnp.where(low, swap_halves(early), late)


def load(arrays, buffers, sems):
    rows = arrays[0].shape[0] // 4
    copies = [
        [
            pltpu.make_async_copy(array.at[pl.ds(at * rows, rows)], buffer.at[pl.ds(at * rows, rows)], sems.at[which, at])
            for at in range(4)
        ]
        for which, (array, buffer) in enumerate(zip(arrays, buffers))
    ]
    for group in copies:
        for copy in group:
            copy.start()
    return copies


def reversal(groups, gather, rest):
    return (rest & 1) * (groups - 1) if gather > 1 else 0


def own_reversal(groups, gather):
    return reversal(groups, gather, lax.axis_index("doc") % gather)


def pack_first_kernel(groups, gather, counts_ref, q_ref, k_ref, v_ref, table_ref, out_ref, table_vmem, sem):
    rank_heads(counts_ref, table_vmem, groups)
    copy = pltpu.make_async_copy(table_vmem, table_ref, sem)
    copy.start()
    copy.wait()
    turn = own_reversal(groups, gather)
    for group in range(groups):
        head = table_ref[0, group ^ turn]
        for at, source in enumerate((v_ref, q_ref, k_ref)):
            out_ref[group, at] = fold_head(source, head)


def pack_rest_kernel(slot, gather, table_ref, q_hbm, k_hbm, v_hbm, out_ref, q_ref, k_ref, v_ref, sems, turned_q, turned_v):
    copies = load((k_hbm, v_hbm, q_hbm), (k_ref, v_ref, q_ref), sems)
    for group in copies:
        for copy in group:
            copy.wait()
    turn_heads(q_ref, turned_q)
    turn_heads(v_ref, turned_v)
    groups = out_ref.shape[0]
    turn = own_reversal(groups, gather)
    for group in range(groups):
        head = table_ref[0, slot * groups + (group ^ turn)]
        out_ref[group, 0] = turned_v[head]
        out_ref[group, 1] = turned_q[head]
        out_ref[group, 2] = fold_head(k_ref, head)


def mirror(value, size):
    bits = size.bit_length() - 1
    return sum(((value >> at) & 1) << (bits - 1 - at) for at in range(bits)) if bits else value


def plan_kernel(uly, gather, table_ref, counts_ref, layout_ref, unit_ref, total_ref, lay_ref, sem):
    slots = total_ref.shape[0]
    groups = H // slots
    parts = groups // uly
    doc = lax.axis_index("doc")
    part, rest = doc // gather, doc % gather
    group = part * uly + mirror(lax.axis_index("uly"), uly)

    def rows_at(at):
        return (at * gather + rest) * uly

    copies = [
        pltpu.make_async_copy(
            layout_ref.at[table_ref[0, slot * groups + group], pl.ds(rows_at(at), uly)],
            lay_ref.at[slot, pl.ds(at * uly, uly)],
            sem.at[slot, at],
        )
        for slot in range(slots)
        for at in range(parts)
    ]
    for copy in copies:
        copy.start()

    def local(block):
        its = block // uly
        place = (its // gather) * uly + mirror(block % uly, uly)
        return ((its % gather) ^ rest) * groups + (place ^ reversal(groups, gather, its % gather))

    for copy in copies:
        copy.wait()
    for slot in range(slots):
        head = table_ref[0, slot * groups + group]

        def idle(base, many, slot=slot):
            for extra in range(many):
                unit_ref[slot, 0, base + extra] = groups
                unit_ref[slot, 1, base + extra] = 0
                unit_ref[slot, 2, base + extra] = 0
                unit_ref[slot, 3, base + extra] = 1

        def place_row(row, base, slot=slot, head=head):
            place = row ^ reversal(groups, gather, rest)
            token = (place // uly) * uly + mirror(place % uly, uly)
            count = counts_ref[head, rows_at(place // uly) + mirror(place % uly, uly)]

            def place_unit(step, _):
                first = lay_ref[slot, token, 2 * step]
                whole = 2 * step + 1 < count
                second = jnp.where(whole, lay_ref[slot, token, jnp.minimum(2 * step + 1, KMAX - 1)], first)
                unit_ref[slot, 0, base + step] = row
                unit_ref[slot, 1, base + step] = local(first)
                unit_ref[slot, 2, base + step] = local(second)
                unit_ref[slot, 3, base + step] = whole.astype(jnp.int32)
                return 0

            units = (count + 1) // 2
            lax.fori_loop(0, units, place_unit, 0)
            return base + units

        idle(0, UNROLL)
        total = lax.fori_loop(0, groups, place_row, jnp.int32(UNROLL))
        idle(total, 4 * UNROLL)
        total_ref[slot] = total


def attend_kernel(slot, gather, unit_ref, total_ref, *refs):
    arrived, refs = refs[:gather], refs[gather:]
    earlier, refs = refs[:slot], refs[slot:]
    out_ref, kv_ref, qz_ref, m_ref, l_ref, acc_ref = refs[:6]
    score, top_of, out_of, sum_of = (refs[6 + 2 * at : 8 + 2 * at] for at in range(4))
    rows = arrived[0].shape[0]
    m_ref[...] = jnp.full(m_ref.shape, -BIG, F32)
    for ref in (l_ref, acc_ref):
        ref[...] = jnp.zeros(ref.shape, F32)
    zeros = jnp.zeros((DH, BLK), BF16)

    def put_query(row, part):
        up = jnp.concatenate([part, zeros], axis=0)
        down = jnp.concatenate([zeros, part], axis=0)
        qz_ref[row] = jnp.concatenate([up, down], axis=1)

    for row in range(0, rows, 2):
        pair = [arrived[0][row, 1], arrived[0][row + 1, 1]]
        for at, part in enumerate(turn_folded(*pair) if slot == 0 else pair):
            put_query(row + at, part)
    qz_ref[rows] = jnp.zeros((2 * DH, 2 * BLK), BF16)
    for at, array in enumerate(arrived):
        for row in range(0, rows, 2):
            place = at * rows + row
            kv_ref[place, 0], kv_ref[place + 1, 0] = array[row, 2], array[row + 1, 2]
            pair = [array[row, 0], array[row + 1, 0]]
            kv_ref[place, 1], kv_ref[place + 1, 1] = turn_folded(*pair) if slot == 0 else pair
    for at, result in enumerate(earlier):
        for row in range(rows):
            out_ref[row, at] = result[row]

    def make_scores(unit, lane, side):
        row, first, second = unit_ref[slot, 0, unit], unit_ref[slot, 1, unit], unit_ref[slot, 2, unit]
        keys = jnp.concatenate([kv_ref[first, 0], kv_ref[second, 0]], axis=0)
        scores = jnp.dot(keys, qz_ref[row], preferred_element_type=F32)
        score[side][lane] = scores
        top = jnp.max(scores.reshape(BLK // 8, 8, 2 * BLK), axis=0)
        top = jnp.maximum(top[:, :BLK], top[:, BLK:])
        top_of[side][lane] = jnp.broadcast_to(jnp.max(top, axis=0, keepdims=True), (8, BLK))

    def make_output(unit, lane, side):
        first, second = unit_ref[slot, 1, unit], unit_ref[slot, 2, unit]
        top = top_of[side][lane]
        limit = jnp.where(unit_ref[slot, 3, unit] == 1, top, top + BIG)
        scores = score[side][lane]
        tiles = (DH // 8, 8, BLK)
        weights = [
            jnp.exp(scores[at : at + DH, lanes : lanes + BLK].reshape(tiles) - bound[None])
            for at, bound in ((0, top), (DH, limit))
            for lanes in (0, BLK)
        ]
        sum_of[side][lane] = jnp.sum(sum(weights[1:], weights[0]), axis=0)
        weights = jnp.concatenate([part.reshape(DH, BLK) for part in weights], axis=0)
        values = jnp.concatenate([kv_ref[first, 1], kv_ref[second, 1]], axis=1)
        out_of[side][lane] = jnp.dot(values, weights.astype(BF16), preferred_element_type=F32)

    def merge(unit, lane, side):
        row = unit_ref[slot, 0, unit]
        top, old = top_of[side][lane], m_ref[row]
        new = jnp.maximum(old, top)
        a, b = jnp.exp(old - new), jnp.exp(top - new)
        m_ref[row] = new
        l_ref[row] = l_ref[row] * a + sum_of[side][lane] * b
        tiles = (DH // 8, 8, BLK)
        acc_ref[row] = (acc_ref[row].reshape(tiles) * a[None] + out_of[side][lane].reshape(tiles) * b[None]).reshape(
            DH, BLK
        )

    def advance(chunk, side):
        for lane in range(UNROLL):
            merge(chunk * UNROLL + lane, lane, side)
            make_scores((chunk + 2) * UNROLL + lane, lane, side)
            make_output((chunk + 1) * UNROLL + lane, lane, 1 - side)

    def step(index, _):
        advance(2 * index, 0)
        advance(2 * index + 1, 1)
        return 0

    chunks = (total_ref[slot] + UNROLL - 1) // UNROLL - 1
    for lane in range(UNROLL):
        make_scores(UNROLL + lane, lane, 1)
    lax.fori_loop(0, chunks // 2, step, 0)

    @pl.when(chunks % 2 == 1)
    def _():
        advance(chunks - 1, 0)
        for lane in range(UNROLL):
            merge(chunks * UNROLL + lane, lane, 1)

    @pl.when(chunks % 2 == 0)
    def _():
        for lane in range(UNROLL):
            merge(chunks * UNROLL + lane, lane, 0)

    for row in range(rows):
        total_w = jnp.sum(l_ref[row], axis=0, keepdims=True)
        result = (acc_ref[row] * (1.0 / total_w)).astype(BF16)
        if len(out_ref.shape) == 4:
            out_ref[row, slot] = result
        else:
            out_ref[row] = result


def unpack_kernel(gather, table_ref, o_ref, out_hbm, out_ref, sem):
    groups = o_ref.shape[0]
    pairs = H // 2 // out_ref.shape[0]
    turn = own_reversal(groups, gather)

    def fetch(head):
        place = table_ref[1, head]
        return o_ref[(place % groups) ^ turn, place // groups]

    copies = []
    for part in range(out_ref.shape[0]):
        for at in range(pairs):
            head = 2 * (part * pairs + at)
            both = jnp.concatenate([fetch(head), fetch(head + 1)], axis=0)
            out_ref[part, :, at * 2 * DH : (at + 1) * 2 * DH] = both.T
        lanes = pl.ds(part * pairs * 2 * DH, pairs * 2 * DH)
        copies.append(pltpu.make_async_copy(out_ref.at[part], out_hbm.at[:, lanes], sem.at[part]))
        copies[-1].start()
    for copy in copies:
        copy.wait()


def shards(queries, key_vectors, value_vectors, layout, counts):
    uly, doc = lax.axis_size("uly"), lax.axis_size("doc")
    parts = max(min(doc // 2, H // (2 * uly)), 1)
    gather = doc // parts
    groups = uly * parts
    slots = H // groups
    shape = jax.ShapeDtypeStruct
    queries, key_vectors, value_vectors = (
        pltpu.with_memory_space_constraint(array, pltpu.HBM) for array in (queries, key_vectors, value_vectors)
    )
    packed_shape = pltpu.HBM((groups, 3, DH, BLK), BF16)
    held = [pltpu.VMEM(queries.shape, BF16)] * 3 + [pltpu.SemaphoreType.DMA((3, 4))]
    table, first = pl.pallas_call(
        functools.partial(pack_first_kernel, groups, gather),
        out_shape=(shape((8, 128), jnp.int32), packed_shape),
        in_specs=[VMEM] * 4,
        out_specs=(SMEM, VMEM),
        scratch_shapes=[pltpu.VMEM((8, 128), jnp.int32), pltpu.SemaphoreType.DMA],
        compiler_params=PARAMS,
        name="pack",
    )(pltpu.with_memory_space_constraint(counts, pltpu.HBM), queries, key_vectors, value_vectors)
    packed = [first]
    for slot in range(1, slots):
        packed.append(
            pl.pallas_call(
                functools.partial(pack_rest_kernel, slot, gather),
                out_shape=packed_shape,
                in_specs=[SMEM] + [HBM] * 3,
                out_specs=VMEM,
                scratch_shapes=[*held] + [pltpu.VMEM((H, DH, BLK), BF16)] * 2,
                compiler_params=PARAMS,
                name="pack",
            )(table, queries, key_vectors, value_vectors)
        )
    units, totals = pl.pallas_call(
        functools.partial(plan_kernel, uly, gather),
        out_shape=(shape((slots, 4, groups * KMAX // 2 + 8 * UNROLL), jnp.int32), shape((slots,), jnp.int32)),
        in_specs=[SMEM, SMEM, VMEM],
        out_specs=(SMEM, SMEM),
        scratch_shapes=[pltpu.SMEM((slots, groups, KMAX), jnp.int32), pltpu.SemaphoreType.DMA((slots, parts))],
        compiler_params=PARAMS,
        name="plan",
    )(table, counts, layout)

    def member(rest, at):
        place = at ^ reversal(groups, gather, rest)
        return ((place // uly) * gather + rest) * uly + mirror(place % uly, uly)

    members = [[member(rest, at) for at in range(groups)] for rest in range(gather)]
    swap = functools.partial(
        lax.all_to_all,
        axis_name=("doc", "uly"),
        split_axis=0,
        concat_axis=0,
        axis_index_groups=members,
        tiled=True,
    )

    def hold(array):
        return pltpu.with_memory_space_constraint(array, pltpu.VMEM)

    def flip(array, bit):
        return lax.ppermute(array, "doc", [(at, at ^ bit) for at in range(doc)])

    arrived = swap(packed[0])
    arrived, units, totals, *packed = lax.optimization_barrier((arrived, units, totals, *packed))
    results = []
    for slot in range(slots):
        if slot:
            arrived, *results = lax.optimization_barrier((swap(packed[slot]), *results))
        arrays, bit = {0: arrived}, gather // 2
        while bit:
            arrays.update({at ^ bit: flip(array, bit) for at, array in list(arrays.items())})
            bit //= 2
        last = slot == slots - 1
        both = [pltpu.VMEM((UNROLL, BLK, 2 * BLK), F32)] * 2 + [pltpu.VMEM((UNROLL, 8, BLK), F32)] * 2
        both += [pltpu.VMEM((UNROLL, DH, BLK), F32)] * 2 + [pltpu.VMEM((UNROLL, 8, BLK), F32)] * 2
        earlier = results if last else []
        results.append(
            pl.pallas_call(
                functools.partial(attend_kernel, slot, gather),
                out_shape=pltpu.VMEM((groups, slots, DH, BLK) if last else (groups, DH, BLK), BF16),
                in_specs=[SMEM, SMEM] + [VMEM] * (gather + len(earlier)),
                out_specs=VMEM,
                scratch_shapes=[
                    pltpu.VMEM((gather * groups, 2, DH, BLK), BF16),
                    pltpu.VMEM((groups + 1, 2 * DH, 2 * BLK), BF16),
                    pltpu.VMEM((groups + 1, 8, BLK), F32),
                    pltpu.VMEM((groups + 1, 8, BLK), F32),
                    pltpu.VMEM((groups + 1, DH, BLK), F32),
                    *both,
                ],
                compiler_params=PARAMS,
                cost_estimate=pl.CostEstimate(flops=10**10, transcendentals=6 * 10**6, bytes_accessed=6 * 10**6),
                name="attend",
            )(units, totals, *[hold(arrays[at]) for at in range(gather)], *[hold(result) for result in earlier])
        )
    return pl.pallas_call(
        functools.partial(unpack_kernel, gather),
        out_shape=pltpu.HBM(queries.shape, BF16),
        in_specs=[SMEM, VMEM],
        out_specs=HBM,
        scratch_shapes=[pltpu.VMEM((4, BLK, H * DH // 4), BF16), pltpu.SemaphoreType.DMA((4,))],
        compiler_params=PARAMS,
        name="unpack",
    )(table, hold(swap(results[-1])))


def solution(mesh):
    placed = (
        P(("grp", "doc", "uly"), None),
        P(("grp", "doc", "uly"), None),
        P(("grp", "doc", "uly"), None),
        P("grp", None, None),
        P("grp", None),
    )
    return jax.shard_map(
        shards,
        mesh=mesh,
        in_specs=placed,
        out_specs=P(("grp", "doc", "uly"), None),
        check_vma=False,
    )
```

```python
import functools

import jax
import jax.numpy as jnp
from jax import lax
from jax.experimental import pallas as pl
from jax.experimental.pallas import tpu as pltpu
from jax.sharding import PartitionSpec as P

H = 32
DH = 64
BLK = 128
KMAX = 32
UNROLL = 6
BIG = 1e30
F32 = jnp.float32
BF16 = jnp.bfloat16
VMEM = pl.BlockSpec(memory_space=pltpu.VMEM)
SMEM = pl.BlockSpec(memory_space=pltpu.SMEM)
HBM = pl.BlockSpec(memory_space=pltpu.HBM)
PARAMS = pltpu.CompilerParams(vmem_limit_bytes=28 << 20)


def rank_heads(counts_ref, table_ref, groups):
    counts = counts_ref[...].astype(BF16)
    blocks = counts.shape[1]
    over = (((1,), (1,)), ((), ()))
    mine = lax.dot_general(counts, jnp.ones((H, blocks), BF16), over, preferred_element_type=F32)
    theirs = lax.dot_general(jnp.ones((H, blocks), BF16), counts, over, preferred_element_type=F32)
    row = lax.broadcasted_iota(jnp.int32, (H, H), 0)
    lane = lax.broadcasted_iota(jnp.int32, (H, H), 1)
    bits = groups.bit_length() - 1

    def place_of(rank):
        slot, seat = rank >> bits, rank & (groups - 1)
        return slot * groups + jnp.where((slot & 1) == 0, seat, groups - 1 - seat)

    behind = (theirs > mine) | ((theirs == mine) & (lane < row))
    rank_down = jnp.sum(jnp.where(behind, 1.0, 0.0), axis=1, keepdims=True).astype(jnp.int32)
    ahead = (mine > theirs) | ((theirs == mine) & (row < lane))
    rank_along = jnp.sum(jnp.where(ahead, 1.0, 0.0), axis=0, keepdims=True).astype(jnp.int32)
    here = place_of(jnp.broadcast_to(rank_down, (H, H))) == lane
    head_at = jnp.sum(jnp.where(here, row.astype(F32), 0.0), axis=0, keepdims=True).astype(jnp.int32)
    table_ref[0:1, 0:H] = head_at
    table_ref[1:2, 0:H] = place_of(rank_along)


def turn_heads(source, turned):
    for pair in range(H // 2):
        tile = source[:, pair * 2 * DH : (pair + 1) * 2 * DH].T
        turned[2 * pair] = tile[:DH]
        turned[2 * pair + 1] = tile[DH:]


def fold_head(source, head):
    odd = head % 2
    low = lax.broadcasted_iota(jnp.int32, (DH, 2 * DH), 1) < DH
    lanes = pl.ds(pl.multiple_of((head // 2) * (2 * DH), 2 * DH), 2 * DH)
    plain = source[pl.ds(pl.multiple_of(odd * DH, DH), DH), lanes]
    other = source[pl.ds(pl.multiple_of((1 - odd) * DH, DH), DH), lanes]
    return jnp.where(low == (odd == 0), plain, swap_halves(other))


def swap_halves(tile):
    return jnp.concatenate([tile[:, DH:], tile[:, :DH]], axis=1)


def turn_folded(first, second):
    low = lax.broadcasted_iota(jnp.int32, (DH, 2 * DH), 1) < DH
    turned = jnp.concatenate([first, second], axis=0).T
    early, late = turned[:DH], turned[DH:]
    return jnp.where(low, early, swap_halves(late)), jnp.where(low, swap_halves(early), late)


def load(arrays, buffers, sems):
    rows = arrays[0].shape[0] // 4
    copies = [
        [
            pltpu.make_async_copy(array.at[pl.ds(at * rows, rows)], buffer.at[pl.ds(at * rows, rows)], sems.at[which, at])
            for at in range(4)
        ]
        for which, (array, buffer) in enumerate(zip(arrays, buffers))
    ]
    for group in copies:
        for copy in group:
            copy.start()
    return copies


def pack_first_kernel(groups, counts_ref, q_ref, k_ref, v_ref, table_ref, out_ref, table_vmem, sem):
    rank_heads(counts_ref, table_vmem, groups)
    copy = pltpu.make_async_copy(table_vmem, table_ref, sem)
    copy.start()
    copy.wait()
    for group in range(groups):
        head = table_ref[0, group]
        for at, source in enumerate((v_ref, q_ref, k_ref)):
            out_ref[group, at] = fold_head(source, head)


def pack_rest_kernel(slot, table_ref, q_hbm, k_hbm, v_hbm, out_ref, q_ref, k_ref, v_ref, sems, turned_q, turned_v):
    copies = load((k_hbm, v_hbm, q_hbm), (k_ref, v_ref, q_ref), sems)
    for group in copies:
        for copy in group:
            copy.wait()
    turn_heads(q_ref, turned_q)
    turn_heads(v_ref, turned_v)
    groups = out_ref.shape[0]
    for group in range(groups):
        head = table_ref[0, slot * groups + group]
        out_ref[group, 0] = turned_v[head]
        out_ref[group, 1] = turned_q[head]
        out_ref[group, 2] = fold_head(k_ref, head)


def mirror(value, size):
    bits = size.bit_length() - 1
    return sum(((value >> at) & 1) << (bits - 1 - at) for at in range(bits)) if bits else value


def plan_kernel(uly, gather, table_ref, counts_ref, layout_ref, unit_ref, total_ref, lay_ref, sem):
    slots = total_ref.shape[0]
    groups = H // slots
    parts = groups // uly
    doc = lax.axis_index("doc")
    part, rest = doc // gather, doc % gather
    group = part * uly + mirror(lax.axis_index("uly"), uly)

    def rows_at(at):
        return (at * gather + rest) * uly

    copies = [
        pltpu.make_async_copy(
            layout_ref.at[table_ref[0, slot * groups + group], pl.ds(rows_at(at), uly)],
            lay_ref.at[slot, pl.ds(at * uly, uly)],
            sem.at[slot, at],
        )
        for slot in range(slots)
        for at in range(parts)
    ]
    for copy in copies:
        copy.start()

    def local(block):
        its = block // uly
        return ((its % gather) ^ rest) * groups + (its // gather) * uly + mirror(block % uly, uly)

    for copy in copies:
        copy.wait()
    for slot in range(slots):
        head = table_ref[0, slot * groups + group]

        def idle(base, many, slot=slot):
            for extra in range(many):
                unit_ref[slot, 0, base + extra] = groups
                unit_ref[slot, 1, base + extra] = 0
                unit_ref[slot, 2, base + extra] = 0
                unit_ref[slot, 3, base + extra] = 1

        def place_row(row, base, slot=slot, head=head):
            token = (row // uly) * uly + mirror(row % uly, uly)
            count = counts_ref[head, rows_at(row // uly) + mirror(row % uly, uly)]

            def place_unit(step, _):
                first = lay_ref[slot, token, 2 * step]
                whole = 2 * step + 1 < count
                second = jnp.where(whole, lay_ref[slot, token, jnp.minimum(2 * step + 1, KMAX - 1)], first)
                unit_ref[slot, 0, base + step] = row
                unit_ref[slot, 1, base + step] = local(first)
                unit_ref[slot, 2, base + step] = local(second)
                unit_ref[slot, 3, base + step] = whole.astype(jnp.int32)
                return 0

            units = (count + 1) // 2
            lax.fori_loop(0, units, place_unit, 0)
            return base + units

        idle(0, UNROLL)
        total = lax.fori_loop(0, groups, place_row, jnp.int32(UNROLL))
        idle(total, 4 * UNROLL)
        total_ref[slot] = total


def attend_kernel(slot, gather, unit_ref, total_ref, *refs):
    arrived, refs = refs[:gather], refs[gather:]
    earlier, refs = refs[:slot], refs[slot:]
    out_ref, kv_ref, qz_ref, m_ref, l_ref, acc_ref = refs[:6]
    score, top_of, out_of, sum_of = (refs[6 + 2 * at : 8 + 2 * at] for at in range(4))
    rows = arrived[0].shape[0]
    m_ref[...] = jnp.full(m_ref.shape, -BIG, F32)
    for ref in (l_ref, acc_ref):
        ref[...] = jnp.zeros(ref.shape, F32)
    zeros = jnp.zeros((DH, BLK), BF16)

    def put_query(row, part):
        up = jnp.concatenate([part, zeros], axis=0)
        down = jnp.concatenate([zeros, part], axis=0)
        qz_ref[row] = jnp.concatenate([up, down], axis=1)

    for row in range(0, rows, 2):
        pair = [arrived[0][row, 1], arrived[0][row + 1, 1]]
        for at, part in enumerate(turn_folded(*pair) if slot == 0 else pair):
            put_query(row + at, part)
    qz_ref[rows] = jnp.zeros((2 * DH, 2 * BLK), BF16)
    for at, array in enumerate(arrived):
        for row in range(0, rows, 2):
            place = at * rows + row
            kv_ref[place, 0], kv_ref[place + 1, 0] = array[row, 2], array[row + 1, 2]
            pair = [array[row, 0], array[row + 1, 0]]
            kv_ref[place, 1], kv_ref[place + 1, 1] = turn_folded(*pair) if slot == 0 else pair
    for at, result in enumerate(earlier):
        for row in range(rows):
            out_ref[row, at] = result[row]

    def make_scores(unit, lane, side):
        row, first, second = unit_ref[slot, 0, unit], unit_ref[slot, 1, unit], unit_ref[slot, 2, unit]
        keys = jnp.concatenate([kv_ref[first, 0], kv_ref[second, 0]], axis=0)
        scores = jnp.dot(keys, qz_ref[row], preferred_element_type=F32)
        score[side][lane] = scores
        top = jnp.max(scores.reshape(BLK // 8, 8, 2 * BLK), axis=0)
        top = jnp.maximum(top[:, :BLK], top[:, BLK:])
        top_of[side][lane] = jnp.broadcast_to(jnp.max(top, axis=0, keepdims=True), (8, BLK))

    def make_output(unit, lane, side):
        first, second = unit_ref[slot, 1, unit], unit_ref[slot, 2, unit]
        top = top_of[side][lane]
        limit = jnp.where(unit_ref[slot, 3, unit] == 1, top, top + BIG)
        scores = score[side][lane]
        tiles = (DH // 8, 8, BLK)
        weights = [
            jnp.exp(scores[at : at + DH, lanes : lanes + BLK].reshape(tiles) - bound[None])
            for at, bound in ((0, top), (DH, limit))
            for lanes in (0, BLK)
        ]
        sum_of[side][lane] = jnp.sum(sum(weights[1:], weights[0]), axis=0)
        weights = jnp.concatenate([part.reshape(DH, BLK) for part in weights], axis=0)
        values = jnp.concatenate([kv_ref[first, 1], kv_ref[second, 1]], axis=1)
        out_of[side][lane] = jnp.dot(values, weights.astype(BF16), preferred_element_type=F32)

    def merge(unit, lane, side):
        row = unit_ref[slot, 0, unit]
        top, old = top_of[side][lane], m_ref[row]
        new = jnp.maximum(old, top)
        a, b = jnp.exp(old - new), jnp.exp(top - new)
        m_ref[row] = new
        l_ref[row] = l_ref[row] * a + sum_of[side][lane] * b
        tiles = (DH // 8, 8, BLK)
        acc_ref[row] = (acc_ref[row].reshape(tiles) * a[None] + out_of[side][lane].reshape(tiles) * b[None]).reshape(
            DH, BLK
        )

    def advance(chunk, side):
        for lane in range(UNROLL):
            merge(chunk * UNROLL + lane, lane, side)
            make_scores((chunk + 2) * UNROLL + lane, lane, side)
            make_output((chunk + 1) * UNROLL + lane, lane, 1 - side)

    def step(index, _):
        advance(2 * index, 0)
        advance(2 * index + 1, 1)
        return 0

    chunks = (total_ref[slot] + UNROLL - 1) // UNROLL - 1
    for lane in range(UNROLL):
        make_scores(UNROLL + lane, lane, 1)
    lax.fori_loop(0, chunks // 2, step, 0)

    @pl.when(chunks % 2 == 1)
    def _():
        advance(chunks - 1, 0)
        for lane in range(UNROLL):
            merge(chunks * UNROLL + lane, lane, 1)

    @pl.when(chunks % 2 == 0)
    def _():
        for lane in range(UNROLL):
            merge(chunks * UNROLL + lane, lane, 0)

    for row in range(rows):
        total_w = jnp.sum(l_ref[row], axis=0, keepdims=True)
        result = (acc_ref[row] * (1.0 / total_w)).astype(BF16)
        if len(out_ref.shape) == 4:
            out_ref[row, slot] = result
        else:
            out_ref[row] = result


def unpack_kernel(table_ref, o_ref, out_hbm, out_ref, sem):
    groups = o_ref.shape[0]
    pairs = H // 2 // out_ref.shape[0]

    def fetch(head):
        place = table_ref[1, head]
        return o_ref[place % groups, place // groups]

    copies = []
    for part in range(out_ref.shape[0]):
        for at in range(pairs):
            head = 2 * (part * pairs + at)
            both = jnp.concatenate([fetch(head), fetch(head + 1)], axis=0)
            out_ref[part, :, at * 2 * DH : (at + 1) * 2 * DH] = both.T
        lanes = pl.ds(part * pairs * 2 * DH, pairs * 2 * DH)
        copies.append(pltpu.make_async_copy(out_ref.at[part], out_hbm.at[:, lanes], sem.at[part]))
        copies[-1].start()
    for copy in copies:
        copy.wait()


def shards(queries, key_vectors, value_vectors, layout, counts):
    uly, doc = lax.axis_size("uly"), lax.axis_size("doc")
    parts = max(min(doc // 2, H // (2 * uly)), 1)
    gather = doc // parts
    groups = uly * parts
    slots = H // groups
    shape = jax.ShapeDtypeStruct
    queries, key_vectors, value_vectors = (
        pltpu.with_memory_space_constraint(array, pltpu.HBM) for array in (queries, key_vectors, value_vectors)
    )
    packed_shape = pltpu.HBM((groups, 3, DH, BLK), BF16)
    held = [pltpu.VMEM(queries.shape, BF16)] * 3 + [pltpu.SemaphoreType.DMA((3, 4))]
    table, first = pl.pallas_call(
        functools.partial(pack_first_kernel, groups),
        out_shape=(shape((8, 128), jnp.int32), packed_shape),
        in_specs=[VMEM] * 4,
        out_specs=(SMEM, VMEM),
        scratch_shapes=[pltpu.VMEM((8, 128), jnp.int32), pltpu.SemaphoreType.DMA],
        compiler_params=PARAMS,
        name="pack",
    )(pltpu.with_memory_space_constraint(counts, pltpu.HBM), queries, key_vectors, value_vectors)
    packed = [first]
    for slot in range(1, slots):
        packed.append(
            pl.pallas_call(
                functools.partial(pack_rest_kernel, slot),
                out_shape=packed_shape,
                in_specs=[SMEM] + [HBM] * 3,
                out_specs=VMEM,
                scratch_shapes=[*held] + [pltpu.VMEM((H, DH, BLK), BF16)] * 2,
                compiler_params=PARAMS,
                name="pack",
            )(table, queries, key_vectors, value_vectors)
        )
    units, totals = pl.pallas_call(
        functools.partial(plan_kernel, uly, gather),
        out_shape=(shape((slots, 4, groups * KMAX // 2 + 8 * UNROLL), jnp.int32), shape((slots,), jnp.int32)),
        in_specs=[SMEM, SMEM, VMEM],
        out_specs=(SMEM, SMEM),
        scratch_shapes=[pltpu.SMEM((slots, groups, KMAX), jnp.int32), pltpu.SemaphoreType.DMA((slots, parts))],
        compiler_params=PARAMS,
        name="plan",
    )(table, counts, layout)

    members = [
        [(part * gather + rest) * uly + mirror(at, uly) for part in range(parts) for at in range(uly)]
        for rest in range(gather)
    ]
    swap = functools.partial(
        lax.all_to_all,
        axis_name=("doc", "uly"),
        split_axis=0,
        concat_axis=0,
        axis_index_groups=members,
        tiled=True,
    )

    def hold(array):
        return pltpu.with_memory_space_constraint(array, pltpu.VMEM)

    def flip(array, bit):
        return lax.ppermute(array, "doc", [(at, at ^ bit) for at in range(doc)])

    arrived = swap(packed[0])
    arrived, units, totals, *packed = lax.optimization_barrier((arrived, units, totals, *packed))
    results = []
    for slot in range(slots):
        if slot:
            arrived, *results = lax.optimization_barrier((swap(packed[slot]), *results))
        arrays, bit = {0: arrived}, gather // 2
        while bit:
            arrays.update({at ^ bit: flip(array, bit) for at, array in list(arrays.items())})
            bit //= 2
        last = slot == slots - 1
        both = [pltpu.VMEM((UNROLL, BLK, 2 * BLK), F32)] * 2 + [pltpu.VMEM((UNROLL, 8, BLK), F32)] * 2
        both += [pltpu.VMEM((UNROLL, DH, BLK), F32)] * 2 + [pltpu.VMEM((UNROLL, 8, BLK), F32)] * 2
        earlier = results if last else []
        results.append(
            pl.pallas_call(
                functools.partial(attend_kernel, slot, gather),
                out_shape=pltpu.VMEM((groups, slots, DH, BLK) if last else (groups, DH, BLK), BF16),
                in_specs=[SMEM, SMEM] + [VMEM] * (gather + len(earlier)),
                out_specs=VMEM,
                scratch_shapes=[
                    pltpu.VMEM((gather * groups, 2, DH, BLK), BF16),
                    pltpu.VMEM((groups + 1, 2 * DH, 2 * BLK), BF16),
                    pltpu.VMEM((groups + 1, 8, BLK), F32),
                    pltpu.VMEM((groups + 1, 8, BLK), F32),
                    pltpu.VMEM((groups + 1, DH, BLK), F32),
                    *both,
                ],
                compiler_params=PARAMS,
                cost_estimate=pl.CostEstimate(flops=10**10, transcendentals=6 * 10**6, bytes_accessed=6 * 10**6),
                name="attend",
            )(units, totals, *[hold(arrays[at]) for at in range(gather)], *[hold(result) for result in earlier])
        )
    return pl.pallas_call(
        unpack_kernel,
        out_shape=pltpu.HBM(queries.shape, BF16),
        in_specs=[SMEM, VMEM],
        out_specs=HBM,
        scratch_shapes=[pltpu.VMEM((4, BLK, H * DH // 4), BF16), pltpu.SemaphoreType.DMA((4,))],
        compiler_params=PARAMS,
        name="unpack",
    )(table, hold(swap(results[-1])))


def solution(mesh):
    placed = (
        P(("grp", "doc", "uly"), None),
        P(("grp", "doc", "uly"), None),
        P(("grp", "doc", "uly"), None),
        P("grp", None, None),
        P("grp", None),
    )
    return jax.shard_map(
        shards,
        mesh=mesh,
        in_specs=placed,
        out_specs=P(("grp", "doc", "uly"), None),
        check_vma=False,
    )
```

```python
import functools

import jax
import jax.numpy as jnp
from jax import lax
from jax.experimental import pallas as pl
from jax.experimental.pallas import tpu as pltpu
from jax.sharding import PartitionSpec as P

H = 32
DH = 64
BLK = 128
KMAX = 32
UNROLL = 6
BIG = 1e30
F32 = jnp.float32
BF16 = jnp.bfloat16
VMEM = pl.BlockSpec(memory_space=pltpu.VMEM)
SMEM = pl.BlockSpec(memory_space=pltpu.SMEM)
HBM = pl.BlockSpec(memory_space=pltpu.HBM)
PARAMS = pltpu.CompilerParams(vmem_limit_bytes=28 << 20)


def rank_heads(counts_ref, table_ref, groups):
    counts = counts_ref[...].astype(BF16)
    blocks = counts.shape[1]
    over = (((1,), (1,)), ((), ()))
    mine = lax.dot_general(counts, jnp.ones((H, blocks), BF16), over, preferred_element_type=F32)
    theirs = lax.dot_general(jnp.ones((H, blocks), BF16), counts, over, preferred_element_type=F32)
    row = lax.broadcasted_iota(jnp.int32, (H, H), 0)
    lane = lax.broadcasted_iota(jnp.int32, (H, H), 1)
    bits = groups.bit_length() - 1

    def place_of(rank):
        slot, seat = rank >> bits, rank & (groups - 1)
        return slot * groups + jnp.where((slot & 1) == 0, seat, groups - 1 - seat)

    behind = (theirs > mine) | ((theirs == mine) & (lane < row))
    rank_down = jnp.sum(jnp.where(behind, 1.0, 0.0), axis=1, keepdims=True).astype(jnp.int32)
    ahead = (mine > theirs) | ((theirs == mine) & (row < lane))
    rank_along = jnp.sum(jnp.where(ahead, 1.0, 0.0), axis=0, keepdims=True).astype(jnp.int32)
    here = place_of(jnp.broadcast_to(rank_down, (H, H))) == lane
    head_at = jnp.sum(jnp.where(here, row.astype(F32), 0.0), axis=0, keepdims=True).astype(jnp.int32)
    table_ref[0:1, 0:H] = head_at
    table_ref[1:2, 0:H] = place_of(rank_along)


def turn_heads(source, turned):
    for pair in range(H // 2):
        tile = source[:, pair * 2 * DH : (pair + 1) * 2 * DH].T
        turned[2 * pair] = tile[:DH]
        turned[2 * pair + 1] = tile[DH:]


def fold_head(source, head):
    odd = head % 2
    low = lax.broadcasted_iota(jnp.int32, (DH, 2 * DH), 1) < DH
    lanes = pl.ds(pl.multiple_of((head // 2) * (2 * DH), 2 * DH), 2 * DH)
    plain = source[pl.ds(pl.multiple_of(odd * DH, DH), DH), lanes]
    other = source[pl.ds(pl.multiple_of((1 - odd) * DH, DH), DH), lanes]
    return jnp.where(low == (odd == 0), plain, swap_halves(other))


def swap_halves(tile):
    return jnp.concatenate([tile[:, DH:], tile[:, :DH]], axis=1)


def turn_folded(first, second):
    low = lax.broadcasted_iota(jnp.int32, (DH, 2 * DH), 1) < DH
    turned = jnp.concatenate([first, second], axis=0).T
    early, late = turned[:DH], turned[DH:]
    return jnp.where(low, early, swap_halves(late)), jnp.where(low, swap_halves(early), late)


def load(arrays, buffers, sems):
    rows = arrays[0].shape[0] // 4
    copies = [
        [
            pltpu.make_async_copy(array.at[pl.ds(at * rows, rows)], buffer.at[pl.ds(at * rows, rows)], sems.at[which, at])
            for at in range(4)
        ]
        for which, (array, buffer) in enumerate(zip(arrays, buffers))
    ]
    for group in copies:
        for copy in group:
            copy.start()
    return copies


def pack_first_kernel(groups, counts_ref, q_ref, k_ref, v_ref, table_ref, out_ref, table_vmem, sem):
    rank_heads(counts_ref, table_vmem, groups)
    copy = pltpu.make_async_copy(table_vmem, table_ref, sem)
    copy.start()
    copy.wait()
    for group in range(groups):
        head = table_ref[0, group]
        for at, source in enumerate((v_ref, q_ref, k_ref)):
            out_ref[group, at] = fold_head(source, head)


def pack_rest_kernel(slot, table_ref, q_hbm, k_hbm, v_hbm, out_ref, q_ref, k_ref, v_ref, sems, turned_q, turned_v):
    copies = load((k_hbm, v_hbm, q_hbm), (k_ref, v_ref, q_ref), sems)
    for group in copies:
        for copy in group:
            copy.wait()
    turn_heads(q_ref, turned_q)
    turn_heads(v_ref, turned_v)
    groups = out_ref.shape[0]
    for group in range(groups):
        head = table_ref[0, slot * groups + group]
        out_ref[group, 0] = turned_v[head]
        out_ref[group, 1] = turned_q[head]
        out_ref[group, 2] = fold_head(k_ref, head)


def mirror(value, size):
    bits = size.bit_length() - 1
    return sum(((value >> at) & 1) << (bits - 1 - at) for at in range(bits)) if bits else value


def plan_kernel(uly, gather, table_ref, counts_ref, layout_ref, unit_ref, total_ref, lay_ref, index_ref, sem):
    slots = total_ref.shape[0]
    groups = H // slots
    parts = groups // uly
    doc = lax.axis_index("doc")
    part, rest = doc // gather, doc % gather
    group = part * uly + mirror(lax.axis_index("uly"), uly)

    def rows_at(at):
        return (at * gather + rest) * uly

    copies = [
        pltpu.make_async_copy(
            layout_ref.at[table_ref[0, slot * groups + group], pl.ds(rows_at(at), uly)],
            lay_ref.at[slot, pl.ds(at * uly, uly)],
            sem.at[slot, at],
        )
        for slot in range(slots)
        for at in range(parts)
    ]
    for copy in copies:
        copy.start()

    def place_block(block, _):
        its = block // uly
        index_ref[block] = ((its % gather) ^ rest) * groups + (its // gather) * uly + mirror(block % uly, uly)
        return 0

    lax.fori_loop(0, counts_ref.shape[1], place_block, 0)
    for copy in copies:
        copy.wait()
    for slot in range(slots):
        head = table_ref[0, slot * groups + group]

        def idle(base, many, slot=slot):
            for extra in range(many):
                unit_ref[slot, 0, base + extra] = groups
                unit_ref[slot, 1, base + extra] = 0
                unit_ref[slot, 2, base + extra] = 0
                unit_ref[slot, 3, base + extra] = 1

        def place_row(row, base, slot=slot, head=head):
            token = (row // uly) * uly + mirror(row % uly, uly)
            count = counts_ref[head, rows_at(row // uly) + mirror(row % uly, uly)]

            def place_unit(step, _):
                first = lay_ref[slot, token, 2 * step]
                whole = 2 * step + 1 < count
                second = jnp.where(whole, lay_ref[slot, token, jnp.minimum(2 * step + 1, KMAX - 1)], first)
                unit_ref[slot, 0, base + step] = row
                unit_ref[slot, 1, base + step] = index_ref[first]
                unit_ref[slot, 2, base + step] = index_ref[second]
                unit_ref[slot, 3, base + step] = whole.astype(jnp.int32)
                return 0

            units = (count + 1) // 2
            lax.fori_loop(0, units, place_unit, 0)
            return base + units

        idle(0, UNROLL)
        total = lax.fori_loop(0, groups, place_row, jnp.int32(UNROLL))
        idle(total, 4 * UNROLL)
        total_ref[slot] = total


def attend_kernel(slot, gather, unit_ref, total_ref, *refs):
    arrived, refs = refs[:gather], refs[gather:]
    earlier, refs = refs[:slot], refs[slot:]
    out_ref, kv_ref, qz_ref, m_ref, l_ref, acc_ref = refs[:6]
    score, top_of, out_of, sum_of = (refs[6 + 2 * at : 8 + 2 * at] for at in range(4))
    rows = arrived[0].shape[0]
    m_ref[...] = jnp.full(m_ref.shape, -BIG, F32)
    for ref in (l_ref, acc_ref):
        ref[...] = jnp.zeros(ref.shape, F32)
    zeros = jnp.zeros((DH, BLK), BF16)

    def put_query(row, part):
        up = jnp.concatenate([part, zeros], axis=0)
        down = jnp.concatenate([zeros, part], axis=0)
        qz_ref[row] = jnp.concatenate([up, down], axis=1)

    for row in range(0, rows, 2):
        pair = [arrived[0][row, 1], arrived[0][row + 1, 1]]
        for at, part in enumerate(turn_folded(*pair) if slot == 0 else pair):
            put_query(row + at, part)
    qz_ref[rows] = jnp.zeros((2 * DH, 2 * BLK), BF16)
    for at, array in enumerate(arrived):
        for row in range(0, rows, 2):
            place = at * rows + row
            kv_ref[place, 0], kv_ref[place + 1, 0] = array[row, 2], array[row + 1, 2]
            pair = [array[row, 0], array[row + 1, 0]]
            kv_ref[place, 1], kv_ref[place + 1, 1] = turn_folded(*pair) if slot == 0 else pair
    for at, result in enumerate(earlier):
        for row in range(rows):
            out_ref[row, at] = result[row]

    def make_scores(unit, lane, side):
        row, first, second = unit_ref[slot, 0, unit], unit_ref[slot, 1, unit], unit_ref[slot, 2, unit]
        keys = jnp.concatenate([kv_ref[first, 0], kv_ref[second, 0]], axis=0)
        scores = jnp.dot(keys, qz_ref[row], preferred_element_type=F32)
        score[side][lane] = scores
        top = jnp.max(scores.reshape(BLK // 8, 8, 2 * BLK), axis=0)
        top = jnp.maximum(top[:, :BLK], top[:, BLK:])
        top_of[side][lane] = jnp.broadcast_to(jnp.max(top, axis=0, keepdims=True), (8, BLK))

    def make_output(unit, lane, side):
        first, second = unit_ref[slot, 1, unit], unit_ref[slot, 2, unit]
        top = top_of[side][lane]
        limit = jnp.where(unit_ref[slot, 3, unit] == 1, top, top + BIG)
        scores = score[side][lane]
        tiles = (DH // 8, 8, BLK)
        weights = [
            jnp.exp(scores[at : at + DH, lanes : lanes + BLK].reshape(tiles) - bound[None])
            for at, bound in ((0, top), (DH, limit))
            for lanes in (0, BLK)
        ]
        sum_of[side][lane] = jnp.sum(sum(weights[1:], weights[0]), axis=0)
        weights = jnp.concatenate([part.reshape(DH, BLK) for part in weights], axis=0)
        values = jnp.concatenate([kv_ref[first, 1], kv_ref[second, 1]], axis=1)
        out_of[side][lane] = jnp.dot(values, weights.astype(BF16), preferred_element_type=F32)

    def merge(unit, lane, side):
        row = unit_ref[slot, 0, unit]
        top, old = top_of[side][lane], m_ref[row]
        new = jnp.maximum(old, top)
        a, b = jnp.exp(old - new), jnp.exp(top - new)
        m_ref[row] = new
        l_ref[row] = l_ref[row] * a + sum_of[side][lane] * b
        tiles = (DH // 8, 8, BLK)
        acc_ref[row] = (acc_ref[row].reshape(tiles) * a[None] + out_of[side][lane].reshape(tiles) * b[None]).reshape(
            DH, BLK
        )

    def advance(chunk, side):
        for lane in range(UNROLL):
            merge(chunk * UNROLL + lane, lane, side)
            make_scores((chunk + 2) * UNROLL + lane, lane, side)
            make_output((chunk + 1) * UNROLL + lane, lane, 1 - side)

    def step(index, _):
        advance(2 * index, 0)
        advance(2 * index + 1, 1)
        return 0

    chunks = (total_ref[slot] + UNROLL - 1) // UNROLL - 1
    for lane in range(UNROLL):
        make_scores(UNROLL + lane, lane, 1)
    lax.fori_loop(0, chunks // 2, step, 0)

    @pl.when(chunks % 2 == 1)
    def _():
        advance(chunks - 1, 0)
        for lane in range(UNROLL):
            merge(chunks * UNROLL + lane, lane, 1)

    @pl.when(chunks % 2 == 0)
    def _():
        for lane in range(UNROLL):
            merge(chunks * UNROLL + lane, lane, 0)

    for row in range(rows):
        total_w = jnp.sum(l_ref[row], axis=0, keepdims=True)
        result = (acc_ref[row] * (1.0 / total_w)).astype(BF16)
        if len(out_ref.shape) == 4:
            out_ref[row, slot] = result
        else:
            out_ref[row] = result


def unpack_kernel(table_ref, o_ref, out_hbm, out_ref, sem):
    groups = o_ref.shape[0]
    pairs = H // 2 // out_ref.shape[0]

    def fetch(head):
        place = table_ref[1, head]
        return o_ref[place % groups, place // groups]

    copies = []
    for part in range(out_ref.shape[0]):
        for at in range(pairs):
            head = 2 * (part * pairs + at)
            both = jnp.concatenate([fetch(head), fetch(head + 1)], axis=0)
            out_ref[part, :, at * 2 * DH : (at + 1) * 2 * DH] = both.T
        lanes = pl.ds(part * pairs * 2 * DH, pairs * 2 * DH)
        copies.append(pltpu.make_async_copy(out_ref.at[part], out_hbm.at[:, lanes], sem.at[part]))
        copies[-1].start()
    for copy in copies:
        copy.wait()


def shards(queries, key_vectors, value_vectors, layout, counts):
    uly, doc = lax.axis_size("uly"), lax.axis_size("doc")
    parts = max(min(doc // 2, H // (2 * uly)), 1)
    gather = doc // parts
    groups = uly * parts
    slots = H // groups
    shape = jax.ShapeDtypeStruct
    queries, key_vectors, value_vectors = (
        pltpu.with_memory_space_constraint(array, pltpu.HBM) for array in (queries, key_vectors, value_vectors)
    )
    packed_shape = pltpu.HBM((groups, 3, DH, BLK), BF16)
    held = [pltpu.VMEM(queries.shape, BF16)] * 3 + [pltpu.SemaphoreType.DMA((3, 4))]
    table, first = pl.pallas_call(
        functools.partial(pack_first_kernel, groups),
        out_shape=(shape((8, 128), jnp.int32), packed_shape),
        in_specs=[VMEM] * 4,
        out_specs=(SMEM, VMEM),
        scratch_shapes=[pltpu.VMEM((8, 128), jnp.int32), pltpu.SemaphoreType.DMA],
        compiler_params=PARAMS,
        name="pack",
    )(pltpu.with_memory_space_constraint(counts, pltpu.HBM), queries, key_vectors, value_vectors)
    packed = [first]
    for slot in range(1, slots):
        packed.append(
            pl.pallas_call(
                functools.partial(pack_rest_kernel, slot),
                out_shape=packed_shape,
                in_specs=[SMEM] + [HBM] * 3,
                out_specs=VMEM,
                scratch_shapes=[*held] + [pltpu.VMEM((H, DH, BLK), BF16)] * 2,
                compiler_params=PARAMS,
                name="pack",
            )(table, queries, key_vectors, value_vectors)
        )
    units, totals = pl.pallas_call(
        functools.partial(plan_kernel, uly, gather),
        out_shape=(shape((slots, 4, groups * KMAX // 2 + 8 * UNROLL), jnp.int32), shape((slots,), jnp.int32)),
        in_specs=[SMEM, SMEM, VMEM],
        out_specs=(SMEM, SMEM),
        scratch_shapes=[pltpu.SMEM((slots, groups, KMAX), jnp.int32), pltpu.SMEM((counts.shape[1],), jnp.int32), pltpu.SemaphoreType.DMA((slots, parts))],
        compiler_params=PARAMS,
        name="plan",
    )(table, counts, layout)

    members = [
        [(part * gather + rest) * uly + mirror(at, uly) for part in range(parts) for at in range(uly)]
        for rest in range(gather)
    ]
    swap = functools.partial(
        lax.all_to_all,
        axis_name=("doc", "uly"),
        split_axis=0,
        concat_axis=0,
        axis_index_groups=members,
        tiled=True,
    )

    def hold(array):
        return pltpu.with_memory_space_constraint(array, pltpu.VMEM)

    def flip(array, bit):
        return lax.ppermute(array, "doc", [(at, at ^ bit) for at in range(doc)])

    arrived = swap(packed[0])
    arrived, units, totals, *packed = lax.optimization_barrier((arrived, units, totals, *packed))
    results = []
    for slot in range(slots):
        if slot:
            arrived, *results = lax.optimization_barrier((swap(packed[slot]), *results))
        arrays, bit = {0: arrived}, gather // 2
        while bit:
            arrays.update({at ^ bit: flip(array, bit) for at, array in list(arrays.items())})
            bit //= 2
        last = slot == slots - 1
        both = [pltpu.VMEM((UNROLL, BLK, 2 * BLK), F32)] * 2 + [pltpu.VMEM((UNROLL, 8, BLK), F32)] * 2
        both += [pltpu.VMEM((UNROLL, DH, BLK), F32)] * 2 + [pltpu.VMEM((UNROLL, 8, BLK), F32)] * 2
        earlier = results if last else []
        results.append(
            pl.pallas_call(
                functools.partial(attend_kernel, slot, gather),
                out_shape=pltpu.VMEM((groups, slots, DH, BLK) if last else (groups, DH, BLK), BF16),
                in_specs=[SMEM, SMEM] + [VMEM] * (gather + len(earlier)),
                out_specs=VMEM,
                scratch_shapes=[
                    pltpu.VMEM((gather * groups, 2, DH, BLK), BF16),
                    pltpu.VMEM((groups + 1, 2 * DH, 2 * BLK), BF16),
                    pltpu.VMEM((groups + 1, 8, BLK), F32),
                    pltpu.VMEM((groups + 1, 8, BLK), F32),
                    pltpu.VMEM((groups + 1, DH, BLK), F32),
                    *both,
                ],
                compiler_params=PARAMS,
                cost_estimate=pl.CostEstimate(flops=10**10, transcendentals=6 * 10**6, bytes_accessed=6 * 10**6),
                name="attend",
            )(units, totals, *[hold(arrays[at]) for at in range(gather)], *[hold(result) for result in earlier])
        )
    return pl.pallas_call(
        unpack_kernel,
        out_shape=pltpu.HBM(queries.shape, BF16),
        in_specs=[SMEM, VMEM],
        out_specs=HBM,
        scratch_shapes=[pltpu.VMEM((4, BLK, H * DH // 4), BF16), pltpu.SemaphoreType.DMA((4,))],
        compiler_params=PARAMS,
        name="unpack",
    )(table, hold(swap(results[-1])))


def solution(mesh):
    placed = (
        P(("grp", "doc", "uly"), None),
        P(("grp", "doc", "uly"), None),
        P(("grp", "doc", "uly"), None),
        P("grp", None, None),
        P("grp", None),
    )
    return jax.shard_map(
        shards,
        mesh=mesh,
        in_specs=placed,
        out_specs=P(("grp", "doc", "uly"), None),
        check_vma=False,
    )
```

```python
import functools

import jax
import jax.numpy as jnp
from jax import lax
from jax.experimental import pallas as pl
from jax.experimental.pallas import tpu as pltpu
from jax.sharding import PartitionSpec as P

H = 32
DH = 64
BLK = 128
KMAX = 32
UNROLL = 7
BIG = 1e30
F32 = jnp.float32
BF16 = jnp.bfloat16
VMEM = pl.BlockSpec(memory_space=pltpu.VMEM)
SMEM = pl.BlockSpec(memory_space=pltpu.SMEM)
HBM = pl.BlockSpec(memory_space=pltpu.HBM)
PARAMS = pltpu.CompilerParams(vmem_limit_bytes=28 << 20)


def rank_heads(counts_ref, table_ref, groups):
    counts = counts_ref[...].astype(BF16)
    blocks = counts.shape[1]
    over = (((1,), (1,)), ((), ()))
    mine = lax.dot_general(counts, jnp.ones((H, blocks), BF16), over, preferred_element_type=F32)
    theirs = lax.dot_general(jnp.ones((H, blocks), BF16), counts, over, preferred_element_type=F32)
    row = lax.broadcasted_iota(jnp.int32, (H, H), 0)
    lane = lax.broadcasted_iota(jnp.int32, (H, H), 1)
    bits = groups.bit_length() - 1

    def place_of(rank):
        slot, seat = rank >> bits, rank & (groups - 1)
        return slot * groups + jnp.where((slot & 1) == 0, seat, groups - 1 - seat)

    behind = (theirs > mine) | ((theirs == mine) & (lane < row))
    rank_down = jnp.sum(jnp.where(behind, 1.0, 0.0), axis=1, keepdims=True).astype(jnp.int32)
    ahead = (mine > theirs) | ((theirs == mine) & (row < lane))
    rank_along = jnp.sum(jnp.where(ahead, 1.0, 0.0), axis=0, keepdims=True).astype(jnp.int32)
    here = place_of(jnp.broadcast_to(rank_down, (H, H))) == lane
    head_at = jnp.sum(jnp.where(here, row.astype(F32), 0.0), axis=0, keepdims=True).astype(jnp.int32)
    table_ref[0:1, 0:H] = head_at
    table_ref[1:2, 0:H] = place_of(rank_along)


def turn_heads(source, turned):
    for pair in range(H // 2):
        tile = source[:, pair * 2 * DH : (pair + 1) * 2 * DH].T
        turned[2 * pair] = tile[:DH]
        turned[2 * pair + 1] = tile[DH:]


def fold_head(source, head):
    odd = head % 2
    low = lax.broadcasted_iota(jnp.int32, (DH, 2 * DH), 1) < DH
    lanes = pl.ds(pl.multiple_of((head // 2) * (2 * DH), 2 * DH), 2 * DH)
    plain = source[pl.ds(pl.multiple_of(odd * DH, DH), DH), lanes]
    other = source[pl.ds(pl.multiple_of((1 - odd) * DH, DH), DH), lanes]
    return jnp.where(low == (odd == 0), plain, swap_halves(other))


def swap_halves(tile):
    return jnp.concatenate([tile[:, DH:], tile[:, :DH]], axis=1)


def turn_folded(first, second):
    low = lax.broadcasted_iota(jnp.int32, (DH, 2 * DH), 1) < DH
    turned = jnp.concatenate([first, second], axis=0).T
    early, late = turned[:DH], turned[DH:]
    return jnp.where(low, early, swap_halves(late)), jnp.where(low, swap_halves(early), late)


def load(arrays, buffers, sems):
    rows = arrays[0].shape[0] // 4
    copies = [
        [
            pltpu.make_async_copy(array.at[pl.ds(at * rows, rows)], buffer.at[pl.ds(at * rows, rows)], sems.at[which, at])
            for at in range(4)
        ]
        for which, (array, buffer) in enumerate(zip(arrays, buffers))
    ]
    for group in copies:
        for copy in group:
            copy.start()
    return copies


def pack_first_kernel(groups, counts_ref, q_ref, k_ref, v_ref, table_ref, out_ref, table_vmem, sem):
    rank_heads(counts_ref, table_vmem, groups)
    copy = pltpu.make_async_copy(table_vmem, table_ref, sem)
    copy.start()
    copy.wait()
    for group in range(groups):
        head = table_ref[0, group]
        for at, source in enumerate((v_ref, q_ref, k_ref)):
            out_ref[group, at] = fold_head(source, head)


def pack_rest_kernel(slot, table_ref, q_hbm, k_hbm, v_hbm, out_ref, q_ref, k_ref, v_ref, sems, turned_q, turned_v):
    copies = load((k_hbm, v_hbm, q_hbm), (k_ref, v_ref, q_ref), sems)
    for group in copies:
        for copy in group:
            copy.wait()
    turn_heads(q_ref, turned_q)
    turn_heads(v_ref, turned_v)
    groups = out_ref.shape[0]
    for group in range(groups):
        head = table_ref[0, slot * groups + group]
        out_ref[group, 0] = turned_v[head]
        out_ref[group, 1] = turned_q[head]
        out_ref[group, 2] = fold_head(k_ref, head)


def mirror(value, size):
    bits = size.bit_length() - 1
    return sum(((value >> at) & 1) << (bits - 1 - at) for at in range(bits)) if bits else value


def plan_kernel(uly, gather, table_ref, counts_ref, layout_ref, unit_ref, total_ref, lay_ref, index_ref, sem):
    slots = total_ref.shape[0]
    groups = H // slots
    parts = groups // uly
    doc = lax.axis_index("doc")
    part, rest = doc // gather, doc % gather
    group = part * uly + mirror(lax.axis_index("uly"), uly)

    def rows_at(at):
        return (at * gather + rest) * uly

    copies = [
        pltpu.make_async_copy(
            layout_ref.at[table_ref[0, slot * groups + group], pl.ds(rows_at(at), uly)],
            lay_ref.at[slot, pl.ds(at * uly, uly)],
            sem.at[slot, at],
        )
        for slot in range(slots)
        for at in range(parts)
    ]
    for copy in copies:
        copy.start()

    def place_block(block, _):
        its = block // uly
        index_ref[block] = ((its % gather) ^ rest) * groups + (its // gather) * uly + mirror(block % uly, uly)
        return 0

    lax.fori_loop(0, counts_ref.shape[1], place_block, 0)
    for copy in copies:
        copy.wait()
    for slot in range(slots):
        head = table_ref[0, slot * groups + group]

        def idle(base, many, slot=slot):
            for extra in range(many):
                unit_ref[slot, 0, base + extra] = groups
                unit_ref[slot, 1, base + extra] = 0
                unit_ref[slot, 2, base + extra] = 0
                unit_ref[slot, 3, base + extra] = 1

        def place_row(row, base, slot=slot, head=head):
            token = (row // uly) * uly + mirror(row % uly, uly)
            count = counts_ref[head, rows_at(row // uly) + mirror(row % uly, uly)]

            def place_unit(step, _):
                first = lay_ref[slot, token, 2 * step]
                whole = 2 * step + 1 < count
                second = jnp.where(whole, lay_ref[slot, token, jnp.minimum(2 * step + 1, KMAX - 1)], first)
                unit_ref[slot, 0, base + step] = row
                unit_ref[slot, 1, base + step] = index_ref[first]
                unit_ref[slot, 2, base + step] = index_ref[second]
                unit_ref[slot, 3, base + step] = whole.astype(jnp.int32)
                return 0

            units = (count + 1) // 2
            lax.fori_loop(0, units, place_unit, 0)
            return base + units

        idle(0, UNROLL)
        total = lax.fori_loop(0, groups, place_row, jnp.int32(UNROLL))
        idle(total, 4 * UNROLL)
        total_ref[slot] = total


def attend_kernel(slot, gather, unit_ref, total_ref, *refs):
    arrived, refs = refs[:gather], refs[gather:]
    earlier, refs = refs[:slot], refs[slot:]
    out_ref, kv_ref, qz_ref, m_ref, l_ref, acc_ref = refs[:6]
    score, top_of, out_of, sum_of = (refs[6 + 2 * at : 8 + 2 * at] for at in range(4))
    rows = arrived[0].shape[0]
    m_ref[...] = jnp.full(m_ref.shape, -BIG, F32)
    for ref in (l_ref, acc_ref):
        ref[...] = jnp.zeros(ref.shape, F32)
    zeros = jnp.zeros((DH, BLK), BF16)

    def put_query(row, part):
        up = jnp.concatenate([part, zeros], axis=0)
        down = jnp.concatenate([zeros, part], axis=0)
        qz_ref[row] = jnp.concatenate([up, down], axis=1)

    for row in range(0, rows, 2):
        pair = [arrived[0][row, 1], arrived[0][row + 1, 1]]
        for at, part in enumerate(turn_folded(*pair) if slot == 0 else pair):
            put_query(row + at, part)
    qz_ref[rows] = jnp.zeros((2 * DH, 2 * BLK), BF16)
    for at, array in enumerate(arrived):
        for row in range(0, rows, 2):
            place = at * rows + row
            kv_ref[place, 0], kv_ref[place + 1, 0] = array[row, 2], array[row + 1, 2]
            pair = [array[row, 0], array[row + 1, 0]]
            kv_ref[place, 1], kv_ref[place + 1, 1] = turn_folded(*pair) if slot == 0 else pair
    for at, result in enumerate(earlier):
        for row in range(rows):
            out_ref[row, at] = result[row]

    def make_scores(unit, lane, side):
        row, first, second = unit_ref[slot, 0, unit], unit_ref[slot, 1, unit], unit_ref[slot, 2, unit]
        keys = jnp.concatenate([kv_ref[first, 0], kv_ref[second, 0]], axis=0)
        scores = jnp.dot(keys, qz_ref[row], preferred_element_type=F32)
        score[side][lane] = scores
        top = jnp.max(scores.reshape(BLK // 8, 8, 2 * BLK), axis=0)
        top = jnp.maximum(top[:, :BLK], top[:, BLK:])
        top_of[side][lane] = jnp.broadcast_to(jnp.max(top, axis=0, keepdims=True), (8, BLK))

    def make_output(unit, lane, side):
        first, second = unit_ref[slot, 1, unit], unit_ref[slot, 2, unit]
        top = top_of[side][lane]
        limit = jnp.where(unit_ref[slot, 3, unit] == 1, top, top + BIG)
        scores = score[side][lane]
        tiles = (DH // 8, 8, BLK)
        weights = [
            jnp.exp(scores[at : at + DH, lanes : lanes + BLK].reshape(tiles) - bound[None])
            for at, bound in ((0, top), (DH, limit))
            for lanes in (0, BLK)
        ]
        sum_of[side][lane] = jnp.sum(sum(weights[1:], weights[0]), axis=0)
        weights = jnp.concatenate([part.reshape(DH, BLK) for part in weights], axis=0)
        values = jnp.concatenate([kv_ref[first, 1], kv_ref[second, 1]], axis=1)
        out_of[side][lane] = jnp.dot(values, weights.astype(BF16), preferred_element_type=F32)

    def merge(unit, lane, side):
        row = unit_ref[slot, 0, unit]
        top, old = top_of[side][lane], m_ref[row]
        new = jnp.maximum(old, top)
        a, b = jnp.exp(old - new), jnp.exp(top - new)
        m_ref[row] = new
        l_ref[row] = l_ref[row] * a + sum_of[side][lane] * b
        tiles = (DH // 8, 8, BLK)
        acc_ref[row] = (acc_ref[row].reshape(tiles) * a[None] + out_of[side][lane].reshape(tiles) * b[None]).reshape(
            DH, BLK
        )

    def advance(chunk, side):
        for lane in range(UNROLL):
            merge(chunk * UNROLL + lane, lane, side)
            make_scores((chunk + 2) * UNROLL + lane, lane, side)
            make_output((chunk + 1) * UNROLL + lane, lane, 1 - side)

    def step(index, _):
        advance(2 * index, 0)
        advance(2 * index + 1, 1)
        return 0

    chunks = (total_ref[slot] + UNROLL - 1) // UNROLL - 1
    for lane in range(UNROLL):
        make_scores(UNROLL + lane, lane, 1)
    lax.fori_loop(0, chunks // 2, step, 0)

    @pl.when(chunks % 2 == 1)
    def _():
        advance(chunks - 1, 0)
        for lane in range(UNROLL):
            merge(chunks * UNROLL + lane, lane, 1)

    @pl.when(chunks % 2 == 0)
    def _():
        for lane in range(UNROLL):
            merge(chunks * UNROLL + lane, lane, 0)

    for row in range(rows):
        total_w = jnp.sum(l_ref[row], axis=0, keepdims=True)
        result = (acc_ref[row] * (1.0 / total_w)).astype(BF16)
        if len(out_ref.shape) == 4:
            out_ref[row, slot] = result
        else:
            out_ref[row] = result


def unpack_kernel(table_ref, o_ref, out_hbm, out_ref, sem):
    groups = o_ref.shape[0]
    pairs = H // 2 // out_ref.shape[0]

    def fetch(head):
        place = table_ref[1, head]
        return o_ref[place % groups, place // groups]

    copies = []
    for part in range(out_ref.shape[0]):
        for at in range(pairs):
            head = 2 * (part * pairs + at)
            both = jnp.concatenate([fetch(head), fetch(head + 1)], axis=0)
            out_ref[part, :, at * 2 * DH : (at + 1) * 2 * DH] = both.T
        lanes = pl.ds(part * pairs * 2 * DH, pairs * 2 * DH)
        copies.append(pltpu.make_async_copy(out_ref.at[part], out_hbm.at[:, lanes], sem.at[part]))
        copies[-1].start()
    for copy in copies:
        copy.wait()


def shards(queries, key_vectors, value_vectors, layout, counts):
    uly, doc = lax.axis_size("uly"), lax.axis_size("doc")
    parts = max(min(doc // 2, H // (2 * uly)), 1)
    gather = doc // parts
    groups = uly * parts
    slots = H // groups
    shape = jax.ShapeDtypeStruct
    queries, key_vectors, value_vectors = (
        pltpu.with_memory_space_constraint(array, pltpu.HBM) for array in (queries, key_vectors, value_vectors)
    )
    packed_shape = pltpu.HBM((groups, 3, DH, BLK), BF16)
    held = [pltpu.VMEM(queries.shape, BF16)] * 3 + [pltpu.SemaphoreType.DMA((3, 4))]
    table, first = pl.pallas_call(
        functools.partial(pack_first_kernel, groups),
        out_shape=(shape((8, 128), jnp.int32), packed_shape),
        in_specs=[VMEM] * 4,
        out_specs=(SMEM, VMEM),
        scratch_shapes=[pltpu.VMEM((8, 128), jnp.int32), pltpu.SemaphoreType.DMA],
        compiler_params=PARAMS,
        name="pack",
    )(pltpu.with_memory_space_constraint(counts, pltpu.HBM), queries, key_vectors, value_vectors)
    packed = [first]
    for slot in range(1, slots):
        packed.append(
            pl.pallas_call(
                functools.partial(pack_rest_kernel, slot),
                out_shape=packed_shape,
                in_specs=[SMEM] + [HBM] * 3,
                out_specs=VMEM,
                scratch_shapes=[*held] + [pltpu.VMEM((H, DH, BLK), BF16)] * 2,
                compiler_params=PARAMS,
                name="pack",
            )(table, queries, key_vectors, value_vectors)
        )
    units, totals = pl.pallas_call(
        functools.partial(plan_kernel, uly, gather),
        out_shape=(shape((slots, 4, groups * KMAX // 2 + 8 * UNROLL), jnp.int32), shape((slots,), jnp.int32)),
        in_specs=[SMEM, SMEM, VMEM],
        out_specs=(SMEM, SMEM),
        scratch_shapes=[pltpu.SMEM((slots, groups, KMAX), jnp.int32), pltpu.SMEM((counts.shape[1],), jnp.int32), pltpu.SemaphoreType.DMA((slots, parts))],
        compiler_params=PARAMS,
        name="plan",
    )(table, counts, layout)

    members = [
        [(part * gather + rest) * uly + mirror(at, uly) for part in range(parts) for at in range(uly)]
        for rest in range(gather)
    ]
    swap = functools.partial(
        lax.all_to_all,
        axis_name=("doc", "uly"),
        split_axis=0,
        concat_axis=0,
        axis_index_groups=members,
        tiled=True,
    )

    def hold(array):
        return pltpu.with_memory_space_constraint(array, pltpu.VMEM)

    def flip(array, bit):
        return lax.ppermute(array, "doc", [(at, at ^ bit) for at in range(doc)])

    arrived = swap(packed[0])
    arrived, units, totals, *packed = lax.optimization_barrier((arrived, units, totals, *packed))
    results = []
    for slot in range(slots):
        if slot:
            arrived, *results = lax.optimization_barrier((swap(packed[slot]), *results))
        arrays, bit = {0: arrived}, gather // 2
        while bit:
            arrays.update({at ^ bit: flip(array, bit) for at, array in list(arrays.items())})
            bit //= 2
        last = slot == slots - 1
        both = [pltpu.VMEM((UNROLL, BLK, 2 * BLK), F32)] * 2 + [pltpu.VMEM((UNROLL, 8, BLK), F32)] * 2
        both += [pltpu.VMEM((UNROLL, DH, BLK), F32)] * 2 + [pltpu.VMEM((UNROLL, 8, BLK), F32)] * 2
        earlier = results if last else []
        results.append(
            pl.pallas_call(
                functools.partial(attend_kernel, slot, gather),
                out_shape=pltpu.VMEM((groups, slots, DH, BLK) if last else (groups, DH, BLK), BF16),
                in_specs=[SMEM, SMEM] + [VMEM] * (gather + len(earlier)),
                out_specs=VMEM,
                scratch_shapes=[
                    pltpu.VMEM((gather * groups, 2, DH, BLK), BF16),
                    pltpu.VMEM((groups + 1, 2 * DH, 2 * BLK), BF16),
                    pltpu.VMEM((groups + 1, 8, BLK), F32),
                    pltpu.VMEM((groups + 1, 8, BLK), F32),
                    pltpu.VMEM((groups + 1, DH, BLK), F32),
                    *both,
                ],
                compiler_params=PARAMS,
                cost_estimate=pl.CostEstimate(flops=10**10, transcendentals=6 * 10**6, bytes_accessed=6 * 10**6),
                name="attend",
            )(units, totals, *[hold(arrays[at]) for at in range(gather)], *[hold(result) for result in earlier])
        )
    return pl.pallas_call(
        unpack_kernel,
        out_shape=pltpu.HBM(queries.shape, BF16),
        in_specs=[SMEM, VMEM],
        out_specs=HBM,
        scratch_shapes=[pltpu.VMEM((4, BLK, H * DH // 4), BF16), pltpu.SemaphoreType.DMA((4,))],
        compiler_params=PARAMS,
        name="unpack",
    )(table, hold(swap(results[-1])))


def solution(mesh):
    placed = (
        P(("grp", "doc", "uly"), None),
        P(("grp", "doc", "uly"), None),
        P(("grp", "doc", "uly"), None),
        P("grp", None, None),
        P("grp", None),
    )
    return jax.shard_map(
        shards,
        mesh=mesh,
        in_specs=placed,
        out_specs=P(("grp", "doc", "uly"), None),
        check_vma=False,
    )
```
